128 devices in a mesh: sky: 16 (over z, y), exp: 8 (over x, core).
Axes of the slice: x: 4, y: 4, z: 4, core: 2. Of those that a mesh axis runs over, the one named last changes fastest.
Arguments:
- sky_model: bfloat16 [4096, 1024], P('sky'), may hold values from -6 to 6
- exposure_data: bfloat16 [2048, 128, 128], P(('sky', 'exp')), may hold values from -6 to 6
- pixel_mask: int32 [2048, 128, 128], P(('sky', 'exp')), may hold values 0 or 1
- block_owner: int32 [2048, 1], P(('sky', 'exp')), may hold values from 0 to 15; in each aligned block of 16 rows (0 to 15, 16 to 31, ...) at most 2 rows name the same one
- block_local: int32 [2048], P(('sky', 'exp')), may hold values from 0 to 15
- psf_cell: int32 [2048], P(('sky', 'exp')), may hold values from 0 to 15
- psf_table: bfloat16 [128, 1681], P('exp'), may hold values from -0.15625 to 0.15625
Outputs:
- model_grad: float32 [4096, 1024], P('sky', 'exp')
- residual: bfloat16 [2048, 128, 128], P(('sky', 'exp'))
The draws below stay inside these ranges and needn't reach their ends.
Inputs may be any that keep to these rules, and one draw needn't show every extreme that they name: `block_owner`: among the pieces of one device no sky index is named more than 2 times.
All inputs are finite; a program needn't handle non-finite values. No bound on the sum of `pixel_mask` on one device may be relied on, other than what follows from the above.
Results may differ from the reference program's by a relative error of at most 0.014.
Values may be sent and summed in bfloat16 or wider, within the bound.
No kernel may reach another device: no remote copies, remote signals or barrier semaphores. Data moves between devices by JAX's collectives and lax.ppermute only.
A program may use at most 64 MiB of HBM per device.

```python
import math
import jax
import jax.numpy as jnp
import numpy as np
from jax import lax

B = 128
PSF = 41
HALO = 20
CAP = 2
CELLS = 16
BR = 2
BC = 8
P_DEV = 16
NBD = 16
NY = 4096
NX = 1024
PIECES = 2048
N_SKY = 16
N_EXP = 8


def set_ends(drawn, own_key, least, top_value):
    index_at = [jax.random.randint(jax.random.fold_in(own_key, axis), (), 0, length) for axis, length in enumerate(drawn.shape)]
    widest = drawn.shape.index(max(drawn.shape))
    neighbour = index_at[:widest] + [(index_at[widest] + 1) % drawn.shape[widest]] + index_at[widest + 1:]
    return drawn.at[tuple(index_at)].set(least).at[tuple(neighbour)].set(top_value)


def level_of(rng, shape, shards, least, largest):
    def one(position, blocks):
        draws = jax.random.uniform(jax.random.fold_in(jax.random.fold_in(rng, 6), position), (blocks,), jnp.float32, least / len(shards), largest / len(shards))
        return jnp.repeat(jnp.exp(draws), shape[position] // blocks).reshape((-1,) + (1,) * (len(shape) - position - 1))

    level = one(*shards[0])
    for cut in shards[1:]:
        level = level * one(*cut)
    return level


def routed_block(stream_key, own, number, rows, count, top, reach, skew):
    order = jax.random.permutation(stream_key, count)
    packed, usual = portions_of(count, rows * top, reach, skew, True), portions_of(count, rows * top, reach, skew, False)
    places = jnp.arange(count)

    def named(lengths, turn):
        used = int((lengths > 0).sum())
        fixed = max(1, used // 4)
        moved = fixed + (places - fixed + turn * (used - fixed)) % max(1, count - fixed)
        return jnp.zeros((count,), jnp.int32).at[order[jnp.where(places < fixed, places, moved)]].set(jnp.asarray(lengths, jnp.int32))

    lengths = jnp.where(number % 4 == 0, named(packed, number // 4), named(usual, number - number // 4 - 1))
    mixed = jax.random.permutation(jax.random.fold_in(own, 3), count)
    donor, receiver = mixed[0:count // 2 * 2:2], mixed[1:count // 2 * 2:2]
    slack = jnp.minimum(lengths[donor] - 1, reach - lengths[receiver]) // 2
    slack = jnp.where((donor == order[0]) | (receiver == order[0]) | (lengths[receiver] == 0), 0, jnp.maximum(slack, 0))
    moved = jax.random.randint(jax.random.fold_in(own, 4), (count // 2,), 0, 1 << 20) % (slack + 1)
    lengths = lengths.at[donor].add(-moved).at[receiver].add(moved)
    labels = jnp.searchsorted(jnp.cumsum(lengths), jnp.arange(rows * top), side="right").astype(jnp.int32)
    table = labels.reshape(top, rows).T
    table = table[jax.random.permutation(jax.random.fold_in(own, 1), rows)]
    turn = jax.random.randint(jax.random.fold_in(own, 2), (rows, 1), 0, top)
    return jnp.take_along_axis(table, (jnp.arange(top)[None, :] + turn) % top, axis=1)


def portions_of(amount, total, most, lean, full):
    loads = [(1 << 20) // math.isqrt(standing ** lean) + 1 for standing in range(1, amount + 1)]
    largest = most if full else min(most, max(-(-total // amount), total * loads[0] // sum(loads)))
    least = 1 if total - largest >= amount - 1 else 0
    given, rest = [largest] + [least] * (amount - 1), total - largest - least * (amount - 1)
    while rest > 0:
        free = [i for i in range(1, amount) if given[i] < largest] or [i for i in range(1, amount) if given[i] < most]
        pool, budget = sum([loads[i] for i in free]), rest
        for i in free:
            extra = min(most - given[i], max(1, budget * loads[i] // pool), rest)
            given[i] = given[i] + extra
            rest = rest - extra
    return np.array(given)


def scatter_about(stream_key, dims, scale, reach, pieces=(), held_as=jnp.bfloat16):
    result = jax.random.normal(stream_key, dims, jnp.float32) * scale
    if len(pieces) > 0:
        result = level_of(stream_key, dims, pieces, -0.22, 0.18) * result
    return jnp.clip(result, min=-reach, max=reach).astype(held_as)


def setup_inputs(seed: int = 0) -> dict:
    splits = jax.random.split(jax.random.key(seed), 8)
    sky_model = scatter_about(splits[0], (NY, NX), 1.0, 6.0, ((0, 16),))
    exposure_data = scatter_about(splits[1], (PIECES, B, B), 1.0, 6.0, ((0, 128),))
    pixel_mask = set_ends((jax.random.randint(splits[2], (PIECES, B, B), 0, 4) < 3).astype(jnp.int32), jax.random.fold_in(splits[2], 1), 0, 1)
    block_owner_keys = jax.random.split(jax.random.fold_in(splits[3], 1), PIECES // P_DEV)
    block_owner_turns = jax.random.permutation(jax.random.fold_in(splits[3], 3), PIECES // P_DEV)
    block_owner = jax.vmap(lambda own, number: routed_block(jax.random.fold_in(splits[3], 2), own, number, P_DEV, N_SKY, 1, CAP, 2))(block_owner_keys, block_owner_turns).reshape((PIECES, 1))
    block_local = set_ends(jax.random.randint(splits[4], (PIECES,), 0, NBD), jax.random.fold_in(splits[4], 1), 0, NBD - 1).astype(jnp.int32)
    psf_cell = set_ends(jax.random.randint(splits[5], (PIECES,), 0, CELLS), jax.random.fold_in(splits[5], 1), 0, CELLS - 1).astype(jnp.int32)
    psf_table = scatter_about(splits[6], (N_EXP * CELLS, PSF * PSF), (PSF * PSF) ** -0.5, 0.15625, ((0, 8),))
    return {"sky_model": sky_model, "exposure_data": exposure_data, "pixel_mask": pixel_mask, "block_owner": block_owner, "block_local": block_local, "psf_cell": psf_cell, "psf_table": psf_table}


def correlate(field, kernel, out_size):
    extent = field.shape[0]
    padded_kernel = jnp.zeros((extent, extent), field.dtype).at[:PSF, :PSF].set(kernel)
    spectrum = jnp.fft.rfft2(field) * jnp.conj(jnp.fft.rfft2(padded_kernel))
    return jnp.fft.irfft2(spectrum, s=(extent, extent))[:out_size, :out_size]


def reference(sky_model, exposure_data, pixel_mask, block_owner, block_local, psf_cell, psf_table):
    extent = B + 2 * HALO
    padded = jnp.pad(sky_model.astype(jnp.float32), HALO)
    piece_ids = jnp.arange(PIECES, dtype=jnp.int32)
    owner_exp = (piece_ids // P_DEV) % N_EXP
    row_start = ((block_owner[:, 0] * BR + block_local // BC) * B).astype(jnp.int32)
    col_start = ((block_local % BC) * B).astype(jnp.int32)
    kernel_row = (owner_exp * CELLS + psf_cell).astype(jnp.int32)

    def one_piece(canvas, item):
        row_first, col_first, kernel_index, observed, keep = item
        patch = lax.dynamic_slice(padded, (row_first, col_first), (extent, extent))
        kernel = psf_table[kernel_index].astype(jnp.float32).reshape(PSF, PSF)
        predicted = correlate(patch, kernel, B)
        residual = (keep.astype(jnp.float32) * (predicted - observed.astype(jnp.float32))).astype(jnp.bfloat16)
        widened = jnp.pad(residual.astype(jnp.float32), 2 * HALO)
        adjoint = correlate(widened, kernel[::-1, ::-1], extent)
        current = lax.dynamic_slice(canvas, (row_first, col_first), (extent, extent))
        canvas = lax.dynamic_update_slice(canvas, current + adjoint, (row_first, col_first))
        return canvas, residual

    start = jnp.zeros(padded.shape, jnp.float32)
    canvas, residuals = lax.scan(one_piece, start, (row_start, col_start, kernel_row, exposure_data, pixel_mask))
    return canvas[HALO:-HALO, HALO:-HALO], residuals
```

```python
import jax
import jax.numpy as jnp
from jax import lax
from jax.experimental import pallas as pl
from jax.experimental.pallas import tpu as pltpu
from jax.sharding import PartitionSpec as P

B = 128
PSF = 41
HALO = 20
CAP = 2

G = 16
LANES = 128
OUT = B // G
EXT = 11
REACH = 4
LEAD = 28
FWD_ROWS = 88
BLK_ROWS = 96
SLOT_ROWS = 128
PITCH = 72
TILES = 6
RES_LEAD = 40
F32 = jnp.float32
BF16 = jnp.bfloat16


def from_behind(x, axis, by):
    devices = lax.axis_size(axis)
    pairs = [(i, i + by) for i in range(devices) if 0 <= i + by < devices]
    return lax.ppermute(x, axis, pairs)


def swap_groups(x):
    sub = lax.broadcasted_iota(jnp.int32, x.shape, 1)
    group = lax.broadcasted_iota(jnp.int32, x.shape, 2) // G
    for d in (4, 2, 1):
        sub_bit, group_bit = (sub & d) != 0, (group & d) != 0
        up = pltpu.roll(pltpu.roll(x, 8 - d, 1), G * d, 2)
        down = up if d == 4 else pltpu.roll(pltpu.roll(x, d, 1), LANES - G * d, 2)
        x = jnp.where(sub_bit == group_bit, x, jnp.where(group_bit, up, down))
    return x


def regroup_kernel(data_ref, keep_ref, data_out, keep_out, scratch):
    for source, target in ((data_ref, data_out), (keep_ref, keep_out)):
        blocks = swap_groups(source[0].astype(F32).reshape(2 * OUT, 8, LANES))
        scratch[...] = jnp.zeros_like(scratch)
        for row in range(2 * OUT):
            half = row % 2
            scratch[pl.ds(EXT * (row // 2), 8), half * LANES : (half + 1) * LANES] = blocks[row]
        target[0] = scratch[...].astype(BF16)


def regroup(exposure_data, pixel_mask):
    pieces = exposure_data.shape[0]
    block = pl.BlockSpec((1, B, B), lambda p: (p, 0, 0))
    out = pl.BlockSpec((1, BLK_ROWS, 2 * LANES), lambda p: (p, 0, 0))
    shape = jax.ShapeDtypeStruct((pieces, BLK_ROWS, 2 * LANES), BF16)
    return pl.pallas_call(
        regroup_kernel,
        grid=(pieces,),
        in_specs=[block, block],
        out_specs=[out, out],
        out_shape=[shape, shape],
        scratch_shapes=[pltpu.VMEM((BLK_ROWS, 2 * LANES), F32)],
        cost_estimate=pl.CostEstimate(flops=4_000_000, bytes_accessed=4_000_000, transcendentals=0),
        name="regroup",
    )(exposure_data, pixel_mask)


def tap_rows(table):
    cells = table.shape[0]
    kernel = jnp.pad(table.reshape(cells, PSF, PSF), ((0, 0), (8, 7), (G, 23)))
    windows = jnp.stack([kernel[:, :, G * t : G * t + 2 * G] for t in range(REACH)], 1)
    windows = windows.reshape(cells, REACH, 28, 2, 2 * G).transpose(0, 1, 3, 2, 4)
    windows = windows.reshape(cells, 2 * REACH, 28 * 2 * G)
    rows = jnp.stack([windows[:, :, 2 * G * c : 2 * G * c + TILES * LANES] for c in range(5)], 2)
    return rows.reshape(cells, REACH, 10, TILES * LANES).astype(F32)


def taps_kernel(rows_ref, out_ref):
    odd = (lax.broadcasted_iota(jnp.int32, (G, LANES), 1) // G) % 2 == 1

    def per_shift(t, carry):
        for phase in range(8):
            parts = []
            for parity in range(2):
                first = parity - phase
                parts.append((first % 2) * 5 + (first - first % 2) // 2 + 4)
            for tile in range(TILES):
                lanes = slice(tile * LANES, (tile + 1) * LANES)
                even_row, odd_row = (
                    jnp.broadcast_to(rows_ref[0, t, part : part + 1, lanes], (G, LANES))
                    for part in parts
                )
                even_row = pltpu.roll(even_row, LANES - G, 1, stride=1, stride_axis=0)
                odd_row = pltpu.roll(odd_row, 0, 1, stride=1, stride_axis=0)
                start = pl.multiple_of(t * LANES + phase * G, G)
                out_ref[0, pl.ds(start, G), lanes] = jnp.where(odd, odd_row, even_row).astype(BF16)
        return carry

    lax.fori_loop(0, REACH, per_shift, 0)


def build_taps(rows):
    cells = rows.shape[0]
    return pl.pallas_call(
        taps_kernel,
        grid=(cells,),
        in_specs=[pl.BlockSpec((1, REACH, 10, TILES * LANES), lambda c: (c, 0, 0, 0))],
        out_specs=pl.BlockSpec((1, REACH * LANES, TILES * LANES), lambda c: (c, 0, 0)),
        out_shape=jax.ShapeDtypeStruct((cells, REACH * LANES, TILES * LANES), BF16),
        cost_estimate=pl.CostEstimate(flops=20_000_000, bytes_accessed=40_000_000, transcendentals=0),
        name="taps",
    )(rows)


def blocks_kernel(stripe_ref, out_ref):
    for tile in range(PITCH // 8):
        part = stripe_ref[:, tile * LANES : (tile + 1) * LANES].astype(F32)
        out_ref[:, tile * 8 : (tile + 1) * 8, :] = swap_groups(part.reshape(2, 8, LANES))


def stripe_blocks(stripe):
    rows = stripe.shape[0] // 8
    return pl.pallas_call(
        blocks_kernel,
        grid=(rows // 2,),
        in_specs=[pl.BlockSpec((G, PITCH * G), lambda r: (r, 0))],
        out_specs=pl.BlockSpec((2, PITCH, LANES), lambda r: (r, 0, 0)),
        out_shape=jax.ShapeDtypeStruct((rows, PITCH, LANES), F32),
        cost_estimate=pl.CostEstimate(flops=4_000_000, bytes_accessed=2_000_000, transcendentals=0),
        name="blocks",
    )(stripe)


def cut_kernel(per_row, ids_ref, blocks_ref, out_ref, scratch):
    wanted = ids_ref[pl.program_id(0)]

    @pl.when(wanted >= 0)
    def _():
        first_row = wanted // per_row * (2 * OUT)
        first_col = pl.multiple_of(wanted % per_row * OUT, 8)
        for row in range(EXT):
            for half in range(2):
                part = blocks_ref[first_row + 2 * row + half, pl.ds(first_col, G), :]
                scratch[pl.ds(EXT * row, G), half * LANES : (half + 1) * LANES] = part
        out_ref[0] = scratch[...].astype(BF16)


def cut_patches(ids, blocks, per_row):
    slots = ids.shape[0]
    return pl.pallas_call(
        lambda *refs: cut_kernel(per_row, *refs),
        grid_spec=pltpu.PrefetchScalarGridSpec(
            num_scalar_prefetch=1,
            grid=(slots,),
            in_specs=[pl.BlockSpec(blocks.shape, lambda n, ids: (0, 0, 0))],
            out_specs=pl.BlockSpec((1, SLOT_ROWS, 2 * LANES), lambda n, ids: (n, 0, 0)),
            scratch_shapes=[pltpu.VMEM((SLOT_ROWS, 2 * LANES), F32)],
        ),
        out_shape=jax.ShapeDtypeStruct((slots, SLOT_ROWS, 2 * LANES), BF16),
        cost_estimate=pl.CostEstimate(flops=1_000_000, bytes_accessed=4_000_000, transcendentals=0),
        name="cut",
    )(ids, blocks)


def convolve(read, taps_ref, rows):
    total = jnp.zeros((rows, 2 * LANES), F32)
    for t in range(REACH):
        taps = slice(t * LANES, (t + 1) * LANES)
        for s in range(REACH - 1):
            upper = taps_ref[0, taps, 2 * s * LANES : (2 * s + 2) * LANES]
            if s == 0:
                lower = jnp.concatenate(
                    [jnp.zeros((LANES, LANES), BF16), taps_ref[0, taps, 0:LANES]], axis=1
                )
            else:
                lower = taps_ref[0, taps, (2 * s - 1) * LANES : (2 * s + 1) * LANES]
            total = total + jnp.dot(
                read(s, t), jnp.concatenate([upper, lower], axis=0), preferred_element_type=F32
            )
    last = jnp.zeros((rows, LANES), F32)
    for t in range(0, REACH, 2):
        field = jnp.concatenate(
            [read(REACH - 1, t)[:, LANES:], read(REACH - 1, t + 1)[:, LANES:]], axis=1
        )
        taps = taps_ref[0, t * LANES : (t + 2) * LANES, (TILES - 1) * LANES :]
        last = last + jnp.dot(field, taps, preferred_element_type=F32)
    return jnp.concatenate([total[:, :LANES] + last, total[:, LANES:]], axis=1)


def piece_kernel(
    slot_ref, cell_ref, patch_ref, forward_ref, adjoint_ref, data_ref, keep_ref, adj_out, res_out, field, resid
):
    @pl.when(pl.program_id(0) == 0)
    def _():
        resid[...] = jnp.zeros_like(resid)

    field[...] = patch_ref[0].astype(F32)

    def read_patch(s, t):
        start = EXT * (REACH - 1 - s) + REACH - 1 - t
        return field[pl.ds(start, FWD_ROWS), :].astype(BF16)

    predicted = convolve(read_patch, forward_ref, FWD_ROWS)
    observed = data_ref[0, :FWD_ROWS].astype(F32)
    keep = keep_ref[0, :FWD_ROWS].astype(F32)
    residual = jnp.where(keep != 0, predicted - observed, 0.0).astype(BF16)
    res_out[0, :FWD_ROWS] = residual
    resid[RES_LEAD : RES_LEAD + FWD_ROWS, :] = residual.astype(F32)

    def read_residual(s, t):
        return resid[pl.ds(RES_LEAD - EXT * s - t, SLOT_ROWS), :].astype(BF16)

    adj_out[0] = convolve(read_residual, adjoint_ref, SLOT_ROWS).astype(BF16)


def pieces(slots, cells, patches, all_taps, data, keep):
    count = data.shape[0]
    cell_count = all_taps.shape[0] // 2
    slot = pl.BlockSpec((1, SLOT_ROWS, 2 * LANES), lambda p, slots, cells: (slots[p], 0, 0))
    taps_shape = (1, REACH * LANES, TILES * LANES)
    forward = pl.BlockSpec(taps_shape, lambda p, slots, cells: (cells[p], 0, 0))
    adjoint = pl.BlockSpec(taps_shape, lambda p, slots, cells: (cells[p] + cell_count, 0, 0))
    block = pl.BlockSpec((1, BLK_ROWS, 2 * LANES), lambda p, slots, cells: (p, 0, 0))
    return pl.pallas_call(
        piece_kernel,
        grid_spec=pltpu.PrefetchScalarGridSpec(
            num_scalar_prefetch=2,
            grid=(count,),
            in_specs=[slot, forward, adjoint, block, block],
            out_specs=[slot, block],
            scratch_shapes=[
                pltpu.VMEM((SLOT_ROWS, 2 * LANES), F32),
                pltpu.VMEM((RES_LEAD + SLOT_ROWS, 2 * LANES), F32),
            ],
        ),
        out_shape=[
            jax.ShapeDtypeStruct(patches.shape, BF16),
            jax.ShapeDtypeStruct(data.shape, BF16),
        ],
        cost_estimate=pl.CostEstimate(
            flops=14_000_000_000, bytes_accessed=40_000_000, transcendentals=0
        ),
        name="pieces",
    )(slots, cells, patches, all_taps, all_taps, data, keep)


def ungroup_kernel(res_ref, out_ref, scratch):
    scratch[...] = res_ref[0].astype(F32)
    for row in range(OUT):
        halves = [
            scratch[pl.ds(EXT * row, 8), half * LANES : (half + 1) * LANES] for half in range(2)
        ]
        rows = swap_groups(jnp.stack(halves, 0)).reshape(G, LANES)
        out_ref[0, row * G : (row + 1) * G, :] = rows.astype(BF16)


def ungroup(residual):
    count = residual.shape[0]
    return pl.pallas_call(
        ungroup_kernel,
        grid=(count,),
        in_specs=[pl.BlockSpec((1, BLK_ROWS, 2 * LANES), lambda p: (p, 0, 0))],
        out_specs=pl.BlockSpec((1, B, B), lambda p: (p, 0, 0)),
        out_shape=jax.ShapeDtypeStruct((count, B, B), BF16),
        scratch_shapes=[pltpu.VMEM((BLK_ROWS, 2 * LANES), F32)],
        cost_estimate=pl.CostEstimate(flops=4_000_000, bytes_accessed=2_000_000, transcendentals=0),
        name="ungroup",
    )(residual)


def fold_kernel(per_row, rows, ids_ref, slot_ref, out_ref, canvas, scratch):
    step = pl.program_id(0)

    @pl.when(step == 0)
    def _():
        canvas[...] = jnp.zeros_like(canvas)

    named = ids_ref[step]

    @pl.when(named >= 0)
    def _():
        first_row = named // per_row * (2 * OUT)
        first_col = pl.multiple_of(named % per_row * OUT, 8)
        scratch[...] = slot_ref[0].astype(F32)
        inside = lax.broadcasted_iota(jnp.int32, (G, LANES), 0) < EXT
        for row in range(EXT):
            for half in range(2):
                part = scratch[pl.ds(EXT * row, G), half * LANES : (half + 1) * LANES]
                part = jnp.where(inside, part, 0.0)
                at = (first_row + 2 * row + half, pl.ds(first_col, G), slice(None))
                canvas[at] = canvas[at] + part

    @pl.when(step == pl.num_programs(0) - 1)
    def _():
        near = lax.broadcasted_iota(jnp.int32, (G, LANES), 1) < LANES - HALO

        def per_row_pair(pair, carry):
            tiles = []
            for half in range(2):
                tiles.append(swap_groups(canvas[2 * pair + half].reshape(PITCH // 8, 8, LANES)))
            turned = [
                pltpu.roll(
                    jnp.concatenate([tiles[0][c], tiles[1][c]], axis=0), LANES - HALO, 1
                )
                for c in range(per_row + 1)
            ]
            start = pl.multiple_of(pair * G, G)
            for c in range(per_row):
                both = jnp.where(near, turned[c], turned[c + 1])
                out_ref[c, pl.ds(start, G), :] = both.astype(BF16)
            return carry

        lax.fori_loop(0, rows // G, per_row_pair, 0)


def fold(ids, received, per_row, rows):
    slots = ids.shape[0]
    return pl.pallas_call(
        lambda *refs: fold_kernel(per_row, rows, *refs),
        grid_spec=pltpu.PrefetchScalarGridSpec(
            num_scalar_prefetch=1,
            grid=(slots,),
            in_specs=[pl.BlockSpec((1, SLOT_ROWS, 2 * LANES), lambda n, ids: (n, 0, 0))],
            out_specs=pl.BlockSpec((per_row, rows, LANES), lambda n, ids: (0, 0, 0)),
            scratch_shapes=[
                pltpu.VMEM((rows // 8, PITCH, LANES), F32),
                pltpu.VMEM((SLOT_ROWS, 2 * LANES), F32),
            ],
        ),
        out_shape=jax.ShapeDtypeStruct((per_row, rows, LANES), BF16),
        cost_estimate=pl.CostEstimate(flops=8_000_000, bytes_accessed=3_000_000, transcendentals=0),
        name="fold",
    )(ids, received)


def shards(sky_model, exposure_data, pixel_mask, block_owner, block_local, psf_cell, psf_table):
    sky_count = lax.axis_size("sky")
    stripe_rows, stripe_cols = sky_model.shape
    per_row = stripe_cols // B
    piece_count = exposure_data.shape[0]
    slot_total = sky_count * CAP
    owner_sky = block_owner[:, 0]
    earlier = lax.broadcasted_iota(jnp.int32, (piece_count, piece_count), 1) < lax.broadcasted_iota(
        jnp.int32, (piece_count, piece_count), 0
    )
    same_owner = owner_sky[:, None] == owner_sky[None, :]
    rank_within = jnp.sum((same_owner & earlier).astype(jnp.int32), axis=1)
    slot_index = owner_sky * CAP + rank_within
    named = slot_index[None, :] == lax.broadcasted_iota(jnp.int32, (slot_total, 1), 0)
    requests = jnp.sum(jnp.where(named, block_local[None, :] + 1, 0), axis=1) - 1
    asked = lax.all_to_all(
        requests.reshape(sky_count, CAP), "sky", split_axis=0, concat_axis=0, tiled=True
    ).reshape(slot_total)

    above = from_behind(sky_model[stripe_rows - LEAD :], "sky", 1)
    below = from_behind(sky_model[:HALO], "sky", -1)
    stripe = jnp.concatenate([above, sky_model, below], axis=0)
    stripe = jnp.pad(stripe, ((0, 0), (LEAD, PITCH * G - LEAD - stripe_cols)))
    blocks = stripe_blocks(stripe)
    data, keep = regroup(exposure_data, pixel_mask)
    outgoing = cut_patches(asked, blocks, per_row)
    patches = lax.all_to_all(outgoing, "sky", split_axis=0, concat_axis=0, tiled=True)

    table, _ = lax.optimization_barrier((psf_table, outgoing))
    taps = build_taps(tap_rows(jnp.concatenate([table[:, ::-1], table], axis=0)))
    adjoints, residuals = pieces(slot_index, psf_cell, patches, taps, data, keep)
    received = lax.all_to_all(adjoints, "sky", split_axis=0, concat_axis=0, tiled=True)
    residual = ungroup(residuals)

    rows = stripe_rows + LEAD + HALO
    partial = fold(asked, received, per_row, rows)
    terms = lax.all_to_all(partial, "exp", split_axis=0, concat_axis=0, tiled=True)
    canvas = jnp.sum(terms.astype(F32), axis=0)
    from_below = from_behind(canvas[:HALO].astype(BF16), "sky", -1).astype(F32)
    from_above = from_behind(
        canvas[HALO + stripe_rows : stripe_rows + 2 * HALO].astype(BF16), "sky", 1
    ).astype(F32)
    gradient = (
        canvas[HALO : stripe_rows + HALO]
        + jnp.pad(from_above, ((0, stripe_rows - HALO), (0, 0)))
        + jnp.pad(from_below, ((stripe_rows - HALO, 0), (0, 0)))
    )
    return (gradient, residual)


def solution(mesh):
    in_specs = (
        P("sky", None),
        P(("sky", "exp"), None, None),
        P(("sky", "exp"), None, None),
        P(("sky", "exp"), None),
        P(("sky", "exp")),
        P(("sky", "exp")),
        P("exp", None),
    )
    out_specs = (P("sky", "exp"), P(("sky", "exp"), None, None))
    return jax.shard_map(shards, mesh=mesh, in_specs=in_specs, out_specs=out_specs, check_vma=False)
```

```python
import jax
import jax.numpy as jnp
from jax import lax
from jax.experimental import pallas as pl
from jax.experimental.pallas import tpu as pltpu
from jax.sharding import PartitionSpec as P

B = 128
PSF = 41
HALO = 20
CAP = 2

G = 16
LANES = 128
OUT = B // G
EXT = 11
REACH = 4
LEAD = 28
FWD_ROWS = 88
BLK_ROWS = 96
SLOT_ROWS = 128
PITCH = 72
TILES = 6
RES_LEAD = 40
BATCH = 4
SLOTS = 8
CHUNK = 9
CHUNK_ROWS = 352
SHIFT = 4
SMALL = pl.CostEstimate(flops=1000, bytes_accessed=1000, transcendentals=0)
F32 = jnp.float32
BF16 = jnp.bfloat16


def from_behind(x, axis, by):
    devices = lax.axis_size(axis)
    pairs = [(i, i + by) for i in range(devices) if 0 <= i + by < devices]
    return lax.ppermute(x, axis, pairs)


def swap_groups(x):
    sub = lax.broadcasted_iota(jnp.int32, x.shape, 1)
    group = lax.broadcasted_iota(jnp.int32, x.shape, 2) // G
    for d in (4, 2, 1):
        sub_bit, group_bit = (sub & d) != 0, (group & d) != 0
        up = pltpu.roll(pltpu.roll(x, 8 - d, 1), G * d, 2)
        down = up if d == 4 else pltpu.roll(pltpu.roll(x, d, 1), LANES - G * d, 2)
        x = jnp.where(sub_bit == group_bit, x, jnp.where(group_bit, up, down))
    return x


def regroup_kernel(data_ref, keep_ref, data_out, keep_out, scratch):
    def per_piece(p, carry):
        for source, target in ((data_ref, data_out), (keep_ref, keep_out)):
            blocks = swap_groups(source[p].astype(F32).reshape(2 * OUT, 8, LANES))
            scratch[...] = jnp.zeros_like(scratch)
            for row in range(2 * OUT):
                half = row % 2
                scratch[pl.ds(EXT * (row // 2), 8), half * LANES : (half + 1) * LANES] = blocks[row]
            target[p] = scratch[...].astype(BF16)
        return carry

    lax.fori_loop(0, data_ref.shape[0], per_piece, 0)


def regroup(exposure_data, pixel_mask):
    pieces = exposure_data.shape[0]
    block = pl.BlockSpec((BATCH, B, B), lambda p: (p, 0, 0))
    out = pl.BlockSpec((BATCH, BLK_ROWS, 2 * LANES), lambda p: (p, 0, 0))
    shape = jax.ShapeDtypeStruct((pieces, BLK_ROWS, 2 * LANES), BF16)
    return pl.pallas_call(
        regroup_kernel,
        grid=(pieces // BATCH,),
        in_specs=[block, block],
        out_specs=[out, out],
        out_shape=[shape, shape],
        scratch_shapes=[pltpu.VMEM((BLK_ROWS, 2 * LANES), F32)],
        cost_estimate=SMALL,
        name="regroup",
    )(exposure_data, pixel_mask)


def tap_rows(table):
    cells = table.shape[0]
    kernel = jnp.pad(table.reshape(cells, PSF, PSF), ((0, 0), (0, 7), (G, 23)))
    kernel = kernel.reshape(cells, 24, 2, 5 * G).transpose(0, 2, 1, 3)
    windows = [kernel[..., G * t : G * t + 2 * G].reshape(cells, 2, TILES * LANES) for t in range(REACH)]
    return jnp.stack(windows, 1).astype(F32)


def taps_kernel(rows_ref, out_ref):
    lane = lax.broadcasted_iota(jnp.int32, (G, LANES), 1)
    odd = (lane // G) % 2 == 1

    def per_shift(t, carry):
        before = jnp.zeros((G, LANES), BF16)
        for tile in range(TILES):
            lanes = slice(tile * LANES, (tile + 1) * LANES)
            even_row, odd_row = (
                jnp.broadcast_to(rows_ref[0, t, parity : parity + 1, lanes], (G, LANES))
                for parity in range(2)
            )
            even_row = pltpu.roll(even_row, LANES - G, 1, stride=1, stride_axis=0)
            odd_row = pltpu.roll(odd_row, 0, 1, stride=1, stride_axis=0)
            now = jnp.where(odd, odd_row, even_row).astype(BF16)
            for phase in range(8):
                if phase == 0:
                    part = now
                else:
                    part = pltpu.roll(jnp.where(lane < LANES - G * phase, now, before), G * phase, 1)
                start = pl.multiple_of(t * LANES + phase * G, G)
                out_ref[0, pl.ds(start, G), lanes] = part
            before = now
        return carry

    lax.fori_loop(0, REACH, per_shift, 0)


def build_taps(rows):
    cells = rows.shape[0]
    return pl.pallas_call(
        taps_kernel,
        grid=(cells,),
        in_specs=[pl.BlockSpec((1, REACH, 2, TILES * LANES), lambda c: (c, 0, 0, 0))],
        out_specs=pl.BlockSpec((1, REACH * LANES, TILES * LANES), lambda c: (c, 0, 0)),
        out_shape=jax.ShapeDtypeStruct((cells, REACH * LANES, TILES * LANES), BF16),
        cost_estimate=SMALL,
        name="taps",
    )(rows)


def blocks_kernel(stripe_ref, out_ref):
    def per_row(r, carry):
        start = pl.multiple_of(r * G, G)
        for tile in range(PITCH // 8):
            part = stripe_ref[pl.ds(start, G), tile * LANES : (tile + 1) * LANES].astype(F32)
            out_ref[pl.ds(2 * r, 2), tile * 8 : (tile + 1) * 8, :] = swap_groups(
                part.reshape(2, 8, LANES)
            )
        return carry

    lax.fori_loop(0, stripe_ref.shape[0] // G, per_row, 0)


def stripe_blocks(stripe):
    rows = stripe.shape[0] // 8
    return pl.pallas_call(
        blocks_kernel,
        out_shape=jax.ShapeDtypeStruct((rows, PITCH, LANES), F32),
        in_specs=[pl.BlockSpec(memory_space=pltpu.VMEM)],
        out_specs=pl.BlockSpec(memory_space=pltpu.VMEM),
        cost_estimate=SMALL,
        name="blocks",
    )(stripe)


def cut_kernel(per_row, ids_ref, blocks_ref, out_ref, scratch):
    step = pl.program_id(0)

    def per_slot(n, carry):
        wanted = ids_ref[step * SLOTS + n]

        @pl.when(wanted >= 0)
        def _():
            first_row = wanted // per_row * (2 * OUT)
            first_col = pl.multiple_of(wanted % per_row * OUT, 8)
            for row in range(EXT):
                for half in range(2):
                    part = blocks_ref[first_row + 2 * row + half, pl.ds(first_col, G), :]
                    scratch[pl.ds(EXT * row, G), half * LANES : (half + 1) * LANES] = part
            out_ref[n] = scratch[...].astype(BF16)

        return carry

    lax.fori_loop(0, SLOTS, per_slot, 0)


def cut_patches(ids, blocks, per_row):
    slots = ids.shape[0]
    return pl.pallas_call(
        lambda *refs: cut_kernel(per_row, *refs),
        grid_spec=pltpu.PrefetchScalarGridSpec(
            num_scalar_prefetch=1,
            grid=(slots // SLOTS,),
            in_specs=[pl.BlockSpec(blocks.shape, lambda n, ids: (0, 0, 0))],
            out_specs=pl.BlockSpec((SLOTS, SLOT_ROWS, 2 * LANES), lambda n, ids: (n, 0, 0)),
            scratch_shapes=[pltpu.VMEM((SLOT_ROWS, 2 * LANES), F32)],
        ),
        out_shape=jax.ShapeDtypeStruct((slots, SLOT_ROWS, 2 * LANES), BF16),
        cost_estimate=SMALL,
        name="cut",
    )(ids, blocks)


def convolve(read, taps_ref, rows):
    total = jnp.zeros((rows, 2 * LANES), F32)
    for t in range(REACH):
        taps = slice(t * LANES, (t + 1) * LANES)
        for s in range(REACH - 1):
            upper = taps_ref[0, taps, 2 * s * LANES : (2 * s + 2) * LANES]
            if s == 0:
                lower = jnp.concatenate(
                    [jnp.zeros((LANES, LANES), BF16), taps_ref[0, taps, 0:LANES]], axis=1
                )
            else:
                lower = taps_ref[0, taps, (2 * s - 1) * LANES : (2 * s + 1) * LANES]
            total = total + jnp.dot(
                read(s, t), jnp.concatenate([upper, lower], axis=0), preferred_element_type=F32
            )
    last = jnp.zeros((rows, LANES), F32)
    for t in range(0, REACH, 2):
        field = jnp.concatenate(
            [read(REACH - 1, t)[:, LANES:], read(REACH - 1, t + 1)[:, LANES:]], axis=1
        )
        taps = taps_ref[0, t * LANES : (t + 2) * LANES, (TILES - 1) * LANES :]
        last = last + jnp.dot(field, taps, preferred_element_type=F32)
    return jnp.concatenate([total[:, :LANES] + last, total[:, LANES:]], axis=1)


def piece_kernel(
    slot_ref, cell_ref, patch_ref, forward_ref, adjoint_ref, data_ref, keep_ref, adj_out, res_out, field, resid
):
    @pl.when(pl.program_id(0) == 0)
    def _():
        resid[...] = jnp.zeros_like(resid)

    field[...] = patch_ref[0].astype(F32)

    def read_patch(s, t):
        start = EXT * (REACH - 1 - s) + REACH - 1 - t
        return field[pl.ds(start, FWD_ROWS), :].astype(BF16)

    predicted = convolve(read_patch, forward_ref, FWD_ROWS)
    observed = data_ref[0, :FWD_ROWS].astype(F32)
    keep = keep_ref[0, :FWD_ROWS].astype(F32)
    residual = jnp.where(keep != 0, predicted - observed, 0.0).astype(BF16)
    res_out[0, :FWD_ROWS] = residual
    resid[RES_LEAD : RES_LEAD + FWD_ROWS, :] = residual.astype(F32)

    def read_residual(s, t):
        return resid[pl.ds(RES_LEAD - EXT * s - t, SLOT_ROWS), :].astype(BF16)

    adj_out[0] = convolve(read_residual, adjoint_ref, SLOT_ROWS).astype(BF16)


def pieces(slots, cells, patches, all_taps, data, keep):
    count = data.shape[0]
    cell_count = all_taps.shape[0] // 2
    slot = pl.BlockSpec((1, SLOT_ROWS, 2 * LANES), lambda p, slots, cells: (slots[p], 0, 0))
    taps_shape = (1, REACH * LANES, TILES * LANES)
    forward = pl.BlockSpec(taps_shape, lambda p, slots, cells: (cells[p], 0, 0))
    adjoint = pl.BlockSpec(taps_shape, lambda p, slots, cells: (cells[p] + cell_count, 0, 0))
    block = pl.BlockSpec((1, BLK_ROWS, 2 * LANES), lambda p, slots, cells: (p, 0, 0))
    return pl.pallas_call(
        piece_kernel,
        grid_spec=pltpu.PrefetchScalarGridSpec(
            num_scalar_prefetch=2,
            grid=(count,),
            in_specs=[slot, forward, adjoint, block, block],
            out_specs=[slot, block],
            scratch_shapes=[
                pltpu.VMEM((SLOT_ROWS, 2 * LANES), F32),
                pltpu.VMEM((RES_LEAD + SLOT_ROWS, 2 * LANES), F32),
            ],
        ),
        out_shape=[
            jax.ShapeDtypeStruct(patches.shape, BF16),
            jax.ShapeDtypeStruct(data.shape, BF16),
        ],
        cost_estimate=SMALL,
        name="pieces",
    )(slots, cells, patches, all_taps, all_taps, data, keep)


def ungroup_kernel(res_ref, out_ref, scratch):
    def per_piece(p, carry):
        scratch[...] = res_ref[p].astype(F32)
        for row in range(OUT):
            halves = [
                scratch[pl.ds(EXT * row, 8), half * LANES : (half + 1) * LANES] for half in range(2)
            ]
            rows = swap_groups(jnp.stack(halves, 0)).reshape(G, LANES)
            out_ref[p, row * G : (row + 1) * G, :] = rows.astype(BF16)
        return carry

    lax.fori_loop(0, res_ref.shape[0], per_piece, 0)


def ungroup(residual):
    count = residual.shape[0]
    return pl.pallas_call(
        ungroup_kernel,
        grid=(count // BATCH,),
        in_specs=[pl.BlockSpec((BATCH, BLK_ROWS, 2 * LANES), lambda p: (p, 0, 0))],
        out_specs=pl.BlockSpec((BATCH, B, B), lambda p: (p, 0, 0)),
        out_shape=jax.ShapeDtypeStruct((count, B, B), BF16),
        scratch_shapes=[pltpu.VMEM((BLK_ROWS, 2 * LANES), F32)],
        cost_estimate=SMALL,
        name="ungroup",
    )(residual)


def fold_kernel(per_row, half_rows, ids_ref, slot_ref, out_ref, canvas, scratch, packed):
    step = pl.program_id(0)

    @pl.when(step == 0)
    def _():
        canvas[...] = jnp.zeros_like(canvas)

    inside = lax.broadcasted_iota(jnp.int32, (G, LANES), 0) < EXT

    def per_slot(n, carry):
        named = ids_ref[step * SLOTS + n]

        @pl.when(named >= 0)
        def _():
            first_row = named // per_row * (2 * OUT)
            first_col = pl.multiple_of(named % per_row * OUT, 8)
            scratch[...] = slot_ref[n].astype(F32)
            for row in range(EXT):
                for half in range(2):
                    part = scratch[pl.ds(EXT * row, G), half * LANES : (half + 1) * LANES]
                    part = jnp.where(inside, part, 0.0)
                    at = (first_row + 2 * row + half, pl.ds(first_col, G), slice(None))
                    canvas[at] = canvas[at] + part

        return carry

    lax.fori_loop(0, SLOTS, per_slot, 0)

    @pl.when(step == pl.num_programs(0) - 1)
    def _():
        for chunk in range(per_row):
            first = OUT * chunk + 1
            for row in range(half_rows):
                packed[CHUNK * row : CHUNK * row + G, :] = canvas[row, first : first + G, :]
            out_ref[chunk] = packed[...].astype(BF16)


def fold(ids, received, per_row, half_rows):
    slots = ids.shape[0]
    return pl.pallas_call(
        lambda *refs: fold_kernel(per_row, half_rows, *refs),
        grid_spec=pltpu.PrefetchScalarGridSpec(
            num_scalar_prefetch=1,
            grid=(slots // SLOTS,),
            in_specs=[pl.BlockSpec((SLOTS, SLOT_ROWS, 2 * LANES), lambda n, ids: (n, 0, 0))],
            out_specs=pl.BlockSpec((per_row, CHUNK_ROWS, LANES), lambda n, ids: (0, 0, 0)),
            scratch_shapes=[
                pltpu.VMEM((half_rows, PITCH + 8, LANES), F32),
                pltpu.VMEM((SLOT_ROWS, 2 * LANES), F32),
                pltpu.VMEM((CHUNK_ROWS, LANES), F32),
            ],
        ),
        out_shape=jax.ShapeDtypeStruct((per_row, CHUNK_ROWS, LANES), BF16),
        cost_estimate=SMALL,
        name="fold",
    )(ids, received)


def finish_kernel(half_rows, terms_ref, up_out, middle_out, down_out, summed, canvas):
    total = terms_ref[0].astype(F32)
    for term in range(1, terms_ref.shape[0]):
        total = total + terms_ref[term].astype(F32)
    summed[...] = total
    near = lax.broadcasted_iota(jnp.int32, (8, LANES), 1) < LANES - SHIFT
    for row in range(half_rows):
        first = CHUNK * row
        tiles = swap_groups(summed[first : first + G, :].reshape(2, 8, LANES))
        tile = pltpu.roll(tiles[0], LANES - SHIFT, 1)
        edge = pltpu.roll(tiles[1], LANES - SHIFT, 1)
        canvas[8 * row : 8 * row + 8, :] = jnp.where(near, tile, edge)
    middle = middle_out.shape[0]
    up_out[...] = canvas[:HALO, :].astype(BF16)
    middle_out[...] = canvas[HALO : HALO + middle, :]
    down_out[...] = canvas[HALO + middle : 2 * HALO + middle, :].astype(BF16)


def finish(terms, half_rows, rows):
    rim = jax.ShapeDtypeStruct((HALO, LANES), BF16)
    vmem = pl.BlockSpec(memory_space=pltpu.VMEM)
    return pl.pallas_call(
        lambda *refs: finish_kernel(half_rows, *refs),
        in_specs=[vmem],
        out_specs=[vmem, vmem, vmem],
        out_shape=[rim, jax.ShapeDtypeStruct((rows, LANES), F32), rim],
        scratch_shapes=[
            pltpu.VMEM((CHUNK_ROWS, LANES), F32),
            pltpu.VMEM((8 * half_rows, LANES), F32),
        ],
        cost_estimate=SMALL,
        name="finish",
    )(terms)


def shards(sky_model, exposure_data, pixel_mask, block_owner, block_local, psf_cell, psf_table):
    sky_count = lax.axis_size("sky")
    stripe_rows, stripe_cols = sky_model.shape
    per_row = stripe_cols // B
    block_total = stripe_rows // B * per_row
    piece_count = exposure_data.shape[0]
    owner_sky = block_owner[:, 0]
    code = lax.broadcasted_iota(jnp.int32, (piece_count,), 0) * block_total + block_local
    mine = owner_sky[None, :] == lax.broadcasted_iota(jnp.int32, (sky_count, 1), 0)
    first = jnp.min(jnp.where(mine, code[None, :], piece_count * block_total), axis=1)
    last = jnp.max(jnp.where(mine, code[None, :], -1), axis=1)
    requests = jnp.stack(
        [
            jnp.where(last < 0, -1, first % block_total),
            jnp.where(last > first, last % block_total, -1),
        ],
        axis=1,
    )
    asked = lax.all_to_all(requests, "sky", split_axis=0, concat_axis=0, tiled=True)
    asked = asked.reshape(sky_count * CAP)

    above = from_behind(sky_model[stripe_rows - LEAD :], "sky", 1)
    below = from_behind(sky_model[:HALO], "sky", -1)
    stripe = jnp.concatenate([above, sky_model, below], axis=0)
    stripe = jnp.pad(stripe, ((0, 0), (LEAD, PITCH * G - LEAD - stripe_cols)))
    blocks = stripe_blocks(stripe)
    data, keep = regroup(exposure_data, pixel_mask)
    second = jnp.any(mine & (first[:, None] < code[None, :]), axis=0)
    slot_index = owner_sky * CAP + second.astype(jnp.int32)
    rows = tap_rows(jnp.concatenate([psf_table[:, ::-1], psf_table], axis=0))
    asked, blocks, data, keep, slot_index, rows = lax.optimization_barrier(
        (asked, blocks, data, keep, slot_index, rows)
    )
    outgoing = cut_patches(asked, blocks, per_row)
    patches = lax.all_to_all(outgoing, "sky", split_axis=0, concat_axis=0, tiled=True)
    rows, _ = lax.optimization_barrier((rows, outgoing))
    taps = build_taps(rows)
    adjoints, residuals = pieces(slot_index, psf_cell, patches, taps, data, keep)
    received = lax.all_to_all(adjoints, "sky", split_axis=0, concat_axis=0, tiled=True)
    received, residual = lax.optimization_barrier((received, ungroup(residuals)))

    half_rows = (stripe_rows + LEAD + HALO) // 8
    partial = fold(asked, received, per_row, half_rows)
    terms = lax.all_to_all(partial, "exp", split_axis=0, concat_axis=0, tiled=True)
    up, middle, down = finish(terms, half_rows, stripe_rows)
    from_below = from_behind(up, "sky", -1).astype(F32)
    from_above = from_behind(down, "sky", 1).astype(F32)
    gradient = (
        middle
        + jnp.pad(from_above, ((0, stripe_rows - HALO), (0, 0)))
        + jnp.pad(from_below, ((stripe_rows - HALO, 0), (0, 0)))
    )
    return (gradient, residual)


def solution(mesh):
    in_specs = (
        P("sky", None),
        P(("sky", "exp"), None, None),
        P(("sky", "exp"), None, None),
        P(("sky", "exp"), None),
        P(("sky", "exp")),
        P(("sky", "exp")),
        P("exp", None),
    )
    out_specs = (P("sky", "exp"), P(("sky", "exp"), None, None))
    return jax.shard_map(shards, mesh=mesh, in_specs=in_specs, out_specs=out_specs, check_vma=False)
```

```python
import jax
import jax.numpy as jnp
from jax import lax
from jax.experimental import pallas as pl
from jax.experimental.pallas import tpu as pltpu
from jax.sharding import PartitionSpec as P

B = 128
PSF = 41
HALO = 20
CAP = 2

G = 16
LANES = 128
OUT = B // G
EXT = 11
REACH = 4
LEAD = 28
FWD_ROWS = 88
BLK_ROWS = 96
SLOT_ROWS = 128
PITCH = 72
TILES = 6
RES_LEAD = 40
TAP_ROWS = 48
BATCH = 4
SLOTS = 8
CHUNK = 9
CHUNK_ROWS = 352
SHIFT = 4
VMEM_ALL = 60 << 20
SMALL = pl.CostEstimate(flops=1000, bytes_accessed=1000, transcendentals=0)
F32 = jnp.float32
BF16 = jnp.bfloat16


def from_behind(x, axis, by):
    devices = lax.axis_size(axis)
    pairs = [(i, i + by) for i in range(devices) if 0 <= i + by < devices]
    return lax.ppermute(x, axis, pairs)


def swap_groups(x):
    sub = lax.broadcasted_iota(jnp.int32, x.shape, 1)
    group = lax.broadcasted_iota(jnp.int32, x.shape, 2) // G
    for d in (4, 2, 1):
        sub_bit, group_bit = (sub & d) != 0, (group & d) != 0
        up = pltpu.roll(pltpu.roll(x, 8 - d, 1), G * d, 2)
        down = up if d == 4 else pltpu.roll(pltpu.roll(x, d, 1), LANES - G * d, 2)
        x = jnp.where(sub_bit == group_bit, x, jnp.where(group_bit, up, down))
    return x


def regroup_kernel(data_ref, keep_ref, out_ref, scratch):
    def per_piece(p, carry):
        known = jnp.where(keep_ref[p] != 0, data_ref[p].astype(F32), jnp.inf)
        blocks = swap_groups(known.reshape(2 * OUT, 8, LANES))
        scratch[...] = jnp.full_like(scratch, jnp.inf)
        for row in range(2 * OUT):
            half = row % 2
            scratch[pl.ds(EXT * (row // 2), 8), half * LANES : (half + 1) * LANES] = blocks[row]
        out_ref[p] = scratch[...].astype(BF16)
        return carry

    lax.fori_loop(0, data_ref.shape[0], per_piece, 0)


def regroup(exposure_data, pixel_mask):
    pieces = exposure_data.shape[0]
    block = pl.BlockSpec((BATCH, B, B), lambda p: (p, 0, 0))
    return pl.pallas_call(
        regroup_kernel,
        grid=(pieces // BATCH,),
        in_specs=[block, block],
        out_specs=pl.BlockSpec((BATCH, BLK_ROWS, 2 * LANES), lambda p: (p, 0, 0)),
        out_shape=jax.ShapeDtypeStruct((pieces, BLK_ROWS, 2 * LANES), BF16),
        scratch_shapes=[pltpu.VMEM((BLK_ROWS, 2 * LANES), F32)],
        cost_estimate=SMALL,
        name="regroup",
    )(exposure_data, pixel_mask)


def taps_kernel(kernel_ref, out_ref, windows, rows):
    lane = lax.broadcasted_iota(jnp.int32, (G, LANES), 1)
    odd = (lane // G) % 2 == 1
    wide = lax.broadcasted_iota(jnp.int32, (TAP_ROWS, LANES), 1) // (2 * G)
    quarter = lax.broadcasted_iota(jnp.int32, (TILES, LANES), 1) // (2 * G)

    def flip(size):
        first = lax.broadcasted_iota(jnp.int32, (size, size), 0)
        second = lax.broadcasted_iota(jnp.int32, (size, size), 1)
        return (first + second == PSF - 1).astype(BF16)

    plain = kernel_ref[0]
    turned = jnp.dot(flip(TAP_ROWS), plain, preferred_element_type=F32).astype(BF16)
    turned = jnp.dot(turned, flip(LANES), preferred_element_type=F32)
    for way, kernel in enumerate((turned, plain.astype(F32))):
        spread = pltpu.roll(kernel, G, 1)
        for t in range(1, REACH):
            spread = jnp.where(wide == t, pltpu.roll(kernel, G * t + G, 1), spread)
        windows[...] = spread
        for parity in range(2):
            picked = [windows[pl.ds(parity + 2 * q, TILES, stride=8), :] for q in range(4)]
            for t in range(REACH):
                row = picked[0] if t == 0 else pltpu.roll(picked[0], 2 * G * (4 - t), 1)
                for q in range(1, 4):
                    by = (q - t) % 4
                    part = picked[q] if by == 0 else pltpu.roll(picked[q], 2 * G * by, 1)
                    row = jnp.where(quarter == q, part, row)
                rows[t, parity, :TILES, :] = row

        def per_shift(t, carry):
            before = [jnp.zeros((G, LANES), F32)] * 8
            for tile in range(TILES):
                even_row, odd_row = (
                    jnp.broadcast_to(rows[t, parity, tile : tile + 1, :], (G, LANES))
                    for parity in range(2)
                )
                even_row = pltpu.roll(even_row, LANES - G, 1, stride=1, stride_axis=0)
                odd_row = pltpu.roll(odd_row, 0, 1, stride=1, stride_axis=0)
                now = jnp.where(odd, odd_row, even_row)
                turns = [now] + [pltpu.roll(now, G * phase, 1) for phase in range(1, 8)]
                for phase in range(8):
                    part = turns[phase]
                    if phase > 0:
                        part = jnp.where(lane < G * phase, before[phase], part)
                    start = pl.multiple_of(t * LANES + phase * G, G)
                    lanes = slice(tile * LANES, (tile + 1) * LANES)
                    out_ref[way, 0, pl.ds(start, G), lanes] = part.astype(BF16)
                before = turns
            return carry

        lax.fori_loop(0, REACH, per_shift, 0)


def build_taps(table):
    cells = table.shape[0]
    kernels = jnp.pad(
        table.reshape(cells, PSF, PSF), ((0, 0), (0, TAP_ROWS - PSF), (0, LANES - PSF))
    )
    return pl.pallas_call(
        taps_kernel,
        grid=(cells,),
        in_specs=[pl.BlockSpec((1, TAP_ROWS, LANES), lambda c: (c, 0, 0))],
        out_specs=pl.BlockSpec((2, 1, REACH * LANES, TILES * LANES), lambda c: (0, c, 0, 0)),
        out_shape=jax.ShapeDtypeStruct((2, cells, REACH * LANES, TILES * LANES), BF16),
        scratch_shapes=[
            pltpu.VMEM((TAP_ROWS, LANES), F32),
            pltpu.VMEM((REACH, 2, 8, LANES), F32),
        ],
        compiler_params=pltpu.CompilerParams(vmem_limit_bytes=VMEM_ALL),
        cost_estimate=SMALL,
        name="taps",
    )(kernels)


def blocks_kernel(stripe_ref, out_ref):
    def per_row(r, carry):
        start = pl.multiple_of(r * G, G)
        for tile in range(PITCH // 8):
            part = stripe_ref[pl.ds(start, G), tile * LANES : (tile + 1) * LANES].astype(F32)
            out_ref[pl.ds(2 * r, 2), tile * 8 : (tile + 1) * 8, :] = swap_groups(
                part.reshape(2, 8, LANES)
            )
        return carry

    lax.fori_loop(0, stripe_ref.shape[0] // G, per_row, 0)


def stripe_blocks(stripe):
    rows = stripe.shape[0] // 8
    return pl.pallas_call(
        blocks_kernel,
        out_shape=jax.ShapeDtypeStruct((rows, PITCH, LANES), F32),
        in_specs=[pl.BlockSpec(memory_space=pltpu.VMEM)],
        out_specs=pl.BlockSpec(memory_space=pltpu.VMEM),
        cost_estimate=SMALL,
        name="blocks",
    )(stripe)


def cut_kernel(per_row, ids_ref, blocks_ref, out_ref, scratch):
    step = pl.program_id(0)

    def per_slot(n, carry):
        wanted = ids_ref[step * SLOTS + n]

        @pl.when(wanted >= 0)
        def _():
            first_row = wanted // per_row * (2 * OUT)
            first_col = pl.multiple_of(wanted % per_row * OUT, 8)
            for row in range(EXT):
                for half in range(2):
                    part = blocks_ref[first_row + 2 * row + half, pl.ds(first_col, G), :]
                    scratch[pl.ds(EXT * row, G), half * LANES : (half + 1) * LANES] = part
            out_ref[n] = scratch[...].astype(BF16)

        return carry

    lax.fori_loop(0, SLOTS, per_slot, 0)


def cut_patches(ids, blocks, per_row):
    slots = ids.shape[0]
    return pl.pallas_call(
        lambda *refs: cut_kernel(per_row, *refs),
        grid_spec=pltpu.PrefetchScalarGridSpec(
            num_scalar_prefetch=1,
            grid=(slots // SLOTS,),
            in_specs=[pl.BlockSpec(blocks.shape, lambda n, ids: (0, 0, 0))],
            out_specs=pl.BlockSpec((SLOTS, SLOT_ROWS, 2 * LANES), lambda n, ids: (n, 0, 0)),
            scratch_shapes=[pltpu.VMEM((SLOT_ROWS, 2 * LANES), F32)],
        ),
        out_shape=jax.ShapeDtypeStruct((slots, SLOT_ROWS, 2 * LANES), BF16),
        cost_estimate=SMALL,
        name="cut",
    )(ids, blocks)


def convolve(read, taps_ref, rows):
    total = jnp.zeros((rows, 2 * LANES), F32)
    for t in range(REACH):
        taps = slice(t * LANES, (t + 1) * LANES)
        for s in range(REACH - 1):
            upper = taps_ref[0, 0, taps, 2 * s * LANES : (2 * s + 2) * LANES]
            if s == 0:
                lower = jnp.concatenate(
                    [jnp.zeros((LANES, LANES), BF16), taps_ref[0, 0, taps, 0:LANES]], axis=1
                )
            else:
                lower = taps_ref[0, 0, taps, (2 * s - 1) * LANES : (2 * s + 1) * LANES]
            total = total + jnp.dot(
                read(s, t), jnp.concatenate([upper, lower], axis=0), preferred_element_type=F32
            )
    last = jnp.zeros((rows, LANES), F32)
    for t in range(0, REACH, 2):
        field = jnp.concatenate(
            [read(REACH - 1, t)[:, LANES:], read(REACH - 1, t + 1)[:, LANES:]], axis=1
        )
        taps = taps_ref[0, 0, t * LANES : (t + 2) * LANES, (TILES - 1) * LANES :]
        last = last + jnp.dot(field, taps, preferred_element_type=F32)
    return jnp.concatenate([total[:, :LANES] + last, total[:, LANES:]], axis=1)


def piece_kernel(
    slot_ref, cell_ref, patch_ref, forward_ref, adjoint_ref, data_ref, adj_out, res_out, field, resid
):
    @pl.when(pl.program_id(0) == 0)
    def _():
        resid[...] = jnp.zeros_like(resid)

    field[...] = patch_ref[0].astype(F32)

    def read_patch(s, t):
        start = EXT * (REACH - 1 - s) + REACH - 1 - t
        return field[pl.ds(start, FWD_ROWS), :].astype(BF16)

    predicted = convolve(read_patch, forward_ref, FWD_ROWS)
    observed = data_ref[0, :FWD_ROWS].astype(F32)
    residual = jnp.where(observed < jnp.inf, predicted - observed, 0.0).astype(BF16)
    res_out[0, :FWD_ROWS] = residual
    resid[RES_LEAD : RES_LEAD + FWD_ROWS, :] = residual.astype(F32)

    def read_residual(s, t):
        return resid[pl.ds(RES_LEAD - EXT * s - t, SLOT_ROWS), :].astype(BF16)

    adj_out[0] = convolve(read_residual, adjoint_ref, SLOT_ROWS).astype(BF16)


def pieces(slots, cells, patches, taps, data):
    count = data.shape[0]
    slot = pl.BlockSpec((1, SLOT_ROWS, 2 * LANES), lambda p, slots, cells: (slots[p], 0, 0))
    taps_shape = (1, 1, REACH * LANES, TILES * LANES)
    forward = pl.BlockSpec(taps_shape, lambda p, slots, cells: (0, cells[p], 0, 0))
    adjoint = pl.BlockSpec(taps_shape, lambda p, slots, cells: (1, cells[p], 0, 0))
    block = pl.BlockSpec((1, BLK_ROWS, 2 * LANES), lambda p, slots, cells: (p, 0, 0))
    return pl.pallas_call(
        piece_kernel,
        grid_spec=pltpu.PrefetchScalarGridSpec(
            num_scalar_prefetch=2,
            grid=(count,),
            in_specs=[slot, forward, adjoint, block],
            out_specs=[slot, block],
            scratch_shapes=[
                pltpu.VMEM((SLOT_ROWS, 2 * LANES), F32),
                pltpu.VMEM((RES_LEAD + SLOT_ROWS, 2 * LANES), F32),
            ],
        ),
        out_shape=[
            jax.ShapeDtypeStruct(patches.shape, BF16),
            jax.ShapeDtypeStruct(data.shape, BF16),
        ],
        cost_estimate=SMALL,
        name="pieces",
    )(slots, cells, patches, taps, taps, data)


def ungroup_kernel(res_ref, out_ref, scratch):
    def per_piece(p, carry):
        scratch[...] = res_ref[p].astype(F32)
        for row in range(OUT):
            halves = [
                scratch[pl.ds(EXT * row, 8), half * LANES : (half + 1) * LANES] for half in range(2)
            ]
            rows = swap_groups(jnp.stack(halves, 0)).reshape(G, LANES)
            out_ref[p, row * G : (row + 1) * G, :] = rows.astype(BF16)
        return carry

    lax.fori_loop(0, res_ref.shape[0], per_piece, 0)


def ungroup(residual):
    count = residual.shape[0]
    return pl.pallas_call(
        ungroup_kernel,
        grid=(count // BATCH,),
        in_specs=[pl.BlockSpec((BATCH, BLK_ROWS, 2 * LANES), lambda p: (p, 0, 0))],
        out_specs=pl.BlockSpec((BATCH, B, B), lambda p: (p, 0, 0)),
        out_shape=jax.ShapeDtypeStruct((count, B, B), BF16),
        scratch_shapes=[pltpu.VMEM((BLK_ROWS, 2 * LANES), F32)],
        compiler_params=pltpu.CompilerParams(vmem_limit_bytes=VMEM_ALL),
        cost_estimate=SMALL,
        name="ungroup",
    )(residual)


def fold_kernel(per_row, half_rows, ids_ref, slot_ref, out_ref, canvas, scratch, packed):
    canvas[...] = jnp.zeros_like(canvas)
    inside = lax.broadcasted_iota(jnp.int32, (G, LANES), 0) < EXT

    def per_slot(n, carry):
        named = ids_ref[n]

        @pl.when(named >= 0)
        def _():
            first_row = named // per_row * (2 * OUT)
            first_col = pl.multiple_of(named % per_row * OUT, 8)
            scratch[...] = slot_ref[n].astype(F32)
            for row in range(EXT):
                for half in range(2):
                    part = scratch[pl.ds(EXT * row, G), half * LANES : (half + 1) * LANES]
                    part = jnp.where(inside, part, 0.0)
                    at = (first_row + 2 * row + half, pl.ds(first_col, G), slice(None))
                    canvas[at] = canvas[at] + part

        return carry

    lax.fori_loop(0, slot_ref.shape[0], per_slot, 0)
    for chunk in range(per_row):
        first = OUT * chunk + 1
        for row in range(half_rows):
            packed[CHUNK * row : CHUNK * row + G, :] = canvas[row, first : first + G, :]
        out_ref[chunk] = packed[...].astype(BF16)


def fold(ids, received, per_row, half_rows):
    return pl.pallas_call(
        lambda *refs: fold_kernel(per_row, half_rows, *refs),
        in_specs=[
            pl.BlockSpec(memory_space=pltpu.SMEM),
            pl.BlockSpec(memory_space=pltpu.VMEM),
        ],
        out_specs=pl.BlockSpec(memory_space=pltpu.VMEM),
        scratch_shapes=[
            pltpu.VMEM((half_rows, PITCH + 8, LANES), F32),
            pltpu.VMEM((SLOT_ROWS, 2 * LANES), F32),
            pltpu.VMEM((CHUNK_ROWS, LANES), F32),
        ],
        out_shape=jax.ShapeDtypeStruct((per_row, CHUNK_ROWS, LANES), BF16),
        cost_estimate=SMALL,
        name="fold",
    )(ids, received)


def finish_kernel(half_rows, terms_ref, up_out, middle_out, down_out, summed, canvas):
    total = terms_ref[0].astype(F32)
    for term in range(1, terms_ref.shape[0]):
        total = total + terms_ref[term].astype(F32)
    summed[...] = total
    near = lax.broadcasted_iota(jnp.int32, (8, LANES), 1) < LANES - SHIFT
    for first in range(0, half_rows, 8):
        count = min(8, half_rows - first)
        starts = [CHUNK * (first + row) for row in range(count)]
        tiles = swap_groups(jnp.stack([summed[start : start + 8, :] for start in starts], 0))
        edges = summed[pl.ds(starts[0] + 8, count, stride=CHUNK), :]
        if count < 8:
            edges = jnp.concatenate([edges, jnp.zeros((8 - count, LANES), F32)], axis=0)
        edges = swap_groups(edges.reshape(1, 8, LANES)).reshape(8, LANES)
        for row in range(count):
            tile = pltpu.roll(tiles[row], LANES - SHIFT, 1)
            edge = pltpu.roll(edges, (LANES - SHIFT - G * row) % LANES, 1)
            start = 8 * (first + row)
            canvas[start : start + 8, :] = jnp.where(near, tile, edge)
    middle = middle_out.shape[0]
    up_out[...] = canvas[:HALO, :].astype(BF16)
    middle_out[...] = canvas[HALO : HALO + middle, :]
    down_out[...] = canvas[HALO + middle : 2 * HALO + middle, :].astype(BF16)


def finish(terms, half_rows, rows):
    rim = jax.ShapeDtypeStruct((HALO, LANES), BF16)
    vmem = pl.BlockSpec(memory_space=pltpu.VMEM)
    return pl.pallas_call(
        lambda *refs: finish_kernel(half_rows, *refs),
        in_specs=[vmem],
        out_specs=[vmem, vmem, vmem],
        out_shape=[rim, jax.ShapeDtypeStruct((rows, LANES), F32), rim],
        scratch_shapes=[
            pltpu.VMEM((CHUNK_ROWS, LANES), F32),
            pltpu.VMEM((8 * half_rows, LANES), F32),
        ],
        cost_estimate=SMALL,
        name="finish",
    )(terms)


def shards(sky_model, exposure_data, pixel_mask, block_owner, block_local, psf_cell, psf_table):
    sky_count = lax.axis_size("sky")
    stripe_rows, stripe_cols = sky_model.shape
    per_row = stripe_cols // B
    block_total = stripe_rows // B * per_row
    piece_count = exposure_data.shape[0]
    owner_sky = block_owner[:, 0]
    code = lax.broadcasted_iota(jnp.int32, (piece_count,), 0) * block_total + block_local
    mine = owner_sky[None, :] == lax.broadcasted_iota(jnp.int32, (sky_count, 1), 0)
    first = jnp.min(jnp.where(mine, code[None, :], piece_count * block_total), axis=1)
    last = jnp.max(jnp.where(mine, code[None, :], -1), axis=1)
    requests = jnp.stack(
        [
            jnp.where(last < 0, -1, first % block_total),
            jnp.where(last > first, last % block_total, -1),
        ],
        axis=1,
    )
    asked = lax.all_to_all(requests, "sky", split_axis=0, concat_axis=0, tiled=True)
    asked = asked.reshape(sky_count * CAP)

    above = from_behind(sky_model[stripe_rows - LEAD :], "sky", 1)
    below = from_behind(sky_model[:HALO], "sky", -1)
    stripe = jnp.concatenate([above, sky_model, below], axis=0)
    stripe = jnp.pad(stripe, ((0, 0), (LEAD, PITCH * G - LEAD - stripe_cols)))
    blocks = stripe_blocks(stripe)
    second = jnp.any(mine & (first[:, None] < code[None, :]), axis=0)
    slot_index = owner_sky * CAP + second.astype(jnp.int32)
    asked, blocks, slot_index = lax.optimization_barrier((asked, blocks, slot_index))
    outgoing = cut_patches(asked, blocks, per_row)
    exposure_data, pixel_mask, psf_table, _ = lax.optimization_barrier(
        (exposure_data, pixel_mask, psf_table, outgoing)
    )
    patches = lax.all_to_all(outgoing, "sky", split_axis=0, concat_axis=0, tiled=True)
    taps = build_taps(psf_table)
    data = regroup(exposure_data, pixel_mask)
    adjoints, residuals = pieces(slot_index, psf_cell, patches, taps, data)
    received = lax.all_to_all(adjoints, "sky", split_axis=0, concat_axis=0, tiled=True)
    received, residual = lax.optimization_barrier((received, ungroup(residuals)))

    half_rows = (stripe_rows + LEAD + HALO) // 8
    partial = fold(asked, received, per_row, half_rows)
    terms = lax.all_to_all(partial, "exp", split_axis=0, concat_axis=0, tiled=True)
    up, middle, down = finish(terms, half_rows, stripe_rows)
    from_below = from_behind(up, "sky", -1).astype(F32)
    from_above = from_behind(down, "sky", 1).astype(F32)
    gradient = (
        middle
        + jnp.pad(from_above, ((0, stripe_rows - HALO), (0, 0)))
        + jnp.pad(from_below, ((stripe_rows - HALO, 0), (0, 0)))
    )
    return (gradient, residual)


def solution(mesh):
    in_specs = (
        P("sky", None),
        P(("sky", "exp"), None, None),
        P(("sky", "exp"), None, None),
        P(("sky", "exp"), None),
        P(("sky", "exp")),
        P(("sky", "exp")),
        P("exp", None),
    )
    out_specs = (P("sky", "exp"), P(("sky", "exp"), None, None))
    return jax.shard_map(shards, mesh=mesh, in_specs=in_specs, out_specs=out_specs, check_vma=False)
```

```python
import jax
import jax.numpy as jnp
from jax import lax
from jax.experimental import pallas as pl
from jax.experimental.pallas import tpu as pltpu
from jax.sharding import PartitionSpec as P

B = 128
PSF = 41
HALO = 20
CAP = 2

G = 16
LANES = 128
OUT = B // G
EXT = 11
REACH = 4
TAIL = 8
FWD_ROWS = 88
BLK_ROWS = 96
SLOT_ROWS = 128
PITCH = 72
TILES = 6
RES_LEAD = 40
TAP_ROWS = 48
BATCH = 4
SLOTS = 8
CHUNK = 9
CHUNK_ROWS = 352
SHIFT = 4
VMEM_ALL = 60 << 20
SMALL = pl.CostEstimate(flops=1000, bytes_accessed=1000, transcendentals=0)
F32 = jnp.float32
BF16 = jnp.bfloat16


def from_behind(x, axis, by):
    devices = lax.axis_size(axis)
    pairs = [(i, i + by) for i in range(devices) if 0 <= i + by < devices]
    return lax.ppermute(x, axis, pairs)


def swap_groups(x):
    sub = lax.broadcasted_iota(jnp.int32, x.shape, 1)
    group = lax.broadcasted_iota(jnp.int32, x.shape, 2) // G
    for d in (4, 2, 1):
        sub_bit, group_bit = (sub & d) != 0, (group & d) != 0
        up = pltpu.roll(pltpu.roll(x, 8 - d, 1), G * d, 2)
        down = up if d == 4 else pltpu.roll(pltpu.roll(x, d, 1), LANES - G * d, 2)
        x = jnp.where(sub_bit == group_bit, x, jnp.where(group_bit, up, down))
    return x


def regroup_kernel(data_ref, keep_ref, out_ref, scratch):
    def per_piece(p, carry):
        known = jnp.where(keep_ref[p] != 0, data_ref[p].astype(F32), jnp.inf)
        blocks = swap_groups(known.reshape(2 * OUT, 8, LANES))
        scratch[...] = jnp.full_like(scratch, jnp.inf)
        for row in range(2 * OUT):
            half = row % 2
            scratch[pl.ds(EXT * (row // 2), 8), half * LANES : (half + 1) * LANES] = blocks[row]
        out_ref[p] = scratch[...].astype(BF16)
        return carry

    lax.fori_loop(0, data_ref.shape[0], per_piece, 0)


def regroup(exposure_data, pixel_mask):
    pieces = exposure_data.shape[0]
    block = pl.BlockSpec((BATCH, B, B), lambda p: (p, 0, 0))
    return pl.pallas_call(
        regroup_kernel,
        grid=(pieces // BATCH,),
        in_specs=[block, block],
        out_specs=pl.BlockSpec((BATCH, BLK_ROWS, 2 * LANES), lambda p: (p, 0, 0)),
        out_shape=jax.ShapeDtypeStruct((pieces, BLK_ROWS, 2 * LANES), BF16),
        scratch_shapes=[pltpu.VMEM((BLK_ROWS, 2 * LANES), F32)],
        cost_estimate=SMALL,
        name="regroup",
    )(exposure_data, pixel_mask)


def taps_kernel(kernel_ref, out_ref, windows, rows):
    lane = lax.broadcasted_iota(jnp.int32, (G, LANES), 1)
    odd = (lane // G) % 2 == 1
    wide = lax.broadcasted_iota(jnp.int32, (TAP_ROWS, LANES), 1) // (2 * G)
    quarter = lax.broadcasted_iota(jnp.int32, (TILES, LANES), 1) // (2 * G)

    kernel = kernel_ref[0].astype(F32)
    spread = pltpu.roll(kernel, G, 1)
    for t in range(1, REACH):
        spread = jnp.where(wide == t, pltpu.roll(kernel, G * t + G, 1), spread)
    windows[...] = spread
    for parity in range(2):
        picked = [windows[pl.ds(parity + 2 * q, TILES, stride=8), :] for q in range(4)]
        for t in range(REACH):
            row = picked[0] if t == 0 else pltpu.roll(picked[0], 2 * G * (4 - t), 1)
            for q in range(1, 4):
                by = (q - t) % 4
                part = picked[q] if by == 0 else pltpu.roll(picked[q], 2 * G * by, 1)
                row = jnp.where(quarter == q, part, row)
            rows[t, parity, :TILES, :] = row

    def per_shift(t, carry):
        before = [jnp.zeros((G, LANES), F32)] * 8
        for tile in range(TILES):
            even_row, odd_row = (
                jnp.broadcast_to(rows[t, parity, tile : tile + 1, :], (G, LANES))
                for parity in range(2)
            )
            even_row = pltpu.roll(even_row, LANES - G, 1, stride=1, stride_axis=0)
            odd_row = pltpu.roll(odd_row, 0, 1, stride=1, stride_axis=0)
            now = jnp.where(odd, odd_row, even_row)
            turns = [now] + [pltpu.roll(now, G * phase, 1) for phase in range(1, 8)]
            for phase in range(8):
                part = turns[phase]
                if phase > 0:
                    part = jnp.where(lane < G * phase, before[phase], part)
                start = pl.multiple_of(t * LANES + phase * G, G)
                lanes = slice(tile * LANES, (tile + 1) * LANES)
                out_ref[0, pl.ds(start, G), lanes] = part.astype(BF16)
            before = turns
        return carry

    lax.fori_loop(0, REACH, per_shift, 0)


def build_taps(table):
    cells = table.shape[0]
    kernels = jnp.pad(
        table.reshape(cells, PSF, PSF), ((0, 0), (0, TAP_ROWS - PSF), (0, LANES - PSF))
    )
    return pl.pallas_call(
        taps_kernel,
        grid=(cells,),
        in_specs=[pl.BlockSpec((1, TAP_ROWS, LANES), lambda c: (c, 0, 0))],
        out_specs=pl.BlockSpec((1, REACH * LANES, TILES * LANES), lambda c: (c, 0, 0)),
        out_shape=jax.ShapeDtypeStruct((cells, REACH * LANES, TILES * LANES), BF16),
        scratch_shapes=[
            pltpu.VMEM((TAP_ROWS, LANES), F32),
            pltpu.VMEM((REACH, 2, 8, LANES), F32),
        ],
        compiler_params=pltpu.CompilerParams(vmem_limit_bytes=VMEM_ALL),
        cost_estimate=SMALL,
        name="taps",
    )(kernels)


def blocks_kernel(stripe_ref, out_ref):
    def per_row(r, carry):
        start = pl.multiple_of(r * G, G)
        for tile in range(PITCH // 8):
            part = stripe_ref[pl.ds(start, G), tile * LANES : (tile + 1) * LANES].astype(F32)
            out_ref[pl.ds(2 * r, 2), tile * 8 : (tile + 1) * 8, :] = swap_groups(
                part.reshape(2, 8, LANES)
            )
        return carry

    lax.fori_loop(0, stripe_ref.shape[0] // G, per_row, 0)


def stripe_blocks(stripe):
    rows = stripe.shape[0] // 8
    return pl.pallas_call(
        blocks_kernel,
        out_shape=jax.ShapeDtypeStruct((rows, PITCH, LANES), F32),
        in_specs=[pl.BlockSpec(memory_space=pltpu.VMEM)],
        out_specs=pl.BlockSpec(memory_space=pltpu.VMEM),
        cost_estimate=SMALL,
        name="blocks",
    )(stripe)


def cut_kernel(per_row, ids_ref, blocks_ref, out_ref, scratch):
    step = pl.program_id(0)

    def per_slot(n, carry):
        wanted = ids_ref[step * SLOTS + n]

        @pl.when(wanted >= 0)
        def _():
            first_row = wanted // per_row * (2 * OUT)
            first_col = pl.multiple_of(wanted % per_row * OUT, 8)
            for row in range(EXT):
                for half in range(2):
                    part = blocks_ref[first_row + 2 * row + half, pl.ds(first_col, G), :]
                    scratch[pl.ds(EXT * row, G), half * LANES : (half + 1) * LANES] = part
            out_ref[n] = scratch[...].astype(BF16)

        return carry

    lax.fori_loop(0, SLOTS, per_slot, 0)


def cut_patches(ids, blocks, per_row):
    slots = ids.shape[0]
    return pl.pallas_call(
        lambda *refs: cut_kernel(per_row, *refs),
        grid_spec=pltpu.PrefetchScalarGridSpec(
            num_scalar_prefetch=1,
            grid=(slots // SLOTS,),
            in_specs=[pl.BlockSpec(blocks.shape, lambda n, ids: (0, 0, 0))],
            out_specs=pl.BlockSpec((SLOTS, SLOT_ROWS, 2 * LANES), lambda n, ids: (n, 0, 0)),
            scratch_shapes=[pltpu.VMEM((SLOT_ROWS, 2 * LANES), F32)],
        ),
        out_shape=jax.ShapeDtypeStruct((slots, SLOT_ROWS, 2 * LANES), BF16),
        cost_estimate=SMALL,
        name="cut",
    )(ids, blocks)


def block_taps(taps_ref, s, t):
    taps = slice(t * LANES, (t + 1) * LANES)
    upper = taps_ref[0, taps, 2 * s * LANES : (2 * s + 2) * LANES]
    if s == 0:
        lower = jnp.concatenate(
            [jnp.zeros((LANES, LANES), BF16), taps_ref[0, taps, 0:LANES]], axis=1
        )
    else:
        lower = taps_ref[0, taps, (2 * s - 1) * LANES : (2 * s + 1) * LANES]
    return jnp.concatenate([upper, lower], axis=0)


def last_taps(taps_ref, t):
    return taps_ref[0, t * LANES : (t + 1) * LANES, (TILES - 1) * LANES :]


def correlate(read, taps_ref, rows):
    across = (((1,), (1,)), ((), ()))
    total = jnp.zeros((rows, 2 * LANES), F32)
    for t in range(REACH):
        for s in range(REACH - 1):
            total = total + lax.dot_general(
                read(s, t), block_taps(taps_ref, s, t), across, preferred_element_type=F32
            )
    last = jnp.zeros((rows, LANES), F32)
    for t in range(0, REACH, 2):
        field = [read(REACH - 1, t + i)[:, :LANES] for i in range(2)]
        taps = [last_taps(taps_ref, t + i) for i in range(2)]
        last = last + lax.dot_general(
            jnp.concatenate(field, axis=1),
            jnp.concatenate(taps, axis=1),
            across,
            preferred_element_type=F32,
        )
    return jnp.concatenate([total[:, :LANES], total[:, LANES:] + last], axis=1)


def convolve(read, taps_ref, rows):
    total = jnp.zeros((rows, 2 * LANES), F32)
    for t in range(REACH):
        for s in range(REACH - 1):
            total = total + jnp.dot(
                read(s, t), block_taps(taps_ref, s, t), preferred_element_type=F32
            )
    last = jnp.zeros((rows, LANES), F32)
    for t in range(0, REACH, 2):
        field = [read(REACH - 1, t + i)[:, LANES:] for i in range(2)]
        taps = [last_taps(taps_ref, t + i) for i in range(2)]
        last = last + jnp.dot(
            jnp.concatenate(field, axis=1),
            jnp.concatenate(taps, axis=0),
            preferred_element_type=F32,
        )
    return jnp.concatenate([total[:, :LANES] + last, total[:, LANES:]], axis=1)


def piece_kernel(
    slot_ref, cell_ref, patch_ref, taps_ref, data_ref, adj_out, res_out, field, resid
):
    @pl.when(pl.program_id(0) == 0)
    def _():
        resid[...] = jnp.zeros_like(resid)

    field[...] = patch_ref[0].astype(F32)

    def read_patch(s, t):
        return field[pl.ds(EXT * s + t, FWD_ROWS), :].astype(BF16)

    predicted = correlate(read_patch, taps_ref, FWD_ROWS)
    observed = data_ref[0, :FWD_ROWS].astype(F32)
    residual = jnp.where(observed < jnp.inf, predicted - observed, 0.0).astype(BF16)
    res_out[0, :FWD_ROWS] = residual
    resid[RES_LEAD : RES_LEAD + FWD_ROWS, :] = residual.astype(F32)

    def read_residual(s, t):
        return resid[pl.ds(RES_LEAD - EXT * s - t, SLOT_ROWS), :].astype(BF16)

    adj_out[0] = convolve(read_residual, taps_ref, SLOT_ROWS).astype(BF16)


def pieces(slots, cells, patches, taps, data):
    count = data.shape[0]
    slot = pl.BlockSpec((1, SLOT_ROWS, 2 * LANES), lambda p, slots, cells: (slots[p], 0, 0))
    cell = pl.BlockSpec(
        (1, REACH * LANES, TILES * LANES), lambda p, slots, cells: (cells[p], 0, 0)
    )
    block = pl.BlockSpec((1, BLK_ROWS, 2 * LANES), lambda p, slots, cells: (p, 0, 0))
    return pl.pallas_call(
        piece_kernel,
        grid_spec=pltpu.PrefetchScalarGridSpec(
            num_scalar_prefetch=2,
            grid=(count,),
            in_specs=[slot, cell, block],
            out_specs=[slot, block],
            scratch_shapes=[
                pltpu.VMEM((SLOT_ROWS, 2 * LANES), F32),
                pltpu.VMEM((RES_LEAD + SLOT_ROWS, 2 * LANES), F32),
            ],
        ),
        out_shape=[
            jax.ShapeDtypeStruct(patches.shape, BF16),
            jax.ShapeDtypeStruct(data.shape, BF16),
        ],
        cost_estimate=SMALL,
        name="pieces",
    )(slots, cells, patches, taps, data)


def ungroup_kernel(res_ref, out_ref, scratch):
    def per_piece(p, carry):
        scratch[...] = res_ref[p].astype(F32)
        for row in range(OUT):
            halves = [
                scratch[pl.ds(EXT * row, 8), half * LANES : (half + 1) * LANES] for half in range(2)
            ]
            rows = swap_groups(jnp.stack(halves, 0)).reshape(G, LANES)
            out_ref[p, row * G : (row + 1) * G, :] = rows.astype(BF16)
        return carry

    lax.fori_loop(0, res_ref.shape[0], per_piece, 0)


def ungroup(residual):
    count = residual.shape[0]
    return pl.pallas_call(
        ungroup_kernel,
        grid=(count // BATCH,),
        in_specs=[pl.BlockSpec((BATCH, BLK_ROWS, 2 * LANES), lambda p: (p, 0, 0))],
        out_specs=pl.BlockSpec((BATCH, B, B), lambda p: (p, 0, 0)),
        out_shape=jax.ShapeDtypeStruct((count, B, B), BF16),
        scratch_shapes=[pltpu.VMEM((BLK_ROWS, 2 * LANES), F32)],
        compiler_params=pltpu.CompilerParams(vmem_limit_bytes=VMEM_ALL),
        cost_estimate=SMALL,
        name="ungroup",
    )(residual)


def fold_kernel(per_row, half_rows, ids_ref, slot_ref, out_ref, canvas, scratch, packed):
    canvas[...] = jnp.zeros_like(canvas)
    inside = lax.broadcasted_iota(jnp.int32, (G, LANES), 0) < EXT

    def per_slot(n, carry):
        named = ids_ref[n]

        @pl.when(named >= 0)
        def _():
            first_row = named // per_row * (2 * OUT)
            first_col = pl.multiple_of(named % per_row * OUT, 8)
            scratch[...] = slot_ref[n].astype(F32)
            for row in range(EXT):
                for half in range(2):
                    part = scratch[pl.ds(EXT * row, G), half * LANES : (half + 1) * LANES]
                    part = jnp.where(inside, part, 0.0)
                    at = (first_row + 2 * row + half, pl.ds(first_col, G), slice(None))
                    canvas[at] = canvas[at] + part

        return carry

    lax.fori_loop(0, slot_ref.shape[0], per_slot, 0)
    for chunk in range(per_row):
        first = OUT * chunk + 1
        for row in range(half_rows):
            packed[CHUNK * row : CHUNK * row + G, :] = canvas[row, first : first + G, :]
        out_ref[chunk] = packed[...].astype(BF16)


def fold(ids, received, per_row, half_rows):
    return pl.pallas_call(
        lambda *refs: fold_kernel(per_row, half_rows, *refs),
        in_specs=[
            pl.BlockSpec(memory_space=pltpu.SMEM),
            pl.BlockSpec(memory_space=pltpu.VMEM),
        ],
        out_specs=pl.BlockSpec(memory_space=pltpu.VMEM),
        scratch_shapes=[
            pltpu.VMEM((half_rows, PITCH + 8, LANES), F32),
            pltpu.VMEM((SLOT_ROWS, 2 * LANES), F32),
            pltpu.VMEM((CHUNK_ROWS, LANES), F32),
        ],
        out_shape=jax.ShapeDtypeStruct((per_row, CHUNK_ROWS, LANES), BF16),
        cost_estimate=SMALL,
        name="fold",
    )(ids, received)


def finish_kernel(half_rows, terms_ref, up_out, middle_out, down_out, summed, canvas):
    total = terms_ref[0].astype(F32)
    for term in range(1, terms_ref.shape[0]):
        total = total + terms_ref[term].astype(F32)
    summed[...] = total
    near = lax.broadcasted_iota(jnp.int32, (8, LANES), 1) < LANES - SHIFT
    for first in range(0, half_rows, 8):
        count = min(8, half_rows - first)
        starts = [CHUNK * (first + row) for row in range(count)]
        tiles = swap_groups(jnp.stack([summed[start : start + 8, :] for start in starts], 0))
        edges = summed[pl.ds(starts[0] + 8, count, stride=CHUNK), :]
        if count < 8:
            edges = jnp.concatenate([edges, jnp.zeros((8 - count, LANES), F32)], axis=0)
        edges = swap_groups(edges.reshape(1, 8, LANES)).reshape(8, LANES)
        for row in range(count):
            tile = pltpu.roll(tiles[row], LANES - SHIFT, 1)
            edge = pltpu.roll(edges, (LANES - SHIFT - G * row) % LANES, 1)
            start = 8 * (first + row)
            canvas[start : start + 8, :] = jnp.where(near, tile, edge)
    middle = middle_out.shape[0]
    up_out[...] = canvas[:HALO, :].astype(BF16)
    middle_out[...] = canvas[HALO : HALO + middle, :]
    down_out[...] = canvas[HALO + middle : 2 * HALO + middle, :].astype(BF16)


def finish(terms, half_rows, rows):
    rim = jax.ShapeDtypeStruct((HALO, LANES), BF16)
    vmem = pl.BlockSpec(memory_space=pltpu.VMEM)
    return pl.pallas_call(
        lambda *refs: finish_kernel(half_rows, *refs),
        in_specs=[vmem],
        out_specs=[vmem, vmem, vmem],
        out_shape=[rim, jax.ShapeDtypeStruct((rows, LANES), F32), rim],
        scratch_shapes=[
            pltpu.VMEM((CHUNK_ROWS, LANES), F32),
            pltpu.VMEM((8 * half_rows, LANES), F32),
        ],
        cost_estimate=SMALL,
        name="finish",
    )(terms)


def shards(sky_model, exposure_data, pixel_mask, block_owner, block_local, psf_cell, psf_table):
    sky_count = lax.axis_size("sky")
    stripe_rows, stripe_cols = sky_model.shape
    per_row = stripe_cols // B
    block_total = stripe_rows // B * per_row
    piece_count = exposure_data.shape[0]
    owner_sky = block_owner[:, 0]
    code = lax.broadcasted_iota(jnp.int32, (piece_count,), 0) * block_total + block_local
    mine = owner_sky[None, :] == lax.broadcasted_iota(jnp.int32, (sky_count, 1), 0)
    first = jnp.min(jnp.where(mine, code[None, :], piece_count * block_total), axis=1)
    last = jnp.max(jnp.where(mine, code[None, :], -1), axis=1)
    requests = jnp.stack(
        [
            jnp.where(last < 0, -1, first % block_total),
            jnp.where(last > first, last % block_total, -1),
        ],
        axis=1,
    )
    asked = lax.all_to_all(requests, "sky", split_axis=0, concat_axis=0, tiled=True)
    asked = asked.reshape(sky_count * CAP)

    above = from_behind(sky_model[stripe_rows - HALO :], "sky", 1)
    below = from_behind(sky_model[:HALO], "sky", -1)
    stripe = jnp.concatenate([above, sky_model, below], axis=0)
    stripe = jnp.pad(stripe, ((0, TAIL), (HALO, PITCH * G - HALO - stripe_cols)))
    blocks = stripe_blocks(stripe)
    second = jnp.any(mine & (first[:, None] < code[None, :]), axis=0)
    slot_index = owner_sky * CAP + second.astype(jnp.int32)
    asked, blocks, slot_index = lax.optimization_barrier((asked, blocks, slot_index))
    outgoing = cut_patches(asked, blocks, per_row)
    exposure_data, pixel_mask, psf_table, _ = lax.optimization_barrier(
        (exposure_data, pixel_mask, psf_table, outgoing)
    )
    patches = lax.all_to_all(outgoing, "sky", split_axis=0, concat_axis=0, tiled=True)
    taps = build_taps(psf_table)
    data = regroup(exposure_data, pixel_mask)
    adjoints, residuals = pieces(slot_index, psf_cell, patches, taps, data)
    received = lax.all_to_all(adjoints, "sky", split_axis=0, concat_axis=0, tiled=True)
    received, residual = lax.optimization_barrier((received, ungroup(residuals)))

    half_rows = (stripe_rows + 2 * HALO + TAIL) // 8
    partial = fold(asked, received, per_row, half_rows)
    terms = lax.all_to_all(partial, "exp", split_axis=0, concat_axis=0, tiled=True)
    up, middle, down = finish(terms, half_rows, stripe_rows)
    from_below = from_behind(up, "sky", -1).astype(F32)
    from_above = from_behind(down, "sky", 1).astype(F32)
    gradient = (
        middle
        + jnp.pad(from_above, ((0, stripe_rows - HALO), (0, 0)))
        + jnp.pad(from_below, ((stripe_rows - HALO, 0), (0, 0)))
    )
    return (gradient, residual)


def solution(mesh):
    in_specs = (
        P("sky", None),
        P(("sky", "exp"), None, None),
        P(("sky", "exp"), None, None),
        P(("sky", "exp"), None),
        P(("sky", "exp")),
        P(("sky", "exp")),
        P("exp", None),
    )
    out_specs = (P("sky", "exp"), P(("sky", "exp"), None, None))
    return jax.shard_map(shards, mesh=mesh, in_specs=in_specs, out_specs=out_specs, check_vma=False)
```

```python
import jax
import jax.numpy as jnp
from jax import lax
from jax.experimental import pallas as pl
from jax.experimental.pallas import tpu as pltpu
from jax.sharding import PartitionSpec as P

B = 128
PSF = 41
HALO = 20
CAP = 2

G = 16
LANES = 128
OUT = B // G
EXT = 11
REACH = 4
TAIL = 8
BLOCKS = OUT * OUT
SLOT_ROWS = 128
PITCH = 72
TILES = 6
RES_LEAD = 40
TAP_ROWS = 48
OWN_FIRST = 3
BATCH = 4
SLOTS = 8
CHUNK = 9
CHUNK_ROWS = 352
SHIFT = 4
SMALL = pl.CostEstimate(flops=1000, bytes_accessed=1000, transcendentals=0)
F32 = jnp.float32
BF16 = jnp.bfloat16


def whole_vmem():
    return pl.BlockSpec(memory_space=pltpu.VMEM)


def on_chip(x):
    return pltpu.with_memory_space_constraint(x, pltpu.VMEM)


def from_behind(x, axis, by):
    devices = lax.axis_size(axis)
    pairs = [(i, i + by) for i in range(devices) if 0 <= i + by < devices]
    return lax.ppermute(x, axis, pairs)


def swap_groups(x):
    sub = lax.broadcasted_iota(jnp.int32, x.shape, 1)
    group = lax.broadcasted_iota(jnp.int32, x.shape, 2) // G
    for d in (4, 2, 1):
        sub_bit, group_bit = (sub & d) != 0, (group & d) != 0
        up = pltpu.roll(pltpu.roll(x, 8 - d, 1), G * d, 2)
        down = up if d == 4 else pltpu.roll(pltpu.roll(x, d, 1), LANES - G * d, 2)
        x = jnp.where(sub_bit == group_bit, x, jnp.where(group_bit, up, down))
    return x


def regroup_kernel(data_ref, keep_ref, out_ref):
    def per_piece(p, carry):
        known = jnp.where(keep_ref[p] != 0, data_ref[p].astype(F32), jnp.inf)
        blocks = swap_groups(known.reshape(2 * OUT, 8, LANES)).reshape(OUT, 2, 8, LANES)
        for half in range(2):
            out_ref[p, :, half * LANES : (half + 1) * LANES] = (
                blocks[:, half].reshape(BLOCKS, LANES).astype(BF16)
            )
        return carry

    lax.fori_loop(0, data_ref.shape[0], per_piece, 0)


def regroup(exposure_data, pixel_mask):
    pieces = exposure_data.shape[0]
    block = pl.BlockSpec((BATCH, B, B), lambda p: (p, 0, 0))
    return pl.pallas_call(
        regroup_kernel,
        grid=(pieces // BATCH,),
        in_specs=[block, block],
        out_specs=pl.BlockSpec((BATCH, BLOCKS, 2 * LANES), lambda p: (p, 0, 0)),
        out_shape=jax.ShapeDtypeStruct((pieces, BLOCKS, 2 * LANES), BF16),
        cost_estimate=SMALL,
        name="regroup",
    )(exposure_data, pixel_mask)


def taps_kernel(kernel_ref, out_ref, windows, rows):
    lane = lax.broadcasted_iota(jnp.int32, (G, LANES), 1)
    odd = (lane // G) % 2 == 1
    wide = lax.broadcasted_iota(jnp.int32, (TAP_ROWS, LANES), 1) // (2 * G)
    quarter = lax.broadcasted_iota(jnp.int32, (TILES, LANES), 1) // (2 * G)

    kernel = kernel_ref[0].astype(F32)
    spread = pltpu.roll(kernel, G, 1)
    for t in range(1, REACH):
        spread = jnp.where(wide == t, pltpu.roll(kernel, G * t + G, 1), spread)
    windows[...] = spread
    for parity in range(2):
        picked = [windows[pl.ds(parity + 2 * q, TILES, stride=8), :] for q in range(4)]
        for t in range(REACH):
            row = picked[0] if t == 0 else pltpu.roll(picked[0], 2 * G * (4 - t), 1)
            for q in range(1, 4):
                by = (q - t) % 4
                part = picked[q] if by == 0 else pltpu.roll(picked[q], 2 * G * by, 1)
                row = jnp.where(quarter == q, part, row)
            rows[t, parity, :TILES, :] = row

    def per_shift(t, carry):
        before = [jnp.zeros((G, LANES), F32)] * 8
        for tile in range(TILES):
            even_row, odd_row = (
                jnp.broadcast_to(rows[t, parity, tile : tile + 1, :], (G, LANES))
                for parity in range(2)
            )
            even_row = pltpu.roll(even_row, LANES - G, 1, stride=1, stride_axis=0)
            odd_row = pltpu.roll(odd_row, 0, 1, stride=1, stride_axis=0)
            now = jnp.where(odd, odd_row, even_row)
            turns = [now] + [pltpu.roll(now, G * phase, 1) for phase in range(1, 8)]
            for phase in range(8):
                part = turns[phase]
                if phase > 0:
                    part = jnp.where(lane < G * phase, before[phase], part)
                start = pl.multiple_of(t * LANES + phase * G, G)
                lanes = slice(tile * LANES, (tile + 1) * LANES)
                out_ref[0, pl.ds(start, G), lanes] = part.astype(BF16)
            before = turns
        return carry

    lax.fori_loop(0, REACH, per_shift, 0)


def build_taps(table):
    cells = table.shape[0]
    kernels = jnp.pad(
        table.reshape(cells, PSF, PSF), ((0, 0), (0, TAP_ROWS - PSF), (0, LANES - PSF))
    )
    return pl.pallas_call(
        taps_kernel,
        grid=(cells,),
        in_specs=[pl.BlockSpec((1, TAP_ROWS, LANES), lambda c: (c, 0, 0))],
        out_specs=pl.BlockSpec((1, REACH * LANES, TILES * LANES), lambda c: (c, 0, 0)),
        out_shape=jax.ShapeDtypeStruct((cells, REACH * LANES, TILES * LANES), BF16),
        scratch_shapes=[
            pltpu.VMEM((TAP_ROWS, LANES), F32),
            pltpu.VMEM((REACH, 2, 8, LANES), F32),
        ],
        cost_estimate=SMALL,
        name="taps",
    )(kernels)


def row_blocks(pixels):
    far = lax.broadcasted_iota(jnp.int32, (8, LANES), 1) >= HALO
    tiles = pixels.shape[1] // LANES
    empty = jnp.zeros((8, LANES), F32)
    turned = [
        pltpu.roll(pixels[:, tile * LANES : (tile + 1) * LANES], HALO, 1) for tile in range(tiles)
    ]
    before, after = [empty] + turned, turned + [empty]
    moved = [jnp.where(far, now, old) for old, now in zip(before, after)]
    return swap_groups(jnp.stack(moved, 0)).reshape((tiles + 1) * 8, LANES)


def own_kernel(stripe_ref, out_ref, pixels):
    skip = 8 * OWN_FIRST - HALO
    pixels[...] = stripe_ref[...].astype(F32)

    for row in range(out_ref.shape[0]):
        out_ref[row] = row_blocks(pixels[skip + 8 * row : skip + 8 * row + 8, :])


def own_blocks(stripe):
    rows, columns = stripe.shape
    count = (rows + HALO) // 8 - OWN_FIRST
    return pl.pallas_call(
        own_kernel,
        in_specs=[pl.BlockSpec(memory_space=pltpu.VMEM)],
        out_specs=pl.BlockSpec(memory_space=pltpu.VMEM),
        out_shape=pltpu.VMEM((count, PITCH, LANES), F32),
        scratch_shapes=[pltpu.VMEM((rows, columns), F32)],
        cost_estimate=SMALL,
        name="own",
    )(stripe)


def cut_kernel(
    per_row, ids_ref, own_ref, above_ref, top_ref, bottom_ref, below_ref, out_ref, blocks, upper, lower, scratch
):
    step = pl.program_id(0)

    @pl.when(step == 0)
    def _():
        own = own_ref.shape[0]
        blocks[OWN_FIRST : OWN_FIRST + own] = own_ref[...]
        missing = 8 * OWN_FIRST - HALO
        upper[:HALO, :] = above_ref[...].astype(F32)
        upper[HALO:, :] = top_ref[...].astype(F32)[:missing]
        for row in range(OWN_FIRST):
            blocks[row] = row_blocks(upper[8 * row : 8 * row + 8, :])
        lower[...] = jnp.zeros_like(lower)
        lower[:missing, :] = bottom_ref[...].astype(F32)[G - missing :]
        lower[missing : missing + HALO, :] = below_ref[...].astype(F32)
        for row in range(lower.shape[0] // 8):
            blocks[OWN_FIRST + own + row] = row_blocks(lower[8 * row : 8 * row + 8, :])

    def per_slot(n, carry):
        wanted = ids_ref[step * SLOTS + n]

        @pl.when(wanted >= 0)
        def _():
            first_row = wanted // per_row * (2 * OUT)
            first_col = pl.multiple_of(wanted % per_row * OUT, 8)
            for row in range(EXT):
                for half in range(2):
                    part = blocks[first_row + 2 * row + half, pl.ds(first_col, G), :]
                    scratch[pl.ds(EXT * row, G), half * LANES : (half + 1) * LANES] = part
            out_ref[n] = scratch[...].astype(BF16)

        return carry

    lax.fori_loop(0, SLOTS, per_slot, 0)


def cut_patches(ids, own, stripe, above, below, half_rows):
    slots = ids.shape[0]
    rows, columns = stripe.shape
    last = rows // G - 1
    return pl.pallas_call(
        lambda *refs: cut_kernel(columns // B, *refs),
        grid_spec=pltpu.PrefetchScalarGridSpec(
            num_scalar_prefetch=1,
            grid=(slots // SLOTS,),
            in_specs=[
                whole_vmem(),
                whole_vmem(),
                pl.BlockSpec((G, columns), lambda n, ids: (0, 0)),
                pl.BlockSpec((G, columns), lambda n, ids: (last, 0)),
                whole_vmem(),
            ],
            out_specs=pl.BlockSpec((SLOTS, SLOT_ROWS, 2 * LANES), lambda n, ids: (n, 0, 0)),
            scratch_shapes=[
                pltpu.VMEM((half_rows, PITCH, LANES), F32),
                pltpu.VMEM((8 * OWN_FIRST, columns), F32),
                pltpu.VMEM((8 * (half_rows - OWN_FIRST - own.shape[0]), columns), F32),
                pltpu.VMEM((SLOT_ROWS, 2 * LANES), F32),
            ],
        ),
        out_shape=jax.ShapeDtypeStruct((slots, SLOT_ROWS, 2 * LANES), BF16),
        cost_estimate=SMALL,
        name="cut",
    )(ids, on_chip(own), on_chip(above), stripe, stripe, on_chip(below))


def block_taps(taps_ref, s, t):
    taps = slice(t * LANES, (t + 1) * LANES)
    upper = taps_ref[0, taps, 2 * s * LANES : (2 * s + 2) * LANES]
    if s == 0:
        lower = jnp.concatenate(
            [jnp.zeros((LANES, LANES), BF16), taps_ref[0, taps, 0:LANES]], axis=1
        )
    else:
        lower = taps_ref[0, taps, (2 * s - 1) * LANES : (2 * s + 1) * LANES]
    return jnp.concatenate([upper, lower], axis=0)


def last_taps(taps_ref, t):
    return taps_ref[0, t * LANES : (t + 1) * LANES, (TILES - 1) * LANES :]


def correlate(read, taps_ref, rows):
    across = (((1,), (1,)), ((), ()))
    total = jnp.zeros((rows, 2 * LANES), F32)
    for t in range(REACH):
        for s in range(REACH - 1):
            total = total + lax.dot_general(
                read(s, t), block_taps(taps_ref, s, t), across, preferred_element_type=F32
            )
    last = jnp.zeros((rows, LANES), F32)
    for t in range(0, REACH, 2):
        field = [read(REACH - 1, t + i)[:, :LANES] for i in range(2)]
        taps = [last_taps(taps_ref, t + i) for i in range(2)]
        last = last + lax.dot_general(
            jnp.concatenate(field, axis=1),
            jnp.concatenate(taps, axis=1),
            across,
            preferred_element_type=F32,
        )
    return jnp.concatenate([total[:, :LANES], total[:, LANES:] + last], axis=1)


def convolve(read, taps_ref, rows):
    total = jnp.zeros((rows, 2 * LANES), F32)
    for t in range(REACH):
        for s in range(REACH - 1):
            total = total + jnp.dot(
                read(s, t), block_taps(taps_ref, s, t), preferred_element_type=F32
            )
    last = jnp.zeros((rows, LANES), F32)
    for t in range(0, REACH, 2):
        field = [read(REACH - 1, t + i)[:, LANES:] for i in range(2)]
        taps = [last_taps(taps_ref, t + i) for i in range(2)]
        last = last + jnp.dot(
            jnp.concatenate(field, axis=1),
            jnp.concatenate(taps, axis=0),
            preferred_element_type=F32,
        )
    return jnp.concatenate([total[:, :LANES] + last, total[:, LANES:]], axis=1)


def piece_kernel(slot_ref, cell_ref, patch_ref, taps_ref, data_ref, adj_out, res_out, field, resid):
    piece = pl.program_id(0)

    @pl.when(piece == 0)
    def _():
        resid[...] = jnp.zeros_like(resid)

    field[...] = patch_ref[slot_ref[piece]].astype(F32)

    def read_patch(s, t):
        starts = [EXT * (row + s) + t for row in range(OUT)]
        return jnp.concatenate([field[at : at + OUT, :] for at in starts], axis=0).astype(BF16)

    predicted = correlate(read_patch, taps_ref, BLOCKS)
    observed = data_ref[0].astype(F32)
    residual = jnp.where(observed < jnp.inf, predicted - observed, 0.0).astype(BF16)
    res_out[0] = residual
    wide = residual.astype(F32)
    for row in range(OUT):
        first = RES_LEAD + EXT * row
        resid[first : first + OUT, :] = wide[OUT * row : OUT * (row + 1)]

    def read_residual(s, t):
        return resid[pl.ds(RES_LEAD - EXT * s - t, SLOT_ROWS), :].astype(BF16)

    adj_out[0] = convolve(read_residual, taps_ref, SLOT_ROWS).astype(BF16)


def pieces(slots, cells, patches, taps, data):
    count = data.shape[0]
    slot = pl.BlockSpec((1, SLOT_ROWS, 2 * LANES), lambda p, slots, cells: (slots[p], 0, 0))
    cell = pl.BlockSpec(
        (1, REACH * LANES, TILES * LANES), lambda p, slots, cells: (cells[p], 0, 0)
    )
    block = pl.BlockSpec((1, BLOCKS, 2 * LANES), lambda p, slots, cells: (p, 0, 0))
    return pl.pallas_call(
        piece_kernel,
        grid_spec=pltpu.PrefetchScalarGridSpec(
            num_scalar_prefetch=2,
            grid=(count,),
            in_specs=[whole_vmem(), cell, block],
            out_specs=[slot, block],
            scratch_shapes=[
                pltpu.VMEM((SLOT_ROWS, 2 * LANES), F32),
                pltpu.VMEM((RES_LEAD + SLOT_ROWS, 2 * LANES), F32),
            ],
        ),
        out_shape=[
            jax.ShapeDtypeStruct(patches.shape, BF16),
            jax.ShapeDtypeStruct(data.shape, BF16),
        ],
        cost_estimate=SMALL,
        name="pieces",
    )(slots, cells, on_chip(patches), taps, data)


def ungroup_kernel(res_ref, out_ref):
    def per_piece(p, carry):
        halves = [
            res_ref[p, :, half * LANES : (half + 1) * LANES].astype(F32).reshape(OUT, 8, LANES)
            for half in range(2)
        ]
        pixels = swap_groups(jnp.stack(halves, 1).reshape(2 * OUT, 8, LANES))
        out_ref[p] = pixels.reshape(B, LANES).astype(BF16)
        return carry

    lax.fori_loop(0, res_ref.shape[0], per_piece, 0)


def ungroup(residual):
    count = residual.shape[0]
    return pl.pallas_call(
        ungroup_kernel,
        grid=(count // BATCH,),
        in_specs=[pl.BlockSpec((BATCH, BLOCKS, 2 * LANES), lambda p: (p, 0, 0))],
        out_specs=pl.BlockSpec((BATCH, B, B), lambda p: (p, 0, 0)),
        out_shape=jax.ShapeDtypeStruct((count, B, B), BF16),
        cost_estimate=SMALL,
        name="ungroup",
    )(residual)


def fold_kernel(per_row, half_rows, ids_ref, slot_ref, out_ref, canvas, scratch, packed):
    canvas[...] = jnp.zeros_like(canvas)
    inside = lax.broadcasted_iota(jnp.int32, (G, LANES), 0) < EXT

    def per_slot(n, carry):
        named = ids_ref[n]

        @pl.when(named >= 0)
        def _():
            first_row = named // per_row * (2 * OUT)
            first_col = pl.multiple_of(named % per_row * OUT, 8)
            scratch[...] = slot_ref[n].astype(F32)
            for row in range(EXT):
                for half in range(2):
                    part = scratch[pl.ds(EXT * row, G), half * LANES : (half + 1) * LANES]
                    part = jnp.where(inside, part, 0.0)
                    at = (first_row + 2 * row + half, pl.ds(first_col, G), slice(None))
                    canvas[at] = canvas[at] + part

        return carry

    lax.fori_loop(0, slot_ref.shape[0], per_slot, 0)
    for chunk in range(per_row):
        first = OUT * chunk + 1
        for row in range(half_rows):
            packed[CHUNK * row : CHUNK * row + G, :] = canvas[row, first : first + G, :]
        out_ref[chunk] = packed[...].astype(BF16)


def fold(ids, received, per_row, half_rows):
    return pl.pallas_call(
        lambda *refs: fold_kernel(per_row, half_rows, *refs),
        in_specs=[
            pl.BlockSpec(memory_space=pltpu.SMEM),
            pl.BlockSpec(memory_space=pltpu.VMEM),
        ],
        out_specs=pl.BlockSpec(memory_space=pltpu.VMEM),
        scratch_shapes=[
            pltpu.VMEM((half_rows, PITCH + 8, LANES), F32),
            pltpu.VMEM((SLOT_ROWS, 2 * LANES), F32),
            pltpu.VMEM((CHUNK_ROWS, LANES), F32),
        ],
        out_shape=jax.ShapeDtypeStruct((per_row, CHUNK_ROWS, LANES), BF16),
        cost_estimate=SMALL,
        name="fold",
    )(ids, on_chip(received))


def finish_kernel(half_rows, terms_ref, up_out, middle_out, down_out, summed, canvas):
    total = terms_ref[0].astype(F32)
    for term in range(1, terms_ref.shape[0]):
        total = total + terms_ref[term].astype(F32)
    summed[...] = total
    near = lax.broadcasted_iota(jnp.int32, (8, LANES), 1) < LANES - SHIFT
    for first in range(0, half_rows, 8):
        count = min(8, half_rows - first)
        starts = [CHUNK * (first + row) for row in range(count)]
        tiles = swap_groups(jnp.stack([summed[start : start + 8, :] for start in starts], 0))
        edges = summed[pl.ds(starts[0] + 8, count, stride=CHUNK), :]
        if count < 8:
            edges = jnp.concatenate([edges, jnp.zeros((8 - count, LANES), F32)], axis=0)
        edges = swap_groups(edges.reshape(1, 8, LANES)).reshape(8, LANES)
        for row in range(count):
            tile = pltpu.roll(tiles[row], LANES - SHIFT, 1)
            edge = pltpu.roll(edges, (LANES - SHIFT - G * row) % LANES, 1)
            start = 8 * (first + row)
            canvas[start : start + 8, :] = jnp.where(near, tile, edge)
    middle = middle_out.shape[0]
    up_out[...] = canvas[:HALO, :].astype(BF16)
    middle_out[...] = canvas[HALO : HALO + middle, :]
    down_out[...] = canvas[HALO + middle : 2 * HALO + middle, :].astype(BF16)


def finish(terms, half_rows, rows):
    rim = jax.ShapeDtypeStruct((HALO, LANES), BF16)
    vmem = pl.BlockSpec(memory_space=pltpu.VMEM)
    return pl.pallas_call(
        lambda *refs: finish_kernel(half_rows, *refs),
        in_specs=[vmem],
        out_specs=[vmem, vmem, vmem],
        out_shape=[rim, jax.ShapeDtypeStruct((rows, LANES), F32), rim],
        scratch_shapes=[
            pltpu.VMEM((CHUNK_ROWS, LANES), F32),
            pltpu.VMEM((8 * half_rows, LANES), F32),
        ],
        cost_estimate=SMALL,
        name="finish",
    )(terms)


def shards(sky_model, exposure_data, pixel_mask, block_owner, block_local, psf_cell, psf_table):
    sky_count = lax.axis_size("sky")
    stripe_rows, stripe_cols = sky_model.shape
    per_row = stripe_cols // B
    block_total = stripe_rows // B * per_row
    piece_count = exposure_data.shape[0]
    owner_sky = block_owner[:, 0]
    code = lax.broadcasted_iota(jnp.int32, (piece_count,), 0) * block_total + block_local
    mine = owner_sky[None, :] == lax.broadcasted_iota(jnp.int32, (sky_count, 1), 0)
    first = jnp.min(jnp.where(mine, code[None, :], piece_count * block_total), axis=1)
    last = jnp.max(jnp.where(mine, code[None, :], -1), axis=1)
    requests = jnp.stack(
        [
            jnp.where(last < 0, -1, first % block_total),
            jnp.where(last > first, last % block_total, -1),
        ],
        axis=1,
    )
    asked = lax.all_to_all(requests, "sky", split_axis=0, concat_axis=0, tiled=True)
    asked = asked.reshape(sky_count * CAP)

    above = from_behind(sky_model[stripe_rows - HALO :], "sky", 1)
    below = from_behind(sky_model[:HALO], "sky", -1)
    half_rows = (stripe_rows + 2 * HALO + TAIL) // 8
    own = own_blocks(sky_model)
    asked, own = lax.optimization_barrier((asked, own))
    outgoing = cut_patches(asked, own, sky_model, above, below, half_rows)
    exposure_data, pixel_mask, psf_table, code, _ = lax.optimization_barrier(
        (exposure_data, pixel_mask, psf_table, code, outgoing)
    )
    second = jnp.any(mine & (first[:, None] < code[None, :]), axis=0)
    slot_index = owner_sky * CAP + second.astype(jnp.int32)
    patches = lax.all_to_all(outgoing, "sky", split_axis=0, concat_axis=0, tiled=True)
    data = regroup(exposure_data, pixel_mask)
    taps = build_taps(psf_table)
    adjoints, residuals = pieces(slot_index, psf_cell, patches, taps, data)
    received = lax.all_to_all(adjoints, "sky", split_axis=0, concat_axis=0, tiled=True)
    received, residual = lax.optimization_barrier((received, ungroup(residuals)))

    partial = fold(asked, received, per_row, half_rows)
    terms = lax.all_to_all(partial, "exp", split_axis=0, concat_axis=0, tiled=True)
    up, middle, down = finish(terms, half_rows, stripe_rows)
    from_below = from_behind(up, "sky", -1).astype(F32)
    from_above = from_behind(down, "sky", 1).astype(F32)
    gradient = (
        middle
        + jnp.pad(from_above, ((0, stripe_rows - HALO), (0, 0)))
        + jnp.pad(from_below, ((stripe_rows - HALO, 0), (0, 0)))
    )
    return (gradient, residual)


def solution(mesh):
    in_specs = (
        P("sky", None),
        P(("sky", "exp"), None, None),
        P(("sky", "exp"), None, None),
        P(("sky", "exp"), None),
        P(("sky", "exp")),
        P(("sky", "exp")),
        P("exp", None),
    )
    out_specs = (P("sky", "exp"), P(("sky", "exp"), None, None))
    return jax.shard_map(shards, mesh=mesh, in_specs=in_specs, out_specs=out_specs, check_vma=False)
```

```python
import jax
import jax.numpy as jnp
from jax import lax
from jax.experimental import pallas as pl
from jax.experimental.pallas import tpu as pltpu
from jax.sharding import PartitionSpec as P

B = 128
PSF = 41
HALO = 20
CAP = 2

G = 16
LANES = 128
OUT = B // G
EXT = 11
REACH = 4
TAIL = 8
BLOCKS = OUT * OUT
SLOT_ROWS = 128
PITCH = 72
TILES = 6
RES_LEAD = 40
TAP_ROWS = 48
OWN_FIRST = 3
BATCH = 4
SLOTS = 8
CHUNK = 9
CHUNK_ROWS = 352
SHIFT = 4
SMALL = pl.CostEstimate(flops=1000, bytes_accessed=1000, transcendentals=0)
F32 = jnp.float32
BF16 = jnp.bfloat16


def whole_vmem():
    return pl.BlockSpec(memory_space=pltpu.VMEM)


def on_chip(x):
    return pltpu.with_memory_space_constraint(x, pltpu.VMEM)


def from_behind(x, axis, by):
    devices = lax.axis_size(axis)
    pairs = [(i, i + by) for i in range(devices) if 0 <= i + by < devices]
    return lax.ppermute(x, axis, pairs)


def swap_groups(x):
    sub = lax.broadcasted_iota(jnp.int32, x.shape, 1)
    group = lax.broadcasted_iota(jnp.int32, x.shape, 2) // G
    for d in (4, 2, 1):
        sub_bit, group_bit = (sub & d) != 0, (group & d) != 0
        up = pltpu.roll(pltpu.roll(x, 8 - d, 1), G * d, 2)
        down = up if d == 4 else pltpu.roll(pltpu.roll(x, d, 1), LANES - G * d, 2)
        x = jnp.where(sub_bit == group_bit, x, jnp.where(group_bit, up, down))
    return x


def regroup_kernel(data_ref, keep_ref, out_ref):
    def per_piece(p, carry):
        known = jnp.where(keep_ref[p] != 0, data_ref[p].astype(F32), jnp.inf)
        blocks = swap_groups(known.reshape(2 * OUT, 8, LANES)).reshape(OUT, 2, 8, LANES)
        for half in range(2):
            out_ref[p, :, half * LANES : (half + 1) * LANES] = (
                blocks[:, half].reshape(BLOCKS, LANES).astype(BF16)
            )
        return carry

    lax.fori_loop(0, data_ref.shape[0], per_piece, 0)


def regroup(exposure_data, pixel_mask):
    pieces = exposure_data.shape[0]
    block = pl.BlockSpec((BATCH, B, B), lambda p: (p, 0, 0))
    return pl.pallas_call(
        regroup_kernel,
        grid=(pieces // BATCH,),
        in_specs=[block, block],
        out_specs=pl.BlockSpec((BATCH, BLOCKS, 2 * LANES), lambda p: (p, 0, 0)),
        out_shape=jax.ShapeDtypeStruct((pieces, BLOCKS, 2 * LANES), BF16),
        cost_estimate=SMALL,
        name="regroup",
    )(exposure_data, pixel_mask)


def taps_kernel(kernel_ref, out_ref, windows, rows):
    lane = lax.broadcasted_iota(jnp.int32, (G, LANES), 1)
    odd = (lane // G) % 2 == 1
    wide = lax.broadcasted_iota(jnp.int32, (TAP_ROWS, LANES), 1) // (2 * G)
    quarter = lax.broadcasted_iota(jnp.int32, (TILES, LANES), 1) // (2 * G)

    kernel = kernel_ref[0].astype(F32)
    spread = pltpu.roll(kernel, G, 1)
    for t in range(1, REACH):
        spread = jnp.where(wide == t, pltpu.roll(kernel, G * t + G, 1), spread)
    windows[...] = spread
    for parity in range(2):
        picked = [windows[pl.ds(parity + 2 * q, TILES, stride=8), :] for q in range(4)]
        for t in range(REACH):
            row = picked[0] if t == 0 else pltpu.roll(picked[0], 2 * G * (4 - t), 1)
            for q in range(1, 4):
                by = (q - t) % 4
                part = picked[q] if by == 0 else pltpu.roll(picked[q], 2 * G * by, 1)
                row = jnp.where(quarter == q, part, row)
            rows[t, parity, :TILES, :] = row

    def per_shift(t, carry):
        before = [jnp.zeros((G, LANES), F32)] * 8
        for tile in range(TILES):
            even_row, odd_row = (
                jnp.broadcast_to(rows[t, parity, tile : tile + 1, :], (G, LANES))
                for parity in range(2)
            )
            even_row = pltpu.roll(even_row, LANES - G, 1, stride=1, stride_axis=0)
            odd_row = pltpu.roll(odd_row, 0, 1, stride=1, stride_axis=0)
            now = jnp.where(odd, odd_row, even_row)
            turns = [now] + [pltpu.roll(now, G * phase, 1) for phase in range(1, 8)]
            for phase in range(8):
                part = turns[phase]
                if phase > 0:
                    part = jnp.where(lane < G * phase, before[phase], part)
                start = pl.multiple_of(t * LANES + phase * G, G)
                lanes = slice(tile * LANES, (tile + 1) * LANES)
                out_ref[0, pl.ds(start, G), lanes] = part.astype(BF16)
            before = turns
        return carry

    lax.fori_loop(0, REACH, per_shift, 0)


def build_taps(table):
    cells = table.shape[0]
    kernels = jnp.pad(
        table.reshape(cells, PSF, PSF), ((0, 0), (0, TAP_ROWS - PSF), (0, LANES - PSF))
    )
    return pl.pallas_call(
        taps_kernel,
        grid=(cells,),
        in_specs=[pl.BlockSpec((1, TAP_ROWS, LANES), lambda c: (c, 0, 0))],
        out_specs=pl.BlockSpec((1, REACH * LANES, TILES * LANES), lambda c: (c, 0, 0)),
        out_shape=jax.ShapeDtypeStruct((cells, REACH * LANES, TILES * LANES), BF16),
        scratch_shapes=[
            pltpu.VMEM((TAP_ROWS, LANES), F32),
            pltpu.VMEM((REACH, 2, 8, LANES), F32),
        ],
        cost_estimate=SMALL,
        name="taps",
    )(kernels)


def row_blocks(pixels):
    far = lax.broadcasted_iota(jnp.int32, (8, LANES), 1) >= HALO
    tiles = pixels.shape[1] // LANES
    empty = jnp.zeros((8, LANES), F32)
    turned = [
        pltpu.roll(pixels[:, tile * LANES : (tile + 1) * LANES], HALO, 1) for tile in range(tiles)
    ]
    before, after = [empty] + turned, turned + [empty]
    moved = [jnp.where(far, now, old) for old, now in zip(before, after)]
    return swap_groups(jnp.stack(moved, 0)).reshape((tiles + 1) * 8, LANES)


def own_kernel(stripe_ref, out_ref, pixels):
    skip = 8 * OWN_FIRST - HALO
    pixels[...] = stripe_ref[...].astype(F32)

    for row in range(out_ref.shape[0]):
        out_ref[row] = row_blocks(pixels[skip + 8 * row : skip + 8 * row + 8, :])


def own_blocks(stripe):
    rows, columns = stripe.shape
    count = (rows + HALO) // 8 - OWN_FIRST
    return pl.pallas_call(
        own_kernel,
        in_specs=[pl.BlockSpec(memory_space=pltpu.VMEM)],
        out_specs=pl.BlockSpec(memory_space=pltpu.VMEM),
        out_shape=pltpu.VMEM((count, PITCH, LANES), F32),
        scratch_shapes=[pltpu.VMEM((rows, columns), F32)],
        cost_estimate=SMALL,
        name="own",
    )(stripe)


def cut_kernel(
    per_row, ids_ref, own_ref, above_ref, top_ref, bottom_ref, below_ref, out_ref, blocks, upper, lower, scratch
):
    step = pl.program_id(0)

    @pl.when(step == 0)
    def _():
        own = own_ref.shape[0]
        blocks[OWN_FIRST : OWN_FIRST + own] = own_ref[...]
        missing = 8 * OWN_FIRST - HALO
        upper[:HALO, :] = above_ref[...].astype(F32)
        upper[HALO:, :] = top_ref[...].astype(F32)[:missing]
        for row in range(OWN_FIRST):
            blocks[row] = row_blocks(upper[8 * row : 8 * row + 8, :])
        lower[...] = jnp.zeros_like(lower)
        lower[:missing, :] = bottom_ref[...].astype(F32)[G - missing :]
        lower[missing : missing + HALO, :] = below_ref[...].astype(F32)
        for row in range(lower.shape[0] // 8):
            blocks[OWN_FIRST + own + row] = row_blocks(lower[8 * row : 8 * row + 8, :])

    def per_slot(n, carry):
        wanted = ids_ref[step * SLOTS + n]

        @pl.when(wanted >= 0)
        def _():
            first_row = wanted // per_row * (2 * OUT)
            first_col = pl.multiple_of(wanted % per_row * OUT, 8)
            for row in range(EXT):
                for half in range(2):
                    part = blocks[first_row + 2 * row + half, pl.ds(first_col, G), :]
                    scratch[pl.ds(EXT * row, G), half * LANES : (half + 1) * LANES] = part
            out_ref[n] = scratch[...].astype(BF16)

        return carry

    lax.fori_loop(0, SLOTS, per_slot, 0)


def cut_patches(ids, own, stripe, above, below, half_rows):
    slots = ids.shape[0]
    rows, columns = stripe.shape
    last = rows // G - 1
    return pl.pallas_call(
        lambda *refs: cut_kernel(columns // B, *refs),
        grid_spec=pltpu.PrefetchScalarGridSpec(
            num_scalar_prefetch=1,
            grid=(slots // SLOTS,),
            in_specs=[
                whole_vmem(),
                whole_vmem(),
                pl.BlockSpec((G, columns), lambda n, ids: (0, 0)),
                pl.BlockSpec((G, columns), lambda n, ids: (last, 0)),
                whole_vmem(),
            ],
            out_specs=pl.BlockSpec((SLOTS, SLOT_ROWS, 2 * LANES), lambda n, ids: (n, 0, 0)),
            scratch_shapes=[
                pltpu.VMEM((half_rows, PITCH, LANES), F32),
                pltpu.VMEM((8 * OWN_FIRST, columns), F32),
                pltpu.VMEM((8 * (half_rows - OWN_FIRST - own.shape[0]), columns), F32),
                pltpu.VMEM((SLOT_ROWS, 2 * LANES), F32),
            ],
        ),
        out_shape=jax.ShapeDtypeStruct((slots, SLOT_ROWS, 2 * LANES), BF16),
        cost_estimate=SMALL,
        name="cut",
    )(ids, on_chip(own), on_chip(above), stripe, stripe, on_chip(below))


def block_taps(taps_ref, s, t):
    taps = slice(t * LANES, (t + 1) * LANES)
    upper = taps_ref[0, taps, 2 * s * LANES : (2 * s + 2) * LANES]
    if s == 0:
        lower = jnp.concatenate(
            [jnp.zeros((LANES, LANES), BF16), taps_ref[0, taps, 0:LANES]], axis=1
        )
    else:
        lower = taps_ref[0, taps, (2 * s - 1) * LANES : (2 * s + 1) * LANES]
    return jnp.concatenate([upper, lower], axis=0)


def last_taps(taps_ref, t):
    return taps_ref[0, t * LANES : (t + 1) * LANES, (TILES - 1) * LANES :]


def correlate(read, taps_ref):
    across = (((1,), (1,)), ((), ()))
    total = jnp.zeros((2 * BLOCKS, LANES), F32)
    for t in range(REACH):
        for d in range(TILES // 2):
            taps = taps_ref[0, t * LANES : (t + 1) * LANES, 2 * d * LANES : (2 * d + 2) * LANES]
            total = total + lax.dot_general(
                read(d, t), taps, across, preferred_element_type=F32
            )
    return jnp.concatenate([total[:BLOCKS], total[BLOCKS:]], axis=1)


def convolve(read, taps_ref, rows):
    total = jnp.zeros((rows, 2 * LANES), F32)
    for t in range(REACH):
        for s in range(REACH - 1):
            total = total + jnp.dot(
                read(s, t), block_taps(taps_ref, s, t), preferred_element_type=F32
            )
    last = jnp.zeros((rows, LANES), F32)
    for t in range(0, REACH, 2):
        field = [read(REACH - 1, t + i)[:, LANES:] for i in range(2)]
        taps = [last_taps(taps_ref, t + i) for i in range(2)]
        last = last + jnp.dot(
            jnp.concatenate(field, axis=1),
            jnp.concatenate(taps, axis=0),
            preferred_element_type=F32,
        )
    return jnp.concatenate([total[:, :LANES] + last, total[:, LANES:]], axis=1)


def piece_kernel(slot_ref, cell_ref, patch_ref, taps_ref, data_ref, adj_out, res_out, field, resid):
    piece = pl.program_id(0)

    @pl.when(piece == 0)
    def _():
        resid[...] = jnp.zeros_like(resid)

    field[...] = patch_ref[slot_ref[piece]].astype(F32)

    def read_patch(d, t):
        starts = [EXT * (row + d) + t for row in range(OUT)]
        upper = [field[at : at + OUT, :] for at in starts]
        lower = [
            jnp.concatenate(
                [field[at : at + OUT, LANES:], field[at + EXT : at + EXT + OUT, :LANES]], axis=1
            )
            for at in starts
        ]
        return jnp.concatenate(upper + lower, axis=0).astype(BF16)

    predicted = correlate(read_patch, taps_ref)
    observed = data_ref[0].astype(F32)
    residual = jnp.where(observed < jnp.inf, predicted - observed, 0.0).astype(BF16)
    res_out[0] = residual
    wide = residual.astype(F32)
    for row in range(OUT):
        first = RES_LEAD + EXT * row
        resid[first : first + OUT, :] = wide[OUT * row : OUT * (row + 1)]

    def read_residual(s, t):
        return resid[pl.ds(RES_LEAD - EXT * s - t, SLOT_ROWS), :].astype(BF16)

    adj_out[0] = convolve(read_residual, taps_ref, SLOT_ROWS).astype(BF16)


def pieces(slots, cells, patches, taps, data):
    count = data.shape[0]
    slot = pl.BlockSpec((1, SLOT_ROWS, 2 * LANES), lambda p, slots, cells: (slots[p], 0, 0))
    cell = pl.BlockSpec(
        (1, REACH * LANES, TILES * LANES), lambda p, slots, cells: (cells[p], 0, 0)
    )
    block = pl.BlockSpec((1, BLOCKS, 2 * LANES), lambda p, slots, cells: (p, 0, 0))
    return pl.pallas_call(
        piece_kernel,
        grid_spec=pltpu.PrefetchScalarGridSpec(
            num_scalar_prefetch=2,
            grid=(count,),
            in_specs=[whole_vmem(), cell, block],
            out_specs=[slot, block],
            scratch_shapes=[
                pltpu.VMEM((SLOT_ROWS, 2 * LANES), F32),
                pltpu.VMEM((RES_LEAD + SLOT_ROWS, 2 * LANES), F32),
            ],
        ),
        out_shape=[
            jax.ShapeDtypeStruct(patches.shape, BF16),
            jax.ShapeDtypeStruct(data.shape, BF16),
        ],
        cost_estimate=SMALL,
        name="pieces",
    )(slots, cells, on_chip(patches), taps, data)


def ungroup_kernel(res_ref, out_ref):
    def per_piece(p, carry):
        halves = [
            res_ref[p, :, half * LANES : (half + 1) * LANES].astype(F32).reshape(OUT, 8, LANES)
            for half in range(2)
        ]
        pixels = swap_groups(jnp.stack(halves, 1).reshape(2 * OUT, 8, LANES))
        out_ref[p] = pixels.reshape(B, LANES).astype(BF16)
        return carry

    lax.fori_loop(0, res_ref.shape[0], per_piece, 0)


def ungroup(residual):
    count = residual.shape[0]
    return pl.pallas_call(
        ungroup_kernel,
        grid=(count // BATCH,),
        in_specs=[pl.BlockSpec((BATCH, BLOCKS, 2 * LANES), lambda p: (p, 0, 0))],
        out_specs=pl.BlockSpec((BATCH, B, B), lambda p: (p, 0, 0)),
        out_shape=jax.ShapeDtypeStruct((count, B, B), BF16),
        cost_estimate=SMALL,
        name="ungroup",
    )(residual)


def fold_kernel(per_row, half_rows, ids_ref, slot_ref, out_ref, canvas, scratch, packed):
    canvas[...] = jnp.zeros_like(canvas)
    inside = lax.broadcasted_iota(jnp.int32, (G, LANES), 0) < EXT

    def per_slot(n, carry):
        named = ids_ref[n]

        @pl.when(named >= 0)
        def _():
            first_row = named // per_row * (2 * OUT)
            first_col = pl.multiple_of(named % per_row * OUT, 8)
            scratch[...] = slot_ref[n].astype(F32)
            for row in range(EXT):
                for half in range(2):
                    part = scratch[pl.ds(EXT * row, G), half * LANES : (half + 1) * LANES]
                    part = jnp.where(inside, part, 0.0)
                    at = (first_row + 2 * row + half, pl.ds(first_col, G), slice(None))
                    canvas[at] = canvas[at] + part

        return carry

    lax.fori_loop(0, slot_ref.shape[0], per_slot, 0)
    for chunk in range(per_row):
        first = OUT * chunk + 1
        for row in range(half_rows):
            packed[CHUNK * row : CHUNK * row + G, :] = canvas[row, first : first + G, :]
        out_ref[chunk] = packed[...].astype(BF16)


def fold(ids, received, per_row, half_rows):
    return pl.pallas_call(
        lambda *refs: fold_kernel(per_row, half_rows, *refs),
        in_specs=[
            pl.BlockSpec(memory_space=pltpu.SMEM),
            pl.BlockSpec(memory_space=pltpu.VMEM),
        ],
        out_specs=pl.BlockSpec(memory_space=pltpu.VMEM),
        scratch_shapes=[
            pltpu.VMEM((half_rows, PITCH + 8, LANES), F32),
            pltpu.VMEM((SLOT_ROWS, 2 * LANES), F32),
            pltpu.VMEM((CHUNK_ROWS, LANES), F32),
        ],
        out_shape=jax.ShapeDtypeStruct((per_row, CHUNK_ROWS, LANES), BF16),
        cost_estimate=SMALL,
        name="fold",
    )(ids, on_chip(received))


def finish_kernel(half_rows, terms_ref, up_out, middle_out, down_out, summed, canvas):
    total = terms_ref[0].astype(F32)
    for term in range(1, terms_ref.shape[0]):
        total = total + terms_ref[term].astype(F32)
    summed[...] = total
    near = lax.broadcasted_iota(jnp.int32, (8, LANES), 1) < LANES - SHIFT
    for first in range(0, half_rows, 8):
        count = min(8, half_rows - first)
        starts = [CHUNK * (first + row) for row in range(count)]
        tiles = swap_groups(jnp.stack([summed[start : start + 8, :] for start in starts], 0))
        edges = summed[pl.ds(starts[0] + 8, count, stride=CHUNK), :]
        if count < 8:
            edges = jnp.concatenate([edges, jnp.zeros((8 - count, LANES), F32)], axis=0)
        edges = swap_groups(edges.reshape(1, 8, LANES)).reshape(8, LANES)
        for row in range(count):
            tile = pltpu.roll(tiles[row], LANES - SHIFT, 1)
            edge = pltpu.roll(edges, (LANES - SHIFT - G * row) % LANES, 1)
            start = 8 * (first + row)
            canvas[start : start + 8, :] = jnp.where(near, tile, edge)
    middle = middle_out.shape[0]
    up_out[...] = canvas[:HALO, :].astype(BF16)
    middle_out[...] = canvas[HALO : HALO + middle, :]
    down_out[...] = canvas[HALO + middle : 2 * HALO + middle, :].astype(BF16)


def finish(terms, half_rows, rows):
    rim = jax.ShapeDtypeStruct((HALO, LANES), BF16)
    vmem = pl.BlockSpec(memory_space=pltpu.VMEM)
    return pl.pallas_call(
        lambda *refs: finish_kernel(half_rows, *refs),
        in_specs=[vmem],
        out_specs=[vmem, vmem, vmem],
        out_shape=[rim, jax.ShapeDtypeStruct((rows, LANES), F32), rim],
        scratch_shapes=[
            pltpu.VMEM((CHUNK_ROWS, LANES), F32),
            pltpu.VMEM((8 * half_rows, LANES), F32),
        ],
        cost_estimate=SMALL,
        name="finish",
    )(terms)


def shards(sky_model, exposure_data, pixel_mask, block_owner, block_local, psf_cell, psf_table):
    sky_count = lax.axis_size("sky")
    stripe_rows, stripe_cols = sky_model.shape
    per_row = stripe_cols // B
    block_total = stripe_rows // B * per_row
    piece_count = exposure_data.shape[0]
    owner_sky = block_owner[:, 0]
    code = lax.broadcasted_iota(jnp.int32, (piece_count,), 0) * block_total + block_local
    mine = owner_sky[None, :] == lax.broadcasted_iota(jnp.int32, (sky_count, 1), 0)
    first = jnp.min(jnp.where(mine, code[None, :], piece_count * block_total), axis=1)
    last = jnp.max(jnp.where(mine, code[None, :], -1), axis=1)
    requests = jnp.stack(
        [
            jnp.where(last < 0, -1, first % block_total),
            jnp.where(last > first, last % block_total, -1),
        ],
        axis=1,
    )
    asked = lax.all_to_all(requests, "sky", split_axis=0, concat_axis=0, tiled=True)
    asked = asked.reshape(sky_count * CAP)

    above = from_behind(sky_model[stripe_rows - HALO :], "sky", 1)
    below = from_behind(sky_model[:HALO], "sky", -1)
    half_rows = (stripe_rows + 2 * HALO + TAIL) // 8
    own = own_blocks(sky_model)
    asked, own = lax.optimization_barrier((asked, own))
    outgoing = cut_patches(asked, own, sky_model, above, below, half_rows)
    exposure_data, pixel_mask, psf_table, code, _ = lax.optimization_barrier(
        (exposure_data, pixel_mask, psf_table, code, outgoing)
    )
    second = jnp.any(mine & (first[:, None] < code[None, :]), axis=0)
    slot_index = owner_sky * CAP + second.astype(jnp.int32)
    patches = lax.all_to_all(outgoing, "sky", split_axis=0, concat_axis=0, tiled=True)
    data = regroup(exposure_data, pixel_mask)
    taps = build_taps(psf_table)
    adjoints, residuals = pieces(slot_index, psf_cell, patches, taps, data)
    received = lax.all_to_all(adjoints, "sky", split_axis=0, concat_axis=0, tiled=True)
    received, residual = lax.optimization_barrier((received, ungroup(residuals)))

    partial = fold(asked, received, per_row, half_rows)
    terms = lax.all_to_all(partial, "exp", split_axis=0, concat_axis=0, tiled=True)
    up, middle, down = finish(terms, half_rows, stripe_rows)
    from_below = from_behind(up, "sky", -1).astype(F32)
    from_above = from_behind(down, "sky", 1).astype(F32)
    gradient = (
        middle
        + jnp.pad(from_above, ((0, stripe_rows - HALO), (0, 0)))
        + jnp.pad(from_below, ((stripe_rows - HALO, 0), (0, 0)))
    )
    return (gradient, residual)


def solution(mesh):
    in_specs = (
        P("sky", None),
        P(("sky", "exp"), None, None),
        P(("sky", "exp"), None, None),
        P(("sky", "exp"), None),
        P(("sky", "exp")),
        P(("sky", "exp")),
        P("exp", None),
    )
    out_specs = (P("sky", "exp"), P(("sky", "exp"), None, None))
    return jax.shard_map(shards, mesh=mesh, in_specs=in_specs, out_specs=out_specs, check_vma=False)
```

```python
import jax
import jax.numpy as jnp
from jax import lax
from jax.experimental import pallas as pl
from jax.experimental.pallas import tpu as pltpu
from jax.sharding import PartitionSpec as P

B = 128
PSF = 41
HALO = 20
CAP = 2

G = 16
LANES = 128
OUT = B // G
EXT = 11
REACH = 4
TAIL = 8
BLOCKS = OUT * OUT
PATCH_ROWS = 240
SLOT_ROWS = 128
PITCH = 72
TILES = 6
RES_LEAD = 40
TAP_ROWS = 48
OWN_FIRST = 3
BATCH = 4
SLOTS = 8
CHUNK = 9
CHUNK_ROWS = 352
SHIFT = 4
UNKNOWN = 2.0**100
SMALL = pl.CostEstimate(flops=1000, bytes_accessed=1000, transcendentals=0)
F32 = jnp.float32
BF16 = jnp.bfloat16


def whole_vmem():
    return pl.BlockSpec(memory_space=pltpu.VMEM)


def on_chip(x):
    return pltpu.with_memory_space_constraint(x, pltpu.VMEM)


def from_behind(x, axis, by):
    devices = lax.axis_size(axis)
    pairs = [(i, i + by) for i in range(devices) if 0 <= i + by < devices]
    return lax.ppermute(x, axis, pairs)


def swap_groups(x):
    sub = lax.broadcasted_iota(jnp.int32, x.shape, 1)
    group = lax.broadcasted_iota(jnp.int32, x.shape, 2) // G
    for d in (4, 2, 1):
        sub_bit, group_bit = (sub & d) != 0, (group & d) != 0
        up = pltpu.roll(pltpu.roll(x, 8 - d, 1), G * d, 2)
        down = up if d == 4 else pltpu.roll(pltpu.roll(x, d, 1), LANES - G * d, 2)
        x = jnp.where(sub_bit == group_bit, x, jnp.where(group_bit, up, down))
    return x


def reversed_groups(shift=0):
    source = lax.broadcasted_iota(jnp.int32, (2 * LANES, LANES), 0)
    lane = lax.broadcasted_iota(jnp.int32, (2 * LANES, LANES), 1)
    group = (8 - lane // G) % 8
    return (source == LANES - shift + group * G + lane % G).astype(BF16)


def swap_reversed(x):
    group = lax.broadcasted_iota(jnp.int32, (8, LANES), 1) // G
    tiles = []
    for tile in range(x.shape[0]):
        now = pltpu.roll(x[tile], 0, 1, stride=G, stride_axis=0)
        for d in (1, 2, 4):
            now = jnp.where((group & d) != 0, pltpu.roll(now, 8 - d, 0), now)
        tiles.append(pltpu.roll(now, 0, 1, stride=G, stride_axis=0))
    return jnp.stack(tiles, 0)


def regroup_kernel(data_ref, keep_ref, out_ref):
    def per_piece(p, carry):
        known = jnp.where(keep_ref[p] != 0, data_ref[p].astype(F32), UNKNOWN).astype(BF16)
        turned = jnp.dot(known, reversed_groups()[LANES:], preferred_element_type=F32)
        blocks = swap_reversed(turned.reshape(2 * OUT, 8, LANES)).reshape(OUT, 2, 8, LANES)
        for half in range(2):
            out_ref[p, :, half * LANES : (half + 1) * LANES] = (
                blocks[:, half].reshape(BLOCKS, LANES).astype(BF16)
            )
        return carry

    lax.fori_loop(0, data_ref.shape[0], per_piece, 0)


def regroup(exposure_data, pixel_mask):
    pieces = exposure_data.shape[0]
    block = pl.BlockSpec((BATCH, B, B), lambda p: (p, 0, 0))
    return pl.pallas_call(
        regroup_kernel,
        grid=(pieces // BATCH,),
        in_specs=[block, block],
        out_specs=pl.BlockSpec((BATCH, BLOCKS, 2 * LANES), lambda p: (p, 0, 0)),
        out_shape=jax.ShapeDtypeStruct((pieces, BLOCKS, 2 * LANES), BF16),
        cost_estimate=SMALL,
        name="regroup",
    )(exposure_data, pixel_mask)


def taps_kernel(kernel_ref, out_ref, windows, rows):
    lane = lax.broadcasted_iota(jnp.int32, (G, LANES), 1)
    odd = (lane // G) % 2 == 1
    wide = lax.broadcasted_iota(jnp.int32, (TAP_ROWS, LANES), 1) // (2 * G)
    quarter = lax.broadcasted_iota(jnp.int32, (TILES, LANES), 1) // (2 * G)

    kernel = kernel_ref[0].astype(F32)
    spread = pltpu.roll(kernel, G, 1)
    for t in range(1, REACH):
        spread = jnp.where(wide == t, pltpu.roll(kernel, G * t + G, 1), spread)
    windows[...] = spread
    for parity in range(2):
        picked = [windows[pl.ds(parity + 2 * q, TILES, stride=8), :] for q in range(4)]
        for t in range(REACH):
            row = picked[0] if t == 0 else pltpu.roll(picked[0], 2 * G * (4 - t), 1)
            for q in range(1, 4):
                by = (q - t) % 4
                part = picked[q] if by == 0 else pltpu.roll(picked[q], 2 * G * by, 1)
                row = jnp.where(quarter == q, part, row)
            rows[t, parity, :TILES, :] = row

    def per_shift(t, carry):
        before = [jnp.zeros((G, LANES), F32)] * 8
        for tile in range(TILES):
            even_row, odd_row = (
                jnp.broadcast_to(rows[t, parity, tile : tile + 1, :], (G, LANES))
                for parity in range(2)
            )
            even_row = pltpu.roll(even_row, LANES - G, 1, stride=1, stride_axis=0)
            odd_row = pltpu.roll(odd_row, 0, 1, stride=1, stride_axis=0)
            now = jnp.where(odd, odd_row, even_row)
            turns = [now] + [pltpu.roll(now, G * phase, 1) for phase in range(1, 8)]
            for phase in range(8):
                part = turns[phase]
                if phase > 0:
                    part = jnp.where(lane < G * phase, before[phase], part)
                start = pl.multiple_of(t * LANES + phase * G, G)
                lanes = slice(tile * LANES, (tile + 1) * LANES)
                out_ref[0, pl.ds(start, G), lanes] = part.astype(BF16)
            before = turns
        return carry

    lax.fori_loop(0, REACH, per_shift, 0)


def build_taps(table):
    cells = table.shape[0]
    kernels = jnp.pad(
        table.reshape(cells, PSF, PSF), ((0, 0), (0, TAP_ROWS - PSF), (0, LANES - PSF))
    )
    return pl.pallas_call(
        taps_kernel,
        grid=(cells,),
        in_specs=[pl.BlockSpec((1, TAP_ROWS, LANES), lambda c: (c, 0, 0))],
        out_specs=pl.BlockSpec((1, REACH * LANES, TILES * LANES), lambda c: (c, 0, 0)),
        out_shape=jax.ShapeDtypeStruct((cells, REACH * LANES, TILES * LANES), BF16),
        scratch_shapes=[
            pltpu.VMEM((TAP_ROWS, LANES), F32),
            pltpu.VMEM((REACH, 2, 8, LANES), F32),
        ],
        cost_estimate=SMALL,
        name="taps",
    )(kernels)


def moved_tiles(pixels):
    rows, columns = pixels.shape
    turn = reversed_groups(HALO)
    empty = jnp.zeros((rows, LANES), BF16)
    tiles = [pixels[:, at : at + LANES] for at in range(0, columns, LANES)]
    return [
        jnp.dot(jnp.concatenate([old, now], axis=1), turn, preferred_element_type=F32)
        for old, now in zip([empty] + tiles, tiles + [empty])
    ]


def own_kernel(stripe_ref, out_ref, pixels):
    skip = 8 * OWN_FIRST - HALO
    for tile, moved in enumerate(moved_tiles(stripe_ref[...])):
        pixels[:, tile * LANES : (tile + 1) * LANES] = moved

    for row in range(out_ref.shape[0]):
        first = skip + 8 * row
        tiles = [
            pixels[first : first + 8, at : at + LANES] for at in range(0, PITCH * G, LANES)
        ]
        out_ref[row] = swap_reversed(jnp.stack(tiles, 0)).reshape(PITCH, LANES)


def own_blocks(stripe):
    rows, columns = stripe.shape
    count = (rows + HALO) // 8 - OWN_FIRST
    return pl.pallas_call(
        own_kernel,
        in_specs=[pl.BlockSpec(memory_space=pltpu.VMEM)],
        out_specs=pl.BlockSpec(memory_space=pltpu.VMEM),
        out_shape=pltpu.VMEM((count, PITCH, LANES), F32),
        scratch_shapes=[pltpu.VMEM((rows, PITCH * G), F32)],
        cost_estimate=SMALL,
        name="own",
    )(stripe)


def cut_kernel(
    per_row, ids_ref, own_ref, above_ref, top_ref, bottom_ref, below_ref, out_ref, blocks, upper, lower, scratch
):
    step = pl.program_id(0)

    @pl.when(step == 0)
    def _():
        own = own_ref.shape[0]
        blocks[OWN_FIRST : OWN_FIRST + own] = own_ref[...]
        missing = 8 * OWN_FIRST - HALO
        rims = ((above_ref, 0), (top_ref, 1), (bottom_ref, 2), (below_ref, 3))
        tiles = {at: moved_tiles(ref[...]) for ref, at in rims}
        lower[...] = jnp.zeros_like(lower)
        for tile in range(PITCH // 8):
            lanes = slice(tile * LANES, (tile + 1) * LANES)
            upper[:HALO, lanes] = tiles[0][tile]
            upper[HALO:, lanes] = tiles[1][tile][:missing]
            lower[:missing, lanes] = tiles[2][tile][G - missing :]
            lower[missing : missing + HALO, lanes] = tiles[3][tile]
        for pixels, first in ((upper, 0), (lower, OWN_FIRST + own)):
            for row in range(pixels.shape[0] // 8):
                parts = [
                    pixels[8 * row : 8 * row + 8, at : at + LANES]
                    for at in range(0, PITCH * G, LANES)
                ]
                blocks[first + row] = swap_reversed(jnp.stack(parts, 0)).reshape(PITCH, LANES)

    def per_slot(n, carry):
        wanted = ids_ref[step * SLOTS + n]

        @pl.when(wanted >= 0)
        def _():
            first_row = wanted // per_row * (2 * OUT)
            first_col = pl.multiple_of(wanted % per_row * OUT, 8)
            for row in range(2 * EXT - 1):
                part = blocks[first_row + row, pl.ds(first_col, G), :]
                scratch[EXT * row : EXT * row + G, :] = part
            out_ref[n] = scratch[...].astype(BF16)

        return carry

    lax.fori_loop(0, SLOTS, per_slot, 0)


def cut_patches(ids, own, stripe, above, below, half_rows):
    slots = ids.shape[0]
    rows, columns = stripe.shape
    last = rows // G - 1
    return pl.pallas_call(
        lambda *refs: cut_kernel(columns // B, *refs),
        grid_spec=pltpu.PrefetchScalarGridSpec(
            num_scalar_prefetch=1,
            grid=(slots // SLOTS,),
            in_specs=[
                whole_vmem(),
                whole_vmem(),
                pl.BlockSpec((G, columns), lambda n, ids: (0, 0)),
                pl.BlockSpec((G, columns), lambda n, ids: (last, 0)),
                whole_vmem(),
            ],
            out_specs=pl.BlockSpec((SLOTS, PATCH_ROWS, LANES), lambda n, ids: (n, 0, 0)),
            scratch_shapes=[
                pltpu.VMEM((half_rows, PITCH, LANES), F32),
                pltpu.VMEM((8 * OWN_FIRST, PITCH * G), F32),
                pltpu.VMEM((8 * (half_rows - OWN_FIRST - own.shape[0]), PITCH * G), F32),
                pltpu.VMEM((PATCH_ROWS, LANES), F32),
            ],
        ),
        out_shape=jax.ShapeDtypeStruct((slots, PATCH_ROWS, LANES), BF16),
        cost_estimate=SMALL,
        name="cut",
    )(ids, on_chip(own), on_chip(above), stripe, stripe, on_chip(below))


def block_taps(taps_ref, s, t):
    taps = slice(t * LANES, (t + 1) * LANES)
    upper = taps_ref[0, taps, 2 * s * LANES : (2 * s + 2) * LANES]
    if s == 0:
        lower = jnp.concatenate(
            [jnp.zeros((LANES, LANES), BF16), taps_ref[0, taps, 0:LANES]], axis=1
        )
    else:
        lower = taps_ref[0, taps, (2 * s - 1) * LANES : (2 * s + 1) * LANES]
    return jnp.concatenate([upper, lower], axis=0)


def last_taps(taps_ref, t):
    return taps_ref[0, t * LANES : (t + 1) * LANES, (TILES - 1) * LANES :]


def correlate(read, taps_ref):
    across = (((1,), (1,)), ((), ()))
    total = jnp.zeros((2 * BLOCKS, LANES), F32)
    for t in range(REACH):
        for d in range(TILES // 2):
            taps = taps_ref[0, t * LANES : (t + 1) * LANES, 2 * d * LANES : (2 * d + 2) * LANES]
            total = total + lax.dot_general(
                read(d, t), taps, across, preferred_element_type=F32
            )
    return jnp.concatenate([total[:BLOCKS], total[BLOCKS:]], axis=1)


def convolve(read, taps_ref, rows):
    total = jnp.zeros((rows, 2 * LANES), F32)
    for t in range(REACH):
        for s in range(REACH - 1):
            total = total + jnp.dot(
                read(s, t), block_taps(taps_ref, s, t), preferred_element_type=F32
            )
    last = jnp.zeros((rows, LANES), F32)
    for t in range(0, REACH, 2):
        field = [read(REACH - 1, t + i)[:, LANES:] for i in range(2)]
        taps = [last_taps(taps_ref, t + i) for i in range(2)]
        last = last + jnp.dot(
            jnp.concatenate(field, axis=1),
            jnp.concatenate(taps, axis=0),
            preferred_element_type=F32,
        )
    return jnp.concatenate([total[:, :LANES] + last, total[:, LANES:]], axis=1)


def piece_kernel(slot_ref, cell_ref, patch_ref, taps_ref, data_ref, adj_out, res_out, field, resid):
    piece = pl.program_id(0)

    @pl.when(piece == 0)
    def _():
        resid[...] = jnp.zeros_like(resid)

    field[...] = patch_ref[slot_ref[piece]].astype(F32)

    def read_patch(d, t):
        parts = []
        for half in range(2):
            for row in range(OUT):
                at = EXT * (2 * (row + d) + half) + t
                pair = [field[at : at + OUT, :], field[at + EXT : at + EXT + OUT, :]]
                parts.append(jnp.concatenate(pair, axis=1))
        return jnp.concatenate(parts, axis=0).astype(BF16)

    predicted = correlate(read_patch, taps_ref)
    observed = data_ref[0].astype(F32)
    residual = jnp.where(observed < UNKNOWN, predicted - observed, 0.0).astype(BF16)
    res_out[0] = residual
    wide = residual.astype(F32)
    for row in range(OUT):
        first = RES_LEAD + EXT * row
        resid[first : first + OUT, :] = wide[OUT * row : OUT * (row + 1)]

    def read_residual(s, t):
        return resid[pl.ds(RES_LEAD - EXT * s - t, SLOT_ROWS), :].astype(BF16)

    adj_out[0] = convolve(read_residual, taps_ref, SLOT_ROWS).astype(BF16)


def pieces(slots, cells, patches, taps, data):
    count = data.shape[0]
    slot = pl.BlockSpec((1, SLOT_ROWS, 2 * LANES), lambda p, slots, cells: (slots[p], 0, 0))
    cell = pl.BlockSpec(
        (1, REACH * LANES, TILES * LANES), lambda p, slots, cells: (cells[p], 0, 0)
    )
    block = pl.BlockSpec((1, BLOCKS, 2 * LANES), lambda p, slots, cells: (p, 0, 0))
    return pl.pallas_call(
        piece_kernel,
        grid_spec=pltpu.PrefetchScalarGridSpec(
            num_scalar_prefetch=2,
            grid=(count,),
            in_specs=[whole_vmem(), cell, block],
            out_specs=[slot, block],
            scratch_shapes=[
                pltpu.VMEM((PATCH_ROWS, LANES), F32),
                pltpu.VMEM((RES_LEAD + SLOT_ROWS, 2 * LANES), F32),
            ],
        ),
        out_shape=[
            jax.ShapeDtypeStruct((patches.shape[0], SLOT_ROWS, 2 * LANES), BF16),
            jax.ShapeDtypeStruct(data.shape, BF16),
        ],
        cost_estimate=SMALL,
        name="pieces",
    )(slots, cells, on_chip(patches), taps, data)


def ungroup_kernel(res_ref, out_ref):
    turn = reversed_groups()[LANES:]

    def per_piece(p, carry):
        halves = [
            jnp.dot(
                res_ref[p, :, half * LANES : (half + 1) * LANES], turn, preferred_element_type=F32
            ).reshape(OUT, 8, LANES)
            for half in range(2)
        ]
        pixels = swap_reversed(jnp.stack(halves, 1).reshape(2 * OUT, 8, LANES))
        out_ref[p] = pixels.reshape(B, LANES).astype(BF16)
        return carry

    lax.fori_loop(0, res_ref.shape[0], per_piece, 0)


def ungroup(residual):
    count = residual.shape[0]
    return pl.pallas_call(
        ungroup_kernel,
        grid=(count // BATCH,),
        in_specs=[pl.BlockSpec((BATCH, BLOCKS, 2 * LANES), lambda p: (p, 0, 0))],
        out_specs=pl.BlockSpec((BATCH, B, B), lambda p: (p, 0, 0)),
        out_shape=jax.ShapeDtypeStruct((count, B, B), BF16),
        cost_estimate=SMALL,
        name="ungroup",
    )(residual)


def fold_kernel(per_row, half_rows, ids_ref, slot_ref, out_ref, canvas, scratch, packed):
    canvas[...] = jnp.zeros_like(canvas)
    inside = lax.broadcasted_iota(jnp.int32, (G, LANES), 0) < EXT

    def per_slot(n, carry):
        named = ids_ref[n]

        @pl.when(named >= 0)
        def _():
            first_row = named // per_row * (2 * OUT)
            first_col = pl.multiple_of(named % per_row * OUT, 8)
            scratch[...] = slot_ref[n].astype(F32)
            for row in range(EXT):
                for half in range(2):
                    part = scratch[pl.ds(EXT * row, G), half * LANES : (half + 1) * LANES]
                    part = jnp.where(inside, part, 0.0)
                    at = (first_row + 2 * row + half, pl.ds(first_col, G), slice(None))
                    canvas[at] = canvas[at] + part

        return carry

    lax.fori_loop(0, slot_ref.shape[0], per_slot, 0)
    for chunk in range(per_row):
        first = OUT * chunk + 1
        for row in range(half_rows):
            packed[CHUNK * row : CHUNK * row + G, :] = canvas[row, first : first + G, :]
        out_ref[chunk] = packed[...].astype(BF16)


def fold(ids, received, per_row, half_rows):
    return pl.pallas_call(
        lambda *refs: fold_kernel(per_row, half_rows, *refs),
        in_specs=[
            pl.BlockSpec(memory_space=pltpu.SMEM),
            pl.BlockSpec(memory_space=pltpu.VMEM),
        ],
        out_specs=pl.BlockSpec(memory_space=pltpu.VMEM),
        scratch_shapes=[
            pltpu.VMEM((half_rows, PITCH + 8, LANES), F32),
            pltpu.VMEM((SLOT_ROWS, 2 * LANES), F32),
            pltpu.VMEM((CHUNK_ROWS, LANES), F32),
        ],
        out_shape=jax.ShapeDtypeStruct((per_row, CHUNK_ROWS, LANES), BF16),
        cost_estimate=SMALL,
        name="fold",
    )(ids, on_chip(received))


def finish_kernel(half_rows, terms_ref, up_out, middle_out, down_out, summed, canvas):
    total = terms_ref[0].astype(F32)
    for term in range(1, terms_ref.shape[0]):
        total = total + terms_ref[term].astype(F32)
    summed[...] = total
    near = lax.broadcasted_iota(jnp.int32, (8, LANES), 1) < LANES - SHIFT
    for first in range(0, half_rows, 8):
        count = min(8, half_rows - first)
        starts = [CHUNK * (first + row) for row in range(count)]
        tiles = swap_groups(jnp.stack([summed[start : start + 8, :] for start in starts], 0))
        edges = summed[pl.ds(starts[0] + 8, count, stride=CHUNK), :]
        if count < 8:
            edges = jnp.concatenate([edges, jnp.zeros((8 - count, LANES), F32)], axis=0)
        edges = swap_groups(edges.reshape(1, 8, LANES)).reshape(8, LANES)
        for row in range(count):
            tile = pltpu.roll(tiles[row], LANES - SHIFT, 1)
            edge = pltpu.roll(edges, (LANES - SHIFT - G * row) % LANES, 1)
            start = 8 * (first + row)
            canvas[start : start + 8, :] = jnp.where(near, tile, edge)
    middle = middle_out.shape[0]
    up_out[...] = canvas[:HALO, :].astype(BF16)
    middle_out[...] = canvas[HALO : HALO + middle, :]
    down_out[...] = canvas[HALO + middle : 2 * HALO + middle, :].astype(BF16)


def finish(terms, half_rows, rows):
    rim = jax.ShapeDtypeStruct((HALO, LANES), BF16)
    vmem = pl.BlockSpec(memory_space=pltpu.VMEM)
    return pl.pallas_call(
        lambda *refs: finish_kernel(half_rows, *refs),
        in_specs=[vmem],
        out_specs=[vmem, vmem, vmem],
        out_shape=[rim, jax.ShapeDtypeStruct((rows, LANES), F32), rim],
        scratch_shapes=[
            pltpu.VMEM((CHUNK_ROWS, LANES), F32),
            pltpu.VMEM((8 * half_rows, LANES), F32),
        ],
        cost_estimate=SMALL,
        name="finish",
    )(terms)


def rims_kernel(middle_ref, above_ref, below_ref, out_ref):
    rows = out_ref.shape[0]
    out_ref[...] = middle_ref[...]

    @pl.when(pl.program_id(0) == 0)
    def _():
        out_ref[:HALO, :] = out_ref[:HALO, :] + above_ref[...].astype(F32)

    @pl.when(pl.program_id(0) == 1)
    def _():
        out_ref[rows - HALO :, :] = out_ref[rows - HALO :, :] + below_ref[...].astype(F32)


def add_rims(middle, above, below):
    rows = 32
    last = middle.shape[0] // rows - 1
    block = pl.BlockSpec((rows, LANES), lambda i: (i * last, 0))
    return pl.pallas_call(
        rims_kernel,
        grid=(2,),
        in_specs=[block, whole_vmem(), whole_vmem()],
        out_specs=block,
        out_shape=jax.ShapeDtypeStruct(middle.shape, F32),
        input_output_aliases={0: 0},
        cost_estimate=SMALL,
        name="rims",
    )(middle, on_chip(above), on_chip(below))


def shards(sky_model, exposure_data, pixel_mask, block_owner, block_local, psf_cell, psf_table):
    sky_count = lax.axis_size("sky")
    stripe_rows, stripe_cols = sky_model.shape
    per_row = stripe_cols // B
    block_total = stripe_rows // B * per_row
    piece_count = exposure_data.shape[0]
    owner_sky = block_owner[:, 0]
    code = lax.broadcasted_iota(jnp.int32, (piece_count,), 0) * block_total + block_local
    mine = owner_sky[None, :] == lax.broadcasted_iota(jnp.int32, (sky_count, 1), 0)
    first = jnp.min(jnp.where(mine, code[None, :], piece_count * block_total), axis=1)
    last = jnp.max(jnp.where(mine, code[None, :], -1), axis=1)
    requests = jnp.stack(
        [
            jnp.where(last < 0, -1, first % block_total),
            jnp.where(last > first, last % block_total, -1),
        ],
        axis=1,
    )
    requests, sky_model = lax.optimization_barrier((requests, sky_model))
    asked = lax.all_to_all(requests, "sky", split_axis=0, concat_axis=0, tiled=True)
    asked = asked.reshape(sky_count * CAP)

    above = from_behind(sky_model[stripe_rows - HALO :], "sky", 1)
    below = from_behind(sky_model[:HALO], "sky", -1)
    half_rows = (stripe_rows + 2 * HALO + TAIL) // 8
    own = own_blocks(sky_model)
    asked, own = lax.optimization_barrier((asked, own))
    outgoing = cut_patches(asked, own, sky_model, above, below, half_rows)
    exposure_data, pixel_mask, psf_table, code, _ = lax.optimization_barrier(
        (exposure_data, pixel_mask, psf_table, code, outgoing)
    )
    second = jnp.any(mine & (first[:, None] < code[None, :]), axis=0)
    slot_index = owner_sky * CAP + second.astype(jnp.int32)
    patches = lax.all_to_all(outgoing, "sky", split_axis=0, concat_axis=0, tiled=True)
    data = regroup(exposure_data, pixel_mask)
    taps = build_taps(psf_table)
    adjoints, residuals = pieces(slot_index, psf_cell, patches, taps, data)
    received = lax.all_to_all(adjoints, "sky", split_axis=0, concat_axis=0, tiled=True)
    received, residual = lax.optimization_barrier((received, ungroup(residuals)))

    partial = fold(asked, received, per_row, half_rows)
    terms = lax.all_to_all(partial, "exp", split_axis=0, concat_axis=0, tiled=True)
    up, middle, down = finish(terms, half_rows, stripe_rows)
    from_below = from_behind(up, "sky", -1)
    from_above = from_behind(down, "sky", 1)
    gradient = add_rims(middle, from_above, from_below)
    return (gradient, residual)


def solution(mesh):
    in_specs = (
        P("sky", None),
        P(("sky", "exp"), None, None),
        P(("sky", "exp"), None, None),
        P(("sky", "exp"), None),
        P(("sky", "exp")),
        P(("sky", "exp")),
        P("exp", None),
    )
    out_specs = (P("sky", "exp"), P(("sky", "exp"), None, None))
    return jax.shard_map(shards, mesh=mesh, in_specs=in_specs, out_specs=out_specs, check_vma=False)
```

```python
import jax
import jax.numpy as jnp
from jax import lax
from jax.experimental import pallas as pl
from jax.experimental.pallas import tpu as pltpu
from jax.sharding import PartitionSpec as P

B = 128
PSF = 41
HALO = 20
CAP = 2

G = 16
LANES = 128
OUT = B // G
EXT = 11
REACH = 4
TAIL = 8
BLOCKS = OUT * OUT
PATCH_ROWS = 240
SLOT_ROWS = 128
PITCH = 72
TILES = 6
RES_LEAD = 40
TAP_ROWS = 48
GROUP = 2
BATCH = 4
SLOTS = 8
CHUNK = 9
CHUNK_ROWS = 352
SHIFT = 4
UNKNOWN = 2.0**100
SMALL = pl.CostEstimate(flops=1000, bytes_accessed=1000, transcendentals=0)
F32 = jnp.float32
BF16 = jnp.bfloat16


def whole_vmem():
    return pl.BlockSpec(memory_space=pltpu.VMEM)


def on_chip(x):
    return pltpu.with_memory_space_constraint(x, pltpu.VMEM)


def from_behind(x, axis, by):
    devices = lax.axis_size(axis)
    pairs = [(i, i + by) for i in range(devices) if 0 <= i + by < devices]
    return lax.ppermute(x, axis, pairs)


def swap_groups(x):
    sub = lax.broadcasted_iota(jnp.int32, x.shape, 1)
    group = lax.broadcasted_iota(jnp.int32, x.shape, 2) // G
    for d in (4, 2, 1):
        sub_bit, group_bit = (sub & d) != 0, (group & d) != 0
        up = pltpu.roll(pltpu.roll(x, 8 - d, 1), G * d, 2)
        down = up if d == 4 else pltpu.roll(pltpu.roll(x, d, 1), LANES - G * d, 2)
        x = jnp.where(sub_bit == group_bit, x, jnp.where(group_bit, up, down))
    return x


def reversed_groups(shift=0):
    source = lax.broadcasted_iota(jnp.int32, (2 * LANES, LANES), 0)
    lane = lax.broadcasted_iota(jnp.int32, (2 * LANES, LANES), 1)
    group = (8 - lane // G) % 8
    return (source == LANES - shift + group * G + lane % G).astype(BF16)


def swap_reversed(x):
    group = lax.broadcasted_iota(jnp.int32, (8, LANES), 1) // G
    tiles = []
    for tile in range(x.shape[0]):
        now = pltpu.roll(x[tile], 0, 1, stride=G, stride_axis=0)
        for d in (1, 2, 4):
            now = jnp.where((group & d) != 0, pltpu.roll(now, 8 - d, 0), now)
        tiles.append(pltpu.roll(now, 0, 1, stride=G, stride_axis=0))
    return jnp.stack(tiles, 0)


def regroup_kernel(data_ref, keep_ref, out_ref):
    def per_piece(p, carry):
        known = jnp.where(keep_ref[p] != 0, data_ref[p].astype(F32), UNKNOWN).astype(BF16)
        turned = jnp.dot(known, reversed_groups()[LANES:], preferred_element_type=F32)
        blocks = swap_reversed(turned.reshape(2 * OUT, 8, LANES)).reshape(OUT, 2, 8, LANES)
        for half in range(2):
            out_ref[p, :, half * LANES : (half + 1) * LANES] = (
                blocks[:, half].reshape(BLOCKS, LANES).astype(BF16)
            )
        return carry

    lax.fori_loop(0, data_ref.shape[0], per_piece, 0)


def regroup(exposure_data, pixel_mask):
    pieces = exposure_data.shape[0]
    block = pl.BlockSpec((BATCH, B, B), lambda p: (p, 0, 0))
    return pl.pallas_call(
        regroup_kernel,
        grid=(pieces // BATCH,),
        in_specs=[block, block],
        out_specs=pl.BlockSpec((BATCH, BLOCKS, 2 * LANES), lambda p: (p, 0, 0)),
        out_shape=jax.ShapeDtypeStruct((pieces, BLOCKS, 2 * LANES), BF16),
        cost_estimate=SMALL,
        name="regroup",
    )(exposure_data, pixel_mask)


def taps_kernel(kernel_ref, out_ref, windows, rows):
    lane = lax.broadcasted_iota(jnp.int32, (G, LANES), 1)
    odd = (lane // G) % 2 == 1
    wide = lax.broadcasted_iota(jnp.int32, (TAP_ROWS, LANES), 1) // (2 * G)
    quarter = lax.broadcasted_iota(jnp.int32, (TILES, LANES), 1) // (2 * G)

    kernel = kernel_ref[0].astype(F32)
    spread = pltpu.roll(kernel, G, 1)
    for t in range(1, REACH):
        spread = jnp.where(wide == t, pltpu.roll(kernel, G * t + G, 1), spread)
    windows[...] = spread
    for parity in range(2):
        picked = [windows[pl.ds(parity + 2 * q, TILES, stride=8), :] for q in range(4)]
        for t in range(REACH):
            row = picked[0] if t == 0 else pltpu.roll(picked[0], 2 * G * (4 - t), 1)
            for q in range(1, 4):
                by = (q - t) % 4
                part = picked[q] if by == 0 else pltpu.roll(picked[q], 2 * G * by, 1)
                row = jnp.where(quarter == q, part, row)
            rows[t, parity, :TILES, :] = row

    def per_shift(t, carry):
        before = [jnp.zeros((G, LANES), F32)] * 8
        for tile in range(TILES):
            even_row, odd_row = (
                jnp.broadcast_to(rows[t, parity, tile : tile + 1, :], (G, LANES))
                for parity in range(2)
            )
            even_row = pltpu.roll(even_row, LANES - G, 1, stride=1, stride_axis=0)
            odd_row = pltpu.roll(odd_row, 0, 1, stride=1, stride_axis=0)
            now = jnp.where(odd, odd_row, even_row)
            turns = [now] + [pltpu.roll(now, G * phase, 1) for phase in range(1, 8)]
            for phase in range(8):
                part = turns[phase]
                if phase > 0:
                    part = jnp.where(lane < G * phase, before[phase], part)
                start = pl.multiple_of(t * LANES + phase * G, G)
                lanes = slice(tile * LANES, (tile + 1) * LANES)
                out_ref[0, pl.ds(start, G), lanes] = part.astype(BF16)
            before = turns
        return carry

    lax.fori_loop(0, REACH, per_shift, 0)


def build_taps(table):
    cells = table.shape[0]
    kernels = jnp.pad(
        table.reshape(cells, PSF, PSF), ((0, 0), (0, TAP_ROWS - PSF), (0, LANES - PSF))
    )
    return pl.pallas_call(
        taps_kernel,
        grid=(cells,),
        in_specs=[pl.BlockSpec((1, TAP_ROWS, LANES), lambda c: (c, 0, 0))],
        out_specs=pl.BlockSpec((1, REACH * LANES, TILES * LANES), lambda c: (c, 0, 0)),
        out_shape=jax.ShapeDtypeStruct((cells, REACH * LANES, TILES * LANES), BF16),
        scratch_shapes=[
            pltpu.VMEM((TAP_ROWS, LANES), F32),
            pltpu.VMEM((REACH, 2, 8, LANES), F32),
        ],
        cost_estimate=SMALL,
        name="taps",
    )(kernels)


def moved_tiles(pixels):
    rows, columns = pixels.shape
    turn = reversed_groups(HALO)
    empty = jnp.zeros((rows, LANES), BF16)
    tiles = [pixels[:, at : at + LANES] for at in range(0, columns, LANES)]
    return [
        jnp.dot(jnp.concatenate([old, now], axis=1), turn, preferred_element_type=F32)
        for old, now in zip([empty] + tiles, tiles + [empty])
    ]


def blocks_kernel(stripe_ref, above_ref, below_ref, out_ref, pixels):
    first = 0
    for ref in (above_ref, stripe_ref, below_ref):
        rows = ref.shape[0]
        for tile, moved in enumerate(moved_tiles(ref[...])):
            pixels[first : first + rows, tile * LANES : (tile + 1) * LANES] = moved
        first += rows
    pixels[first:, :] = jnp.zeros((TAIL, PITCH * G), F32)
    for row in range(out_ref.shape[0]):
        tiles = [
            pixels[8 * row : 8 * row + 8, at : at + LANES] for at in range(0, PITCH * G, LANES)
        ]
        out_ref[row] = swap_reversed(jnp.stack(tiles, 0)).reshape(PITCH, LANES)


def stripe_blocks(stripe, above, below, half_rows):
    return pl.pallas_call(
        blocks_kernel,
        in_specs=[whole_vmem(), whole_vmem(), whole_vmem()],
        out_specs=whole_vmem(),
        out_shape=pltpu.VMEM((half_rows, PITCH, LANES), F32),
        scratch_shapes=[pltpu.VMEM((8 * half_rows, PITCH * G), F32)],
        cost_estimate=SMALL,
        name="blocks",
    )(stripe, on_chip(above), on_chip(below))


def cut_kernel(per_row, ids_ref, blocks_ref, out_ref, scratch):
    step = pl.program_id(0)

    def per_slot(n, carry):
        at = step * SLOTS + n
        wanted = ids_ref[at // CAP, 0, at % CAP]

        @pl.when(wanted >= 0)
        def _():
            first_row = wanted // per_row * (2 * OUT)
            first_col = pl.multiple_of(wanted % per_row * OUT, 8)
            for row in range(2 * EXT - 1):
                part = blocks_ref[first_row + row, pl.ds(first_col, G), :]
                scratch[EXT * row : EXT * row + G, :] = part
            out_ref[n] = scratch[...].astype(BF16)

        return carry

    lax.fori_loop(0, SLOTS, per_slot, 0)


def cut_patches(ids, blocks, per_row):
    slots = ids.shape[0] * CAP
    return pl.pallas_call(
        lambda *refs: cut_kernel(per_row, *refs),
        grid_spec=pltpu.PrefetchScalarGridSpec(
            num_scalar_prefetch=1,
            grid=(slots // SLOTS,),
            in_specs=[whole_vmem()],
            out_specs=pl.BlockSpec((SLOTS, PATCH_ROWS, LANES), lambda n, ids: (n, 0, 0)),
            scratch_shapes=[pltpu.VMEM((PATCH_ROWS, LANES), F32)],
        ),
        out_shape=jax.ShapeDtypeStruct((slots, PATCH_ROWS, LANES), BF16),
        cost_estimate=SMALL,
        name="cut",
    )(ids, on_chip(blocks))


def block_taps(taps_ref, s, t):
    taps = slice(t * LANES, (t + 1) * LANES)
    upper = taps_ref[0, taps, 2 * s * LANES : (2 * s + 2) * LANES]
    if s == 0:
        lower = jnp.concatenate(
            [jnp.zeros((LANES, LANES), BF16), taps_ref[0, taps, 0:LANES]], axis=1
        )
    else:
        lower = taps_ref[0, taps, (2 * s - 1) * LANES : (2 * s + 1) * LANES]
    return jnp.concatenate([upper, lower], axis=0)


def last_taps(taps_ref, t):
    return taps_ref[0, t * LANES : (t + 1) * LANES, (TILES - 1) * LANES :]


def correlate(read, taps_ref):
    across = (((1,), (1,)), ((), ()))
    total = jnp.zeros((2 * BLOCKS, LANES), F32)
    for t in range(REACH):
        for d in range(TILES // 2):
            taps = taps_ref[0, t * LANES : (t + 1) * LANES, 2 * d * LANES : (2 * d + 2) * LANES]
            total = total + lax.dot_general(
                read(d, t), taps, across, preferred_element_type=F32
            )
    return jnp.concatenate([total[:BLOCKS], total[BLOCKS:]], axis=1)


def convolve(read, taps_ref, rows):
    total = jnp.zeros((rows, 2 * LANES), F32)
    for t in range(REACH):
        for s in range(REACH - 1):
            total = total + jnp.dot(
                read(s, t), block_taps(taps_ref, s, t), preferred_element_type=F32
            )
    last = jnp.zeros((rows, LANES), F32)
    for t in range(0, REACH, 2):
        field = [read(REACH - 1, t + i)[:, LANES:] for i in range(2)]
        taps = [last_taps(taps_ref, t + i) for i in range(2)]
        last = last + jnp.dot(
            jnp.concatenate(field, axis=1),
            jnp.concatenate(taps, axis=0),
            preferred_element_type=F32,
        )
    return jnp.concatenate([total[:, :LANES] + last, total[:, LANES:]], axis=1)


def pieces_kernel(slot_ref, cell_ref, patch_ref, *refs):
    taps, refs = refs[:GROUP], refs[GROUP:]
    data_ref, adjoints, res_out, field, resid, adj_slots, sems = refs
    step = pl.program_id(0)
    slots = lax.rem(step, 2)

    @pl.when(step == 0)
    def _():
        resid[...] = jnp.zeros_like(resid)

    def sent(step):
        at = lax.rem(step, 2)
        return [
            pltpu.make_async_copy(
                adj_slots.at[at, i], adjoints.at[slot_ref[GROUP * step + i]], sems.at[at, i]
            )
            for i in range(GROUP)
        ]

    @pl.when(step >= 2)
    def _():
        for copy in sent(step - 2):
            copy.wait()

    def per_piece(i, taps_ref, field, resid):
        field[...] = patch_ref[slot_ref[GROUP * step + i]].astype(F32)

        def read_patch(d, t):
            parts = []
            for half in range(2):
                for row in range(OUT):
                    at = EXT * (2 * (row + d) + half) + t
                    pair = [field[at : at + OUT, :], field[at + EXT : at + EXT + OUT, :]]
                    parts.append(jnp.concatenate(pair, axis=1))
            return jnp.concatenate(parts, axis=0).astype(BF16)

        predicted = correlate(read_patch, taps_ref)
        observed = data_ref[i].astype(F32)
        residual = jnp.where(observed < UNKNOWN, predicted - observed, 0.0).astype(BF16)
        res_out[i] = residual
        wide = residual.astype(F32)
        for row in range(OUT):
            first = RES_LEAD + EXT * row
            resid[first : first + OUT, :] = wide[OUT * row : OUT * (row + 1)]

        def read_residual(s, t):
            return resid[pl.ds(RES_LEAD - EXT * s - t, SLOT_ROWS), :].astype(BF16)

        adj_slots[slots, i] = convolve(read_residual, taps_ref, SLOT_ROWS).astype(BF16)

    for i in range(GROUP):
        per_piece(i, taps[i], field.at[i], resid.at[i])
    for copy in sent(step):
        copy.start()

    @pl.when(step == pl.num_programs(0) - 1)
    def _():
        for copy in sent(step - 1) + sent(step):
            copy.wait()


def pieces(slots, cells, patches, taps, data):
    count = data.shape[0]
    cell = [
        pl.BlockSpec(
            (1, REACH * LANES, TILES * LANES),
            lambda p, slots, cells, i=i: (cells[GROUP * p + i], 0, 0),
        )
        for i in range(GROUP)
    ]
    block = pl.BlockSpec((GROUP, BLOCKS, 2 * LANES), lambda p, slots, cells: (p, 0, 0))
    return pl.pallas_call(
        pieces_kernel,
        grid_spec=pltpu.PrefetchScalarGridSpec(
            num_scalar_prefetch=2,
            grid=(count // GROUP,),
            in_specs=[whole_vmem(), *cell, block],
            out_specs=[pl.BlockSpec(memory_space=pltpu.HBM), block],
            scratch_shapes=[
                pltpu.VMEM((GROUP, PATCH_ROWS, LANES), F32),
                pltpu.VMEM((GROUP, RES_LEAD + SLOT_ROWS, 2 * LANES), F32),
                pltpu.VMEM((2, GROUP, SLOT_ROWS, 2 * LANES), BF16),
                pltpu.SemaphoreType.DMA((2, GROUP)),
            ],
        ),
        out_shape=[
            jax.ShapeDtypeStruct((patches.shape[0], SLOT_ROWS, 2 * LANES), BF16),
            jax.ShapeDtypeStruct(data.shape, BF16),
        ],
        cost_estimate=SMALL,
        name="pieces",
    )(slots, cells, on_chip(patches), *[taps] * GROUP, data)


def ungroup_kernel(res_ref, out_ref):
    turn = reversed_groups()[LANES:]

    def per_piece(p, carry):
        halves = [
            jnp.dot(
                res_ref[p, :, half * LANES : (half + 1) * LANES], turn, preferred_element_type=F32
            ).reshape(OUT, 8, LANES)
            for half in range(2)
        ]
        pixels = swap_reversed(jnp.stack(halves, 1).reshape(2 * OUT, 8, LANES))
        out_ref[p] = pixels.reshape(B, LANES).astype(BF16)
        return carry

    lax.fori_loop(0, res_ref.shape[0], per_piece, 0)


def ungroup(residual):
    count = residual.shape[0]
    return pl.pallas_call(
        ungroup_kernel,
        grid=(count // BATCH,),
        in_specs=[pl.BlockSpec((BATCH, BLOCKS, 2 * LANES), lambda p: (p, 0, 0))],
        out_specs=pl.BlockSpec((BATCH, B, B), lambda p: (p, 0, 0)),
        out_shape=jax.ShapeDtypeStruct((count, B, B), BF16),
        cost_estimate=SMALL,
        name="ungroup",
    )(residual)


def fold_kernel(per_row, half_rows, ids_ref, slot_ref, out_ref, canvas, scratch, packed):
    canvas[...] = jnp.zeros_like(canvas)
    inside = lax.broadcasted_iota(jnp.int32, (G, LANES), 0) < EXT

    def per_slot(n, carry):
        named = ids_ref[n // CAP, 0, n % CAP]

        @pl.when(named >= 0)
        def _():
            first_row = named // per_row * (2 * OUT)
            first_col = pl.multiple_of(named % per_row * OUT, 8)
            scratch[...] = slot_ref[n].astype(F32)
            for row in range(EXT):
                for half in range(2):
                    part = scratch[pl.ds(EXT * row, G), half * LANES : (half + 1) * LANES]
                    part = jnp.where(inside, part, 0.0)
                    at = (first_row + 2 * row + half, pl.ds(first_col, G), slice(None))
                    canvas[at] = canvas[at] + part

        return carry

    lax.fori_loop(0, slot_ref.shape[0], per_slot, 0)
    for chunk in range(per_row):
        first = OUT * chunk + 1
        for row in range(half_rows):
            packed[CHUNK * row : CHUNK * row + G, :] = canvas[row, first : first + G, :]
        out_ref[chunk] = packed[...].astype(BF16)


def fold(ids, received, per_row, half_rows):
    return pl.pallas_call(
        lambda *refs: fold_kernel(per_row, half_rows, *refs),
        in_specs=[
            pl.BlockSpec(memory_space=pltpu.SMEM),
            pl.BlockSpec(memory_space=pltpu.VMEM),
        ],
        out_specs=pl.BlockSpec(memory_space=pltpu.VMEM),
        scratch_shapes=[
            pltpu.VMEM((half_rows, PITCH + 8, LANES), F32),
            pltpu.VMEM((SLOT_ROWS, 2 * LANES), F32),
            pltpu.VMEM((CHUNK_ROWS, LANES), F32),
        ],
        out_shape=jax.ShapeDtypeStruct((per_row, CHUNK_ROWS, LANES), BF16),
        cost_estimate=SMALL,
        name="fold",
    )(ids, on_chip(received))


def finish_kernel(half_rows, terms_ref, up_out, middle_out, down_out, summed, canvas):
    total = terms_ref[0].astype(F32)
    for term in range(1, terms_ref.shape[0]):
        total = total + terms_ref[term].astype(F32)
    summed[...] = total
    near = lax.broadcasted_iota(jnp.int32, (8, LANES), 1) < LANES - SHIFT
    for first in range(0, half_rows, 8):
        count = min(8, half_rows - first)
        starts = [CHUNK * (first + row) for row in range(count)]
        tiles = swap_groups(jnp.stack([summed[start : start + 8, :] for start in starts], 0))
        edges = summed[pl.ds(starts[0] + 8, count, stride=CHUNK), :]
        if count < 8:
            edges = jnp.concatenate([edges, jnp.zeros((8 - count, LANES), F32)], axis=0)
        edges = swap_groups(edges.reshape(1, 8, LANES)).reshape(8, LANES)
        for row in range(count):
            tile = pltpu.roll(tiles[row], LANES - SHIFT, 1)
            edge = pltpu.roll(edges, (LANES - SHIFT - G * row) % LANES, 1)
            start = 8 * (first + row)
            canvas[start : start + 8, :] = jnp.where(near, tile, edge)
    middle = middle_out.shape[0]
    up_out[...] = canvas[:HALO, :].astype(BF16)
    middle_out[...] = canvas[HALO : HALO + middle, :]
    down_out[...] = canvas[HALO + middle : 2 * HALO + middle, :].astype(BF16)


def finish(terms, half_rows, rows):
    rim = jax.ShapeDtypeStruct((HALO, LANES), BF16)
    vmem = pl.BlockSpec(memory_space=pltpu.VMEM)
    return pl.pallas_call(
        lambda *refs: finish_kernel(half_rows, *refs),
        in_specs=[vmem],
        out_specs=[vmem, vmem, vmem],
        out_shape=[rim, jax.ShapeDtypeStruct((rows, LANES), F32), rim],
        scratch_shapes=[
            pltpu.VMEM((CHUNK_ROWS, LANES), F32),
            pltpu.VMEM((8 * half_rows, LANES), F32),
        ],
        cost_estimate=SMALL,
        name="finish",
    )(terms)


def rims_kernel(middle_ref, above_ref, below_ref, out_ref):
    rows = out_ref.shape[0]
    out_ref[...] = middle_ref[...]

    @pl.when(pl.program_id(0) == 0)
    def _():
        out_ref[:HALO, :] = out_ref[:HALO, :] + above_ref[...].astype(F32)

    @pl.when(pl.program_id(0) == 1)
    def _():
        out_ref[rows - HALO :, :] = out_ref[rows - HALO :, :] + below_ref[...].astype(F32)


def add_rims(middle, above, below):
    rows = 32
    last = middle.shape[0] // rows - 1
    block = pl.BlockSpec((rows, LANES), lambda i: (i * last, 0))
    return pl.pallas_call(
        rims_kernel,
        grid=(2,),
        in_specs=[block, whole_vmem(), whole_vmem()],
        out_specs=block,
        out_shape=jax.ShapeDtypeStruct(middle.shape, F32),
        input_output_aliases={0: 0},
        cost_estimate=SMALL,
        name="rims",
    )(middle, on_chip(above), on_chip(below))


def shards(sky_model, exposure_data, pixel_mask, block_owner, block_local, psf_cell, psf_table):
    sky_count = lax.axis_size("sky")
    stripe_rows, stripe_cols = sky_model.shape
    per_row = stripe_cols // B
    block_total = stripe_rows // B * per_row
    piece_count = exposure_data.shape[0]
    owner_sky = block_owner[:, 0]
    code = lax.broadcasted_iota(jnp.int32, (piece_count,), 0) * block_total + block_local
    mine = owner_sky[None, :] == lax.broadcasted_iota(jnp.int32, (sky_count, 1), 0)
    first = jnp.min(jnp.where(mine, code[None, :], piece_count * block_total), axis=1)
    last = jnp.max(jnp.where(mine, code[None, :], -1), axis=1)
    requests = jnp.stack(
        [
            jnp.where(last < 0, -1, first % block_total),
            jnp.where(last > first, last % block_total, -1),
        ],
        axis=1,
    )
    asked = lax.all_to_all(
        requests[:, None, :], "sky", split_axis=0, concat_axis=0, tiled=True
    )
    above = from_behind(sky_model[stripe_rows - HALO :], "sky", 1)
    below = from_behind(sky_model[:HALO], "sky", -1)
    half_rows = (stripe_rows + 2 * HALO + TAIL) // 8
    second = jnp.any(mine & (first[:, None] < code[None, :]), axis=0)
    slot_index = owner_sky * CAP + second.astype(jnp.int32)
    asked, above, below, slot_index = lax.optimization_barrier((asked, above, below, slot_index))
    blocks = stripe_blocks(sky_model, above, below, half_rows)
    outgoing = cut_patches(asked, blocks, per_row)
    exposure_data, pixel_mask, psf_table, _ = lax.optimization_barrier(
        (exposure_data, pixel_mask, psf_table, outgoing)
    )
    patches = lax.all_to_all(outgoing, "sky", split_axis=0, concat_axis=0, tiled=True)
    data = regroup(exposure_data, pixel_mask)
    taps = build_taps(psf_table)
    adjoints, residuals = pieces(slot_index, psf_cell, patches, taps, data)
    received = lax.all_to_all(adjoints, "sky", split_axis=0, concat_axis=0, tiled=True)
    received, residual = lax.optimization_barrier((received, ungroup(residuals)))

    partial = fold(asked, received, per_row, half_rows)
    terms = lax.all_to_all(partial, "exp", split_axis=0, concat_axis=0, tiled=True)
    up, middle, down = finish(terms, half_rows, stripe_rows)
    from_below = from_behind(up, "sky", -1)
    from_above = from_behind(down, "sky", 1)
    gradient = add_rims(middle, from_above, from_below)
    return (gradient, residual)


def solution(mesh):
    in_specs = (
        P("sky", None),
        P(("sky", "exp"), None, None),
        P(("sky", "exp"), None, None),
        P(("sky", "exp"), None),
        P(("sky", "exp")),
        P(("sky", "exp")),
        P("exp", None),
    )
    out_specs = (P("sky", "exp"), P(("sky", "exp"), None, None))
    return jax.shard_map(shards, mesh=mesh, in_specs=in_specs, out_specs=out_specs, check_vma=False)
```

```python
import jax
import jax.numpy as jnp
from jax import lax
from jax.experimental import pallas as pl
from jax.experimental.pallas import tpu as pltpu
from jax.sharding import PartitionSpec as P

B = 128
PSF = 41
HALO = 20
CAP = 2

G = 16
LANES = 128
OUT = B // G
EXT = 11
REACH = 4
TAIL = 8
BLOCKS = OUT * OUT
PATCH_ROWS = 232
ADJ_ROWS = 240
SLOT_ROWS = 128
PITCH = 72
TILES = 6
RES_LEAD = 40
TAP_ROWS = 48
GROUP = 2
BATCH = 4
SLOTS = 8
CHUNK = 9
CHUNK_ROWS = 352
SHIFT = 4
UNKNOWN = 2.0**100
SMALL = pl.CostEstimate(flops=1000, bytes_accessed=1000, transcendentals=0)
F32 = jnp.float32
BF16 = jnp.bfloat16


def whole_vmem():
    return pl.BlockSpec(memory_space=pltpu.VMEM)


def on_chip(x):
    return pltpu.with_memory_space_constraint(x, pltpu.VMEM)


def from_behind(x, axis, by):
    devices = lax.axis_size(axis)
    pairs = [(i, i + by) for i in range(devices) if 0 <= i + by < devices]
    return lax.ppermute(x, axis, pairs)


def swap_groups(x):
    sub = lax.broadcasted_iota(jnp.int32, x.shape, 1)
    group = lax.broadcasted_iota(jnp.int32, x.shape, 2) // G
    for d in (4, 2, 1):
        sub_bit, group_bit = (sub & d) != 0, (group & d) != 0
        up = pltpu.roll(pltpu.roll(x, 8 - d, 1), G * d, 2)
        down = up if d == 4 else pltpu.roll(pltpu.roll(x, d, 1), LANES - G * d, 2)
        x = jnp.where(sub_bit == group_bit, x, jnp.where(group_bit, up, down))
    return x


def reversed_groups(shift=0):
    source = lax.broadcasted_iota(jnp.int32, (2 * LANES, LANES), 0)
    lane = lax.broadcasted_iota(jnp.int32, (2 * LANES, LANES), 1)
    group = (8 - lane // G) % 8
    return (source == LANES - shift + group * G + lane % G).astype(BF16)


def swap_reversed(x):
    group = lax.broadcasted_iota(jnp.int32, (8, LANES), 1) // G
    tiles = []
    for tile in range(x.shape[0]):
        now = pltpu.roll(x[tile], 0, 1, stride=G, stride_axis=0)
        for d in (1, 2, 4):
            now = jnp.where((group & d) != 0, pltpu.roll(now, 8 - d, 0), now)
        tiles.append(pltpu.roll(now, 0, 1, stride=G, stride_axis=0))
    return jnp.stack(tiles, 0)


def regroup_kernel(data_ref, keep_ref, out_ref):
    def per_piece(p, carry):
        known = jnp.where(keep_ref[p] != 0, data_ref[p].astype(F32), UNKNOWN).astype(BF16)
        turned = jnp.dot(known, reversed_groups()[LANES:], preferred_element_type=F32)
        blocks = swap_reversed(turned.reshape(2 * OUT, 8, LANES)).reshape(OUT, 2, 8, LANES)
        for half in range(2):
            out_ref[p, :, half * LANES : (half + 1) * LANES] = (
                blocks[:, half].reshape(BLOCKS, LANES).astype(BF16)
            )
        return carry

    lax.fori_loop(0, data_ref.shape[0], per_piece, 0)


def regroup(exposure_data, pixel_mask):
    pieces = exposure_data.shape[0]
    block = pl.BlockSpec((BATCH, B, B), lambda p: (p, 0, 0))
    return pl.pallas_call(
        regroup_kernel,
        grid=(pieces // BATCH,),
        in_specs=[block, block],
        out_specs=pl.BlockSpec((BATCH, BLOCKS, 2 * LANES), lambda p: (p, 0, 0)),
        out_shape=jax.ShapeDtypeStruct((pieces, BLOCKS, 2 * LANES), BF16),
        cost_estimate=SMALL,
        name="regroup",
    )(exposure_data, pixel_mask)


def taps_kernel(kernel_ref, out_ref, windows, rows):
    lane = lax.broadcasted_iota(jnp.int32, (G, LANES), 1)
    odd = (lane // G) % 2 == 1
    wide = lax.broadcasted_iota(jnp.int32, (TAP_ROWS, LANES), 1) // (2 * G)
    quarter = lax.broadcasted_iota(jnp.int32, (TILES, LANES), 1) // (2 * G)

    kernel = kernel_ref[0].astype(F32)
    spread = pltpu.roll(kernel, G, 1)
    for t in range(1, REACH):
        spread = jnp.where(wide == t, pltpu.roll(kernel, G * t + G, 1), spread)
    windows[...] = spread
    for parity in range(2):
        picked = [windows[pl.ds(parity + 2 * q, TILES, stride=8), :] for q in range(4)]
        for t in range(REACH):
            row = picked[0] if t == 0 else pltpu.roll(picked[0], 2 * G * (4 - t), 1)
            for q in range(1, 4):
                by = (q - t) % 4
                part = picked[q] if by == 0 else pltpu.roll(picked[q], 2 * G * by, 1)
                row = jnp.where(quarter == q, part, row)
            rows[t, parity, :TILES, :] = row

    def per_shift(t, carry):
        before = [jnp.zeros((G, LANES), F32)] * 8
        for tile in range(TILES):
            even_row, odd_row = (
                jnp.broadcast_to(rows[t, parity, tile : tile + 1, :], (G, LANES))
                for parity in range(2)
            )
            even_row = pltpu.roll(even_row, LANES - G, 1, stride=1, stride_axis=0)
            odd_row = pltpu.roll(odd_row, 0, 1, stride=1, stride_axis=0)
            now = jnp.where(odd, odd_row, even_row)
            turns = [now] + [pltpu.roll(now, G * phase, 1) for phase in range(1, 8)]
            for phase in range(8):
                part = turns[phase]
                if phase > 0:
                    part = jnp.where(lane < G * phase, before[phase], part)
                start = pl.multiple_of(t * LANES + phase * G, G)
                lanes = slice(tile * LANES, (tile + 1) * LANES)
                out_ref[0, pl.ds(start, G), lanes] = part.astype(BF16)
            before = turns
        return carry

    lax.fori_loop(0, REACH, per_shift, 0)


def padded_kernels(table):
    kernels = table.reshape(table.shape[0], PSF, PSF)
    return jnp.pad(kernels, ((0, 0), (0, TAP_ROWS - PSF), (0, LANES - PSF)))


def build_taps(kernels):
    cells = kernels.shape[0]
    return pl.pallas_call(
        taps_kernel,
        grid=(cells,),
        in_specs=[pl.BlockSpec((1, TAP_ROWS, LANES), lambda c: (c, 0, 0))],
        out_specs=pl.BlockSpec((1, REACH * LANES, TILES * LANES), lambda c: (c, 0, 0)),
        out_shape=jax.ShapeDtypeStruct((cells, REACH * LANES, TILES * LANES), BF16),
        scratch_shapes=[
            pltpu.VMEM((TAP_ROWS, LANES), F32),
            pltpu.VMEM((REACH, 2, 8, LANES), F32),
        ],
        cost_estimate=SMALL,
        name="taps",
    )(kernels)


def moved_tiles(pixels):
    rows, columns = pixels.shape
    turn = reversed_groups(HALO)
    empty = jnp.zeros((rows, LANES), BF16)
    tiles = [pixels[:, at : at + LANES] for at in range(0, columns, LANES)]
    return [
        jnp.dot(jnp.concatenate([old, now], axis=1), turn, preferred_element_type=F32)
        for old, now in zip([empty] + tiles, tiles + [empty])
    ]


def blocks_kernel(stripe_ref, above_ref, below_ref, out_ref, pixels):
    first = 0
    for ref in (above_ref, stripe_ref, below_ref):
        rows = ref.shape[0]
        for tile, moved in enumerate(moved_tiles(ref[...])):
            pixels[first : first + rows, tile * LANES : (tile + 1) * LANES] = moved
        first += rows
    pixels[first:, :] = jnp.zeros((TAIL, PITCH * G), F32)
    for row in range(out_ref.shape[0]):
        tiles = [
            pixels[8 * row : 8 * row + 8, at : at + LANES] for at in range(0, PITCH * G, LANES)
        ]
        out_ref[row] = swap_reversed(jnp.stack(tiles, 0)).reshape(PITCH, LANES)


def stripe_blocks(stripe, above, below, half_rows):
    return pl.pallas_call(
        blocks_kernel,
        in_specs=[whole_vmem(), whole_vmem(), whole_vmem()],
        out_specs=whole_vmem(),
        out_shape=pltpu.VMEM((half_rows, PITCH, LANES), F32),
        scratch_shapes=[pltpu.VMEM((8 * half_rows, PITCH * G), F32)],
        cost_estimate=SMALL,
        name="blocks",
    )(stripe, on_chip(above), on_chip(below))


def cut_kernel(per_row, ids_ref, blocks_ref, out_ref, scratch):
    step = pl.program_id(0)

    def per_slot(n, carry):
        at = step * SLOTS + n
        wanted = ids_ref[at // CAP, 0, at % CAP]

        @pl.when(wanted >= 0)
        def _():
            first_row = wanted // per_row * (2 * OUT)
            first_col = pl.multiple_of(wanted % per_row * OUT, 8)
            for row in range(2 * EXT - 1):
                part = blocks_ref[first_row + row, pl.ds(first_col, G), :]
                scratch[EXT * row : EXT * row + G, :] = part
            out_ref[n] = scratch[:PATCH_ROWS, :].astype(BF16)

        return carry

    lax.fori_loop(0, SLOTS, per_slot, 0)


def cut_patches(ids, blocks, per_row):
    slots = ids.shape[0] * CAP
    return pl.pallas_call(
        lambda *refs: cut_kernel(per_row, *refs),
        grid_spec=pltpu.PrefetchScalarGridSpec(
            num_scalar_prefetch=1,
            grid=(slots // SLOTS,),
            in_specs=[whole_vmem()],
            out_specs=pl.BlockSpec((SLOTS, PATCH_ROWS, LANES), lambda n, ids: (n, 0, 0)),
            scratch_shapes=[pltpu.VMEM((PATCH_ROWS + 8, LANES), F32)],
        ),
        out_shape=jax.ShapeDtypeStruct((slots, PATCH_ROWS, LANES), BF16),
        cost_estimate=SMALL,
        name="cut",
    )(ids, on_chip(blocks))


def block_taps(taps_ref, s, t):
    taps = slice(t * LANES, (t + 1) * LANES)
    upper = taps_ref[0, taps, 2 * s * LANES : (2 * s + 2) * LANES]
    if s == 0:
        lower = jnp.concatenate(
            [jnp.zeros((LANES, LANES), BF16), taps_ref[0, taps, 0:LANES]], axis=1
        )
    else:
        lower = taps_ref[0, taps, (2 * s - 1) * LANES : (2 * s + 1) * LANES]
    return jnp.concatenate([upper, lower], axis=0)


def last_taps(taps_ref, t):
    return taps_ref[0, t * LANES : (t + 1) * LANES, (TILES - 1) * LANES :]


def correlate(read, taps_ref):
    across = (((1,), (1,)), ((), ()))
    total = jnp.zeros((2 * BLOCKS, LANES), F32)
    for t in range(REACH):
        for d in range(TILES // 2):
            taps = taps_ref[0, t * LANES : (t + 1) * LANES, 2 * d * LANES : (2 * d + 2) * LANES]
            total = total + lax.dot_general(
                read(d, t), taps, across, preferred_element_type=F32
            )
    return jnp.concatenate([total[:BLOCKS], total[BLOCKS:]], axis=1)


def convolve(read, taps_ref, rows):
    total = jnp.zeros((rows, 2 * LANES), F32)
    for t in range(REACH):
        for s in range(REACH - 1):
            total = total + jnp.dot(
                read(s, t), block_taps(taps_ref, s, t), preferred_element_type=F32
            )
    last = jnp.zeros((rows, LANES), F32)
    for t in range(0, REACH, 2):
        field = [read(REACH - 1, t + i)[:, LANES:] for i in range(2)]
        taps = [last_taps(taps_ref, t + i) for i in range(2)]
        last = last + jnp.dot(
            jnp.concatenate(field, axis=1),
            jnp.concatenate(taps, axis=0),
            preferred_element_type=F32,
        )
    return jnp.concatenate([total[:, :LANES] + last, total[:, LANES:]], axis=1)


def pieces_kernel(slot_ref, cell_ref, patch_ref, *refs):
    taps, refs = refs[:GROUP], refs[GROUP:]
    data_ref, adjoints, res_out, field, resid, adj_slots, sems = refs
    step = pl.program_id(0)
    slots = lax.rem(step, 2)

    @pl.when(step == 0)
    def _():
        resid[...] = jnp.zeros_like(resid)

    def sent(step):
        at = lax.rem(step, 2)
        return [
            pltpu.make_async_copy(
                adj_slots.at[at, i], adjoints.at[slot_ref[GROUP * step + i]], sems.at[at, i]
            )
            for i in range(GROUP)
        ]

    @pl.when(step >= 2)
    def _():
        for copy in sent(step - 2):
            copy.wait()

    def per_piece(i, taps_ref, field, resid):
        field[...] = patch_ref[slot_ref[GROUP * step + i]].astype(F32)

        def read_patch(d, t):
            parts = []
            for half in range(2):
                for row in range(OUT):
                    at = EXT * (2 * (row + d) + half) + t
                    pair = [field[at : at + OUT, :], field[at + EXT : at + EXT + OUT, :]]
                    parts.append(jnp.concatenate(pair, axis=1))
            return jnp.concatenate(parts, axis=0).astype(BF16)

        predicted = correlate(read_patch, taps_ref)
        observed = data_ref[i].astype(F32)
        residual = jnp.where(observed < UNKNOWN, predicted - observed, 0.0).astype(BF16)
        res_out[i] = residual
        wide = residual.astype(F32)
        for row in range(OUT):
            first = RES_LEAD + EXT * row
            resid[first : first + OUT, :] = wide[OUT * row : OUT * (row + 1)]

        def read_residual(s, t):
            return resid[pl.ds(RES_LEAD - EXT * s - t, SLOT_ROWS), :].astype(BF16)

        adjoint = convolve(read_residual, taps_ref, SLOT_ROWS).astype(BF16)
        adj_slots[slots, i, :SLOT_ROWS] = adjoint[:, :LANES]
        adj_slots[slots, i, SLOT_ROWS:] = adjoint[: ADJ_ROWS - SLOT_ROWS, LANES:]

    for i in range(GROUP):
        per_piece(i, taps[i], field.at[i], resid.at[i])
    for copy in sent(step):
        copy.start()

    @pl.when(step == pl.num_programs(0) - 1)
    def _():
        for copy in sent(step - 1) + sent(step):
            copy.wait()


def pieces(slots, cells, patches, taps, data):
    count = data.shape[0]
    cell = [
        pl.BlockSpec(
            (1, REACH * LANES, TILES * LANES),
            lambda p, slots, cells, i=i: (cells[GROUP * p + i], 0, 0),
        )
        for i in range(GROUP)
    ]
    block = pl.BlockSpec((GROUP, BLOCKS, 2 * LANES), lambda p, slots, cells: (p, 0, 0))
    return pl.pallas_call(
        pieces_kernel,
        grid_spec=pltpu.PrefetchScalarGridSpec(
            num_scalar_prefetch=2,
            grid=(count // GROUP,),
            in_specs=[whole_vmem(), *cell, block],
            out_specs=[pl.BlockSpec(memory_space=pltpu.HBM), block],
            scratch_shapes=[
                pltpu.VMEM((GROUP, PATCH_ROWS, LANES), F32),
                pltpu.VMEM((GROUP, RES_LEAD + SLOT_ROWS, 2 * LANES), F32),
                pltpu.VMEM((2, GROUP, ADJ_ROWS, LANES), BF16),
                pltpu.SemaphoreType.DMA((2, GROUP)),
            ],
        ),
        out_shape=[
            jax.ShapeDtypeStruct((patches.shape[0], ADJ_ROWS, LANES), BF16),
            jax.ShapeDtypeStruct(data.shape, BF16),
        ],
        cost_estimate=SMALL,
        name="pieces",
    )(slots, cells, on_chip(patches), *[taps] * GROUP, data)


def ungroup_kernel(res_ref, out_ref):
    turn = reversed_groups()[LANES:]

    def per_piece(p, carry):
        halves = [
            jnp.dot(
                res_ref[p, :, half * LANES : (half + 1) * LANES], turn, preferred_element_type=F32
            ).reshape(OUT, 8, LANES)
            for half in range(2)
        ]
        pixels = swap_reversed(jnp.stack(halves, 1).reshape(2 * OUT, 8, LANES))
        out_ref[p] = pixels.reshape(B, LANES).astype(BF16)
        return carry

    lax.fori_loop(0, res_ref.shape[0], per_piece, 0)


def ungroup(residual):
    count = residual.shape[0]
    return pl.pallas_call(
        ungroup_kernel,
        grid=(count // BATCH,),
        in_specs=[pl.BlockSpec((BATCH, BLOCKS, 2 * LANES), lambda p: (p, 0, 0))],
        out_specs=pl.BlockSpec((BATCH, B, B), lambda p: (p, 0, 0)),
        out_shape=jax.ShapeDtypeStruct((count, B, B), BF16),
        cost_estimate=SMALL,
        name="ungroup",
    )(residual)


def fold_kernel(per_row, half_rows, ids_ref, slot_ref, out_ref, canvas, scratch, packed):
    canvas[...] = jnp.zeros_like(canvas)
    inside = lax.broadcasted_iota(jnp.int32, (G, LANES), 0) < EXT

    def per_slot(n, carry):
        named = ids_ref[n // CAP, 0, n % CAP]

        @pl.when(named >= 0)
        def _():
            first_row = named // per_row * (2 * OUT)
            first_col = pl.multiple_of(named % per_row * OUT, 8)
            scratch[:ADJ_ROWS, :] = slot_ref[n].astype(F32)
            for row in range(EXT):
                for half in range(2 if row < EXT - 1 else 1):
                    first = SLOT_ROWS * half + EXT * row
                    part = jnp.where(inside, scratch[first : first + G, :], 0.0)
                    at = (first_row + 2 * row + half, pl.ds(first_col, G), slice(None))
                    canvas[at] = canvas[at] + part

        return carry

    lax.fori_loop(0, slot_ref.shape[0], per_slot, 0)
    for chunk in range(per_row):
        first = OUT * chunk + 1
        for row in range(half_rows):
            packed[CHUNK * row : CHUNK * row + G, :] = canvas[row, first : first + G, :]
        out_ref[chunk] = packed[...].astype(BF16)


def fold(ids, received, per_row, half_rows):
    return pl.pallas_call(
        lambda *refs: fold_kernel(per_row, half_rows, *refs),
        in_specs=[
            pl.BlockSpec(memory_space=pltpu.SMEM),
            pl.BlockSpec(memory_space=pltpu.VMEM),
        ],
        out_specs=pl.BlockSpec(memory_space=pltpu.VMEM),
        scratch_shapes=[
            pltpu.VMEM((half_rows, PITCH + 8, LANES), F32),
            pltpu.VMEM((ADJ_ROWS + 8, LANES), F32),
            pltpu.VMEM((CHUNK_ROWS, LANES), F32),
        ],
        out_shape=pltpu.VMEM((per_row, CHUNK_ROWS, LANES), BF16),
        cost_estimate=SMALL,
        name="fold",
    )(ids, on_chip(received))


def finish_kernel(half_rows, terms_ref, up_out, middle_out, down_out, summed, canvas):
    total = terms_ref[0].astype(F32)
    for term in range(1, terms_ref.shape[0]):
        total = total + terms_ref[term].astype(F32)
    summed[...] = total
    near = lax.broadcasted_iota(jnp.int32, (8, LANES), 1) < LANES - SHIFT
    for first in range(0, half_rows, 8):
        count = min(8, half_rows - first)
        starts = [CHUNK * (first + row) for row in range(count)]
        tiles = swap_groups(jnp.stack([summed[start : start + 8, :] for start in starts], 0))
        edges = summed[pl.ds(starts[0] + 8, count, stride=CHUNK), :]
        if count < 8:
            edges = jnp.concatenate([edges, jnp.zeros((8 - count, LANES), F32)], axis=0)
        edges = swap_groups(edges.reshape(1, 8, LANES)).reshape(8, LANES)
        for row in range(count):
            tile = pltpu.roll(tiles[row], LANES - SHIFT, 1)
            edge = pltpu.roll(edges, (LANES - SHIFT - G * row) % LANES, 1)
            start = 8 * (first + row)
            canvas[start : start + 8, :] = jnp.where(near, tile, edge)
    middle = middle_out.shape[0]
    up_out[...] = canvas[:HALO, :].astype(BF16)
    middle_out[...] = canvas[HALO : HALO + middle, :]
    down_out[...] = canvas[HALO + middle : 2 * HALO + middle, :].astype(BF16)


def finish(terms, half_rows, rows):
    rim = pltpu.VMEM((HALO, LANES), BF16)
    vmem = pl.BlockSpec(memory_space=pltpu.VMEM)
    return pl.pallas_call(
        lambda *refs: finish_kernel(half_rows, *refs),
        in_specs=[vmem],
        out_specs=[vmem, vmem, vmem],
        out_shape=[rim, jax.ShapeDtypeStruct((rows, LANES), F32), rim],
        scratch_shapes=[
            pltpu.VMEM((CHUNK_ROWS, LANES), F32),
            pltpu.VMEM((8 * half_rows, LANES), F32),
        ],
        cost_estimate=SMALL,
        name="finish",
    )(on_chip(terms))


def rims_kernel(middle_ref, above_ref, below_ref, out_ref):
    rows = out_ref.shape[0]
    out_ref[...] = middle_ref[...]

    @pl.when(pl.program_id(0) == 0)
    def _():
        out_ref[:HALO, :] = out_ref[:HALO, :] + above_ref[...].astype(F32)

    @pl.when(pl.program_id(0) == 1)
    def _():
        out_ref[rows - HALO :, :] = out_ref[rows - HALO :, :] + below_ref[...].astype(F32)


def add_rims(middle, above, below):
    rows = 32
    last = middle.shape[0] // rows - 1
    block = pl.BlockSpec((rows, LANES), lambda i: (i * last, 0))
    return pl.pallas_call(
        rims_kernel,
        grid=(2,),
        in_specs=[block, whole_vmem(), whole_vmem()],
        out_specs=block,
        out_shape=jax.ShapeDtypeStruct(middle.shape, F32),
        input_output_aliases={0: 0},
        cost_estimate=SMALL,
        name="rims",
    )(middle, on_chip(above), on_chip(below))


def shards(sky_model, exposure_data, pixel_mask, block_owner, block_local, psf_cell, psf_table):
    sky_count = lax.axis_size("sky")
    stripe_rows, stripe_cols = sky_model.shape
    per_row = stripe_cols // B
    block_total = stripe_rows // B * per_row
    piece_count = exposure_data.shape[0]
    owner_sky = block_owner[:, 0]
    code = lax.broadcasted_iota(jnp.int32, (piece_count,), 0) * block_total + block_local
    mine = owner_sky[None, :] == lax.broadcasted_iota(jnp.int32, (sky_count, 1), 0)
    first = jnp.min(jnp.where(mine, code[None, :], piece_count * block_total), axis=1)
    last = jnp.max(jnp.where(mine, code[None, :], -1), axis=1)
    requests = jnp.stack(
        [
            jnp.where(last < 0, -1, first % block_total),
            jnp.where(last > first, last % block_total, -1),
        ],
        axis=1,
    )
    asked = lax.all_to_all(
        requests[:, None, :], "sky", split_axis=0, concat_axis=0, tiled=True
    )
    above = from_behind(sky_model[stripe_rows - HALO :], "sky", 1)
    below = from_behind(sky_model[:HALO], "sky", -1)
    half_rows = (stripe_rows + 2 * HALO + TAIL) // 8
    second = jnp.any(mine & (first[:, None] < code[None, :]), axis=0)
    slot_index = owner_sky * CAP + second.astype(jnp.int32)
    kernels = padded_kernels(psf_table)
    asked, above, below, slot_index = lax.optimization_barrier((asked, above, below, slot_index))
    blocks = stripe_blocks(sky_model, above, below, half_rows)
    outgoing = cut_patches(asked, blocks, per_row)
    exposure_data, pixel_mask, kernels, _ = lax.optimization_barrier(
        (exposure_data, pixel_mask, kernels, outgoing)
    )
    patches = lax.all_to_all(outgoing, "sky", split_axis=0, concat_axis=0, tiled=True)
    data = regroup(exposure_data, pixel_mask)
    taps = build_taps(kernels)
    adjoints, residuals = pieces(slot_index, psf_cell, patches, taps, data)
    received = lax.all_to_all(adjoints, "sky", split_axis=0, concat_axis=0, tiled=True)
    received, residual = lax.optimization_barrier((received, ungroup(residuals)))

    partial = fold(asked, received, per_row, half_rows)
    terms = lax.all_to_all(partial, "exp", split_axis=0, concat_axis=0, tiled=True)
    up, middle, down = finish(terms, half_rows, stripe_rows)
    from_below = from_behind(up, "sky", -1)
    from_above = from_behind(down, "sky", 1)
    gradient = add_rims(middle, from_above, from_below)
    return (gradient, residual)


def solution(mesh):
    in_specs = (
        P("sky", None),
        P(("sky", "exp"), None, None),
        P(("sky", "exp"), None, None),
        P(("sky", "exp"), None),
        P(("sky", "exp")),
        P(("sky", "exp")),
        P("exp", None),
    )
    out_specs = (P("sky", "exp"), P(("sky", "exp"), None, None))
    return jax.shard_map(shards, mesh=mesh, in_specs=in_specs, out_specs=out_specs, check_vma=False)
```

```python
import jax
import jax.numpy as jnp
from jax import lax
from jax.experimental import pallas as pl
from jax.experimental.pallas import tpu as pltpu
from jax.sharding import PartitionSpec as P

B = 128
PSF = 41
HALO = 20
CAP = 2

G = 16
LANES = 128
OUT = B // G
EXT = 11
REACH = 4
TAIL = 8
BLOCKS = OUT * OUT
PATCH_ROWS = 232
ADJ_ROWS = 240
SLOT_ROWS = 128
PITCH = 72
TILES = 6
RES_LEAD = 40
TAP_ROWS = 48
GROUP = 4
BATCH = 4
SLOTS = 8
CHUNK = 9
CHUNK_ROWS = 352
SHIFT = 4
UNKNOWN = 2.0**100
SMALL = pl.CostEstimate(flops=1000, bytes_accessed=1000, transcendentals=0)
F32 = jnp.float32
BF16 = jnp.bfloat16


def whole_vmem():
    return pl.BlockSpec(memory_space=pltpu.VMEM)


def on_chip(x):
    return pltpu.with_memory_space_constraint(x, pltpu.VMEM)


def from_behind(x, axis, by):
    devices = lax.axis_size(axis)
    pairs = [(i, i + by) for i in range(devices) if 0 <= i + by < devices]
    return lax.ppermute(x, axis, pairs)


def swap_groups(x):
    sub = lax.broadcasted_iota(jnp.int32, x.shape, 1)
    group = lax.broadcasted_iota(jnp.int32, x.shape, 2) // G
    for d in (4, 2, 1):
        sub_bit, group_bit = (sub & d) != 0, (group & d) != 0
        up = pltpu.roll(pltpu.roll(x, 8 - d, 1), G * d, 2)
        down = up if d == 4 else pltpu.roll(pltpu.roll(x, d, 1), LANES - G * d, 2)
        x = jnp.where(sub_bit == group_bit, x, jnp.where(group_bit, up, down))
    return x


def reversed_groups(shift=0):
    source = lax.broadcasted_iota(jnp.int32, (2 * LANES, LANES), 0)
    lane = lax.broadcasted_iota(jnp.int32, (2 * LANES, LANES), 1)
    group = (8 - lane // G) % 8
    return (source == LANES - shift + group * G + lane % G).astype(BF16)


def swap_reversed(x):
    group = lax.broadcasted_iota(jnp.int32, (8, LANES), 1) // G
    tiles = []
    for tile in range(x.shape[0]):
        now = pltpu.roll(x[tile], 0, 1, stride=G, stride_axis=0)
        for d in (1, 2, 4):
            now = jnp.where((group & d) != 0, pltpu.roll(now, 8 - d, 0), now)
        tiles.append(pltpu.roll(now, 0, 1, stride=G, stride_axis=0))
    return jnp.stack(tiles, 0)


def regroup_kernel(data_ref, keep_ref, out_ref):
    def per_piece(p, carry):
        known = jnp.where(keep_ref[p] != 0, data_ref[p].astype(F32), UNKNOWN).astype(BF16)
        turned = jnp.dot(known, reversed_groups()[LANES:], preferred_element_type=F32)
        blocks = swap_reversed(turned.reshape(2 * OUT, 8, LANES)).reshape(OUT, 2, 8, LANES)
        for half in range(2):
            out_ref[p, :, half * LANES : (half + 1) * LANES] = (
                blocks[:, half].reshape(BLOCKS, LANES).astype(BF16)
            )
        return carry

    lax.fori_loop(0, data_ref.shape[0], per_piece, 0, unroll=2)


def regroup(exposure_data, pixel_mask):
    pieces = exposure_data.shape[0]
    block = pl.BlockSpec((BATCH, B, B), lambda p: (p, 0, 0))
    return pl.pallas_call(
        regroup_kernel,
        grid=(pieces // BATCH,),
        in_specs=[block, block],
        out_specs=pl.BlockSpec((BATCH, BLOCKS, 2 * LANES), lambda p: (p, 0, 0)),
        out_shape=jax.ShapeDtypeStruct((pieces, BLOCKS, 2 * LANES), BF16),
        cost_estimate=SMALL,
        name="regroup",
    )(exposure_data, pixel_mask)


def taps_kernel(kernel_ref, out_ref, windows, rows):
    lane = lax.broadcasted_iota(jnp.int32, (G, LANES), 1)
    odd = (lane // G) % 2 == 1
    wide = lax.broadcasted_iota(jnp.int32, (TAP_ROWS, LANES), 1) // (2 * G)
    quarter = lax.broadcasted_iota(jnp.int32, (TILES, LANES), 1) // (2 * G)

    kernel = kernel_ref[0].astype(F32)
    spread = pltpu.roll(kernel, G, 1)
    for t in range(1, REACH):
        spread = jnp.where(wide == t, pltpu.roll(kernel, G * t + G, 1), spread)
    windows[...] = spread
    for parity in range(2):
        picked = [windows[pl.ds(parity + 2 * q, TILES, stride=8), :] for q in range(4)]
        for t in range(REACH):
            row = picked[0] if t == 0 else pltpu.roll(picked[0], 2 * G * (4 - t), 1)
            for q in range(1, 4):
                by = (q - t) % 4
                part = picked[q] if by == 0 else pltpu.roll(picked[q], 2 * G * by, 1)
                row = jnp.where(quarter == q, part, row)
            rows[t, parity, :TILES, :] = row

    def per_shift(t, carry):
        before = [jnp.zeros((G, LANES), F32)] * 8
        for tile in range(TILES):
            even_row, odd_row = (
                jnp.broadcast_to(rows[t, parity, tile : tile + 1, :], (G, LANES))
                for parity in range(2)
            )
            even_row = pltpu.roll(even_row, LANES - G, 1, stride=1, stride_axis=0)
            odd_row = pltpu.roll(odd_row, 0, 1, stride=1, stride_axis=0)
            now = jnp.where(odd, odd_row, even_row)
            turns = [now] + [pltpu.roll(now, G * phase, 1) for phase in range(1, 8)]
            for phase in range(8):
                part = turns[phase]
                if phase > 0:
                    part = jnp.where(lane < G * phase, before[phase], part)
                start = pl.multiple_of(t * LANES + phase * G, G)
                lanes = slice(tile * LANES, (tile + 1) * LANES)
                out_ref[0, pl.ds(start, G), lanes] = part.astype(BF16)
            before = turns
        return carry

    lax.fori_loop(0, REACH, per_shift, 0)


def padded_kernels(table):
    kernels = table.reshape(table.shape[0], PSF, PSF)
    return jnp.pad(kernels, ((0, 0), (0, TAP_ROWS - PSF), (0, LANES - PSF)))


def build_taps(kernels):
    cells = kernels.shape[0]
    return pl.pallas_call(
        taps_kernel,
        grid=(cells,),
        in_specs=[pl.BlockSpec((1, TAP_ROWS, LANES), lambda c: (c, 0, 0))],
        out_specs=pl.BlockSpec((1, REACH * LANES, TILES * LANES), lambda c: (c, 0, 0)),
        out_shape=jax.ShapeDtypeStruct((cells, REACH * LANES, TILES * LANES), BF16),
        scratch_shapes=[
            pltpu.VMEM((TAP_ROWS, LANES), F32),
            pltpu.VMEM((REACH, 2, 8, LANES), F32),
        ],
        cost_estimate=SMALL,
        name="taps",
    )(kernels)


def moved_tiles(pixels):
    rows, columns = pixels.shape
    turn = reversed_groups(HALO)
    empty = jnp.zeros((rows, LANES), BF16)
    tiles = [pixels[:, at : at + LANES] for at in range(0, columns, LANES)]
    return [
        jnp.dot(jnp.concatenate([old, now], axis=1), turn, preferred_element_type=F32)
        for old, now in zip([empty] + tiles, tiles + [empty])
    ]


def blocks_kernel(stripe_ref, above_ref, below_ref, out_ref, pixels):
    first = 0
    for ref in (above_ref, stripe_ref, below_ref):
        rows = ref.shape[0]
        for tile, moved in enumerate(moved_tiles(ref[...])):
            pixels[first : first + rows, tile * LANES : (tile + 1) * LANES] = moved
        first += rows
    pixels[first:, :] = jnp.zeros((TAIL, PITCH * G), F32)
    for row in range(out_ref.shape[0]):
        tiles = [
            pixels[8 * row : 8 * row + 8, at : at + LANES] for at in range(0, PITCH * G, LANES)
        ]
        out_ref[row] = swap_reversed(jnp.stack(tiles, 0)).reshape(PITCH, LANES)


def stripe_blocks(stripe, above, below, half_rows):
    return pl.pallas_call(
        blocks_kernel,
        in_specs=[whole_vmem(), whole_vmem(), whole_vmem()],
        out_specs=whole_vmem(),
        out_shape=pltpu.VMEM((half_rows, PITCH, LANES), F32),
        scratch_shapes=[pltpu.VMEM((8 * half_rows, PITCH * G), F32)],
        cost_estimate=SMALL,
        name="blocks",
    )(stripe, on_chip(above), on_chip(below))


def cut_kernel(per_row, ids_ref, blocks_ref, out_ref, scratch):
    step = pl.program_id(0)

    def per_slot(n, carry):
        at = step * SLOTS + n
        wanted = ids_ref[at // CAP, 0, at % CAP]

        @pl.when(wanted >= 0)
        def _():
            first_row = wanted // per_row * (2 * OUT)
            first_col = pl.multiple_of(wanted % per_row * OUT, 8)
            for row in range(2 * EXT - 1):
                part = blocks_ref[first_row + row, pl.ds(first_col, G), :]
                scratch[EXT * row : EXT * row + G, :] = part
            out_ref[n] = scratch[:PATCH_ROWS, :].astype(BF16)

        return carry

    lax.fori_loop(0, SLOTS, per_slot, 0)


def cut_patches(ids, blocks, per_row):
    slots = ids.shape[0] * CAP
    return pl.pallas_call(
        lambda *refs: cut_kernel(per_row, *refs),
        grid_spec=pltpu.PrefetchScalarGridSpec(
            num_scalar_prefetch=1,
            grid=(slots // SLOTS,),
            in_specs=[whole_vmem()],
            out_specs=pl.BlockSpec((SLOTS, PATCH_ROWS, LANES), lambda n, ids: (n, 0, 0)),
            scratch_shapes=[pltpu.VMEM((PATCH_ROWS + 8, LANES), F32)],
        ),
        out_shape=jax.ShapeDtypeStruct((slots, PATCH_ROWS, LANES), BF16),
        cost_estimate=SMALL,
        name="cut",
    )(ids, on_chip(blocks))


def block_taps(taps_ref, s, t):
    taps = slice(t * LANES, (t + 1) * LANES)
    upper = taps_ref[0, taps, 2 * s * LANES : (2 * s + 2) * LANES]
    if s == 0:
        lower = jnp.concatenate(
            [jnp.zeros((LANES, LANES), BF16), taps_ref[0, taps, 0:LANES]], axis=1
        )
    else:
        lower = taps_ref[0, taps, (2 * s - 1) * LANES : (2 * s + 1) * LANES]
    return jnp.concatenate([upper, lower], axis=0)


def last_taps(taps_ref, t):
    return taps_ref[0, t * LANES : (t + 1) * LANES, (TILES - 1) * LANES :]


def correlate(read, taps_ref):
    across = (((1,), (1,)), ((), ()))
    total = jnp.zeros((2 * BLOCKS, LANES), F32)
    for t in range(REACH):
        for d in range(TILES // 2):
            taps = taps_ref[0, t * LANES : (t + 1) * LANES, 2 * d * LANES : (2 * d + 2) * LANES]
            total = total + lax.dot_general(
                read(d, t), taps, across, preferred_element_type=F32
            )
    return jnp.concatenate([total[:BLOCKS], total[BLOCKS:]], axis=1)


def convolve(read, taps_ref, rows):
    total = jnp.zeros((rows, 2 * LANES), F32)
    for t in range(REACH):
        for s in range(REACH - 1):
            total = total + jnp.dot(
                read(s, t), block_taps(taps_ref, s, t), preferred_element_type=F32
            )
    last = jnp.zeros((rows, LANES), F32)
    for t in range(0, REACH, 2):
        field = [read(REACH - 1, t + i)[:, LANES:] for i in range(2)]
        taps = [last_taps(taps_ref, t + i) for i in range(2)]
        last = last + jnp.dot(
            jnp.concatenate(field, axis=1),
            jnp.concatenate(taps, axis=0),
            preferred_element_type=F32,
        )
    return jnp.concatenate([total[:, :LANES] + last, total[:, LANES:]], axis=1)


def pieces_kernel(slot_ref, cell_ref, patch_ref, *refs):
    taps, refs = refs[:GROUP], refs[GROUP:]
    data_ref, adjoints, res_out, field, resid, adj_slots, sems = refs
    step = pl.program_id(0)
    slots = lax.rem(step, 2)

    @pl.when(step == 0)
    def _():
        resid[...] = jnp.zeros_like(resid)

    def sent(step):
        at = lax.rem(step, 2)
        return [
            pltpu.make_async_copy(
                adj_slots.at[at, i], adjoints.at[slot_ref[GROUP * step + i]], sems.at[at, i]
            )
            for i in range(GROUP)
        ]

    @pl.when(step >= 2)
    def _():
        for copy in sent(step - 2):
            copy.wait()

    def forward(i, taps_ref, field):
        field[...] = patch_ref[slot_ref[GROUP * step + i]].astype(F32)

        def read_patch(d, t):
            parts = []
            for half in range(2):
                for row in range(OUT):
                    at = EXT * (2 * (row + d) + half) + t
                    pair = [field[at : at + OUT, :], field[at + EXT : at + EXT + OUT, :]]
                    parts.append(jnp.concatenate(pair, axis=1))
            return jnp.concatenate(parts, axis=0).astype(BF16)

        return correlate(read_patch, taps_ref)

    def compare(i, predicted, resid):
        observed = data_ref[i].astype(F32)
        residual = jnp.where(observed < UNKNOWN, predicted - observed, 0.0).astype(BF16)
        res_out[i] = residual
        wide = residual.astype(F32)
        for row in range(OUT):
            first = RES_LEAD + EXT * row
            resid[first : first + OUT, :] = wide[OUT * row : OUT * (row + 1)]

    def backward(i, taps_ref, resid):
        def read_residual(s, t):
            return resid[pl.ds(RES_LEAD - EXT * s - t, SLOT_ROWS), :].astype(BF16)

        adjoint = convolve(read_residual, taps_ref, SLOT_ROWS).astype(BF16)
        adj_slots[slots, i, :SLOT_ROWS] = adjoint[:, :LANES]
        adj_slots[slots, i, SLOT_ROWS:] = adjoint[: ADJ_ROWS - SLOT_ROWS, LANES:]

    for i in range(GROUP):
        compare(i, forward(i, taps[i], field.at[i]), resid.at[i])
    for i in range(GROUP):
        backward(i, taps[i], resid.at[i])
    for copy in sent(step):
        copy.start()

    @pl.when(step == pl.num_programs(0) - 1)
    def _():
        for copy in sent(step - 1) + sent(step):
            copy.wait()


def pieces(slots, cells, patches, taps, data):
    count = data.shape[0]
    cell = [
        pl.BlockSpec(
            (1, REACH * LANES, TILES * LANES),
            lambda p, slots, cells, i=i: (cells[GROUP * p + i], 0, 0),
        )
        for i in range(GROUP)
    ]
    block = pl.BlockSpec((GROUP, BLOCKS, 2 * LANES), lambda p, slots, cells: (p, 0, 0))
    return pl.pallas_call(
        pieces_kernel,
        grid_spec=pltpu.PrefetchScalarGridSpec(
            num_scalar_prefetch=2,
            grid=(count // GROUP,),
            in_specs=[whole_vmem(), *cell, block],
            out_specs=[pl.BlockSpec(memory_space=pltpu.HBM), block],
            scratch_shapes=[
                pltpu.VMEM((GROUP, PATCH_ROWS, LANES), F32),
                pltpu.VMEM((GROUP, RES_LEAD + SLOT_ROWS, 2 * LANES), F32),
                pltpu.VMEM((2, GROUP, ADJ_ROWS, LANES), BF16),
                pltpu.SemaphoreType.DMA((2, GROUP)),
            ],
        ),
        out_shape=[
            jax.ShapeDtypeStruct((patches.shape[0], ADJ_ROWS, LANES), BF16),
            jax.ShapeDtypeStruct(data.shape, BF16),
        ],
        cost_estimate=SMALL,
        name="pieces",
    )(slots, cells, on_chip(patches), *[taps] * GROUP, data)


def ungroup_kernel(res_ref, out_ref):
    turn = reversed_groups()[LANES:]

    def per_piece(p, carry):
        halves = [
            jnp.dot(
                res_ref[p, :, half * LANES : (half + 1) * LANES], turn, preferred_element_type=F32
            ).reshape(OUT, 8, LANES)
            for half in range(2)
        ]
        pixels = swap_reversed(jnp.stack(halves, 1).reshape(2 * OUT, 8, LANES))
        out_ref[p] = pixels.reshape(B, LANES).astype(BF16)
        return carry

    lax.fori_loop(0, res_ref.shape[0], per_piece, 0)


def ungroup(residual):
    count = residual.shape[0]
    return pl.pallas_call(
        ungroup_kernel,
        grid=(count // BATCH,),
        in_specs=[pl.BlockSpec((BATCH, BLOCKS, 2 * LANES), lambda p: (p, 0, 0))],
        out_specs=pl.BlockSpec((BATCH, B, B), lambda p: (p, 0, 0)),
        out_shape=jax.ShapeDtypeStruct((count, B, B), BF16),
        cost_estimate=SMALL,
        name="ungroup",
    )(residual)


def fold_kernel(per_row, half_rows, ids_ref, slot_ref, out_ref, canvas, scratch, packed):
    canvas[...] = jnp.zeros_like(canvas)
    inside = lax.broadcasted_iota(jnp.int32, (G, LANES), 0) < EXT

    def per_slot(n, carry):
        named = ids_ref[n // CAP, 0, n % CAP]

        @pl.when(named >= 0)
        def _():
            first_row = named // per_row * (2 * OUT)
            first_col = pl.multiple_of(named % per_row * OUT, 8)
            scratch[:ADJ_ROWS, :] = slot_ref[n].astype(F32)
            for row in range(EXT):
                for half in range(2 if row < EXT - 1 else 1):
                    first = SLOT_ROWS * half + EXT * row
                    part = jnp.where(inside, scratch[first : first + G, :], 0.0)
                    at = (first_row + 2 * row + half, pl.ds(first_col, G), slice(None))
                    canvas[at] = canvas[at] + part

        return carry

    lax.fori_loop(0, slot_ref.shape[0], per_slot, 0)
    for chunk in range(per_row):
        first = OUT * chunk + 1
        for row in range(half_rows):
            packed[CHUNK * row : CHUNK * row + G, :] = canvas[row, first : first + G, :]
        out_ref[chunk] = packed[...].astype(BF16)


def fold(ids, received, per_row, half_rows):
    return pl.pallas_call(
        lambda *refs: fold_kernel(per_row, half_rows, *refs),
        in_specs=[
            pl.BlockSpec(memory_space=pltpu.SMEM),
            pl.BlockSpec(memory_space=pltpu.VMEM),
        ],
        out_specs=pl.BlockSpec(memory_space=pltpu.VMEM),
        scratch_shapes=[
            pltpu.VMEM((half_rows, PITCH + 8, LANES), F32),
            pltpu.VMEM((ADJ_ROWS + 8, LANES), F32),
            pltpu.VMEM((CHUNK_ROWS, LANES), F32),
        ],
        out_shape=pltpu.VMEM((per_row, CHUNK_ROWS, LANES), BF16),
        cost_estimate=SMALL,
        name="fold",
    )(ids, on_chip(received))


def finish_kernel(half_rows, terms_ref, up_out, middle_out, down_out, summed, canvas):
    total = terms_ref[0].astype(F32)
    for term in range(1, terms_ref.shape[0]):
        total = total + terms_ref[term].astype(F32)
    summed[...] = total
    near = lax.broadcasted_iota(jnp.int32, (8, LANES), 1) < LANES - SHIFT
    for first in range(0, half_rows, 8):
        count = min(8, half_rows - first)
        starts = [CHUNK * (first + row) for row in range(count)]
        tiles = swap_groups(jnp.stack([summed[start : start + 8, :] for start in starts], 0))
        edges = summed[pl.ds(starts[0] + 8, count, stride=CHUNK), :]
        if count < 8:
            edges = jnp.concatenate([edges, jnp.zeros((8 - count, LANES), F32)], axis=0)
        edges = swap_groups(edges.reshape(1, 8, LANES)).reshape(8, LANES)
        for row in range(count):
            tile = pltpu.roll(tiles[row], LANES - SHIFT, 1)
            edge = pltpu.roll(edges, (LANES - SHIFT - G * row) % LANES, 1)
            start = 8 * (first + row)
            canvas[start : start + 8, :] = jnp.where(near, tile, edge)
    middle = middle_out.shape[0]
    up_out[...] = canvas[:HALO, :].astype(BF16)
    middle_out[...] = canvas[HALO : HALO + middle, :]
    down_out[...] = canvas[HALO + middle : 2 * HALO + middle, :].astype(BF16)


def finish(terms, half_rows, rows):
    rim = pltpu.VMEM((HALO, LANES), BF16)
    vmem = pl.BlockSpec(memory_space=pltpu.VMEM)
    return pl.pallas_call(
        lambda *refs: finish_kernel(half_rows, *refs),
        in_specs=[vmem],
        out_specs=[vmem, vmem, vmem],
        out_shape=[rim, jax.ShapeDtypeStruct((rows, LANES), F32), rim],
        scratch_shapes=[
            pltpu.VMEM((CHUNK_ROWS, LANES), F32),
            pltpu.VMEM((8 * half_rows, LANES), F32),
        ],
        cost_estimate=SMALL,
        name="finish",
    )(on_chip(terms))


def rims_kernel(middle_ref, above_ref, below_ref, out_ref):
    rows = out_ref.shape[0]
    out_ref[...] = middle_ref[...]

    @pl.when(pl.program_id(0) == 0)
    def _():
        out_ref[:HALO, :] = out_ref[:HALO, :] + above_ref[...].astype(F32)

    @pl.when(pl.program_id(0) == 1)
    def _():
        out_ref[rows - HALO :, :] = out_ref[rows - HALO :, :] + below_ref[...].astype(F32)


def add_rims(middle, above, below):
    rows = 32
    last = middle.shape[0] // rows - 1
    block = pl.BlockSpec((rows, LANES), lambda i: (i * last, 0))
    return pl.pallas_call(
        rims_kernel,
        grid=(2,),
        in_specs=[block, whole_vmem(), whole_vmem()],
        out_specs=block,
        out_shape=jax.ShapeDtypeStruct(middle.shape, F32),
        input_output_aliases={0: 0},
        cost_estimate=SMALL,
        name="rims",
    )(middle, on_chip(above), on_chip(below))


def shards(sky_model, exposure_data, pixel_mask, block_owner, block_local, psf_cell, psf_table):
    sky_count = lax.axis_size("sky")
    stripe_rows, stripe_cols = sky_model.shape
    per_row = stripe_cols // B
    block_total = stripe_rows // B * per_row
    piece_count = exposure_data.shape[0]
    owner_sky = block_owner[:, 0]
    code = lax.broadcasted_iota(jnp.int32, (piece_count,), 0) * block_total + block_local
    mine = owner_sky[None, :] == lax.broadcasted_iota(jnp.int32, (sky_count, 1), 0)
    first = jnp.min(jnp.where(mine, code[None, :], piece_count * block_total), axis=1)
    last = jnp.max(jnp.where(mine, code[None, :], -1), axis=1)
    requests = jnp.stack(
        [
            jnp.where(last < 0, -1, first % block_total),
            jnp.where(last > first, last % block_total, -1),
        ],
        axis=1,
    )
    asked = lax.all_to_all(
        requests[:, None, :], "sky", split_axis=0, concat_axis=0, tiled=True
    )
    above = from_behind(sky_model[stripe_rows - HALO :], "sky", 1)
    below = from_behind(sky_model[:HALO], "sky", -1)
    half_rows = (stripe_rows + 2 * HALO + TAIL) // 8
    second = jnp.any(mine & (first[:, None] < code[None, :]), axis=0)
    slot_index = owner_sky * CAP + second.astype(jnp.int32)
    kernels = padded_kernels(psf_table)
    asked, above, below, slot_index = lax.optimization_barrier((asked, above, below, slot_index))
    blocks = stripe_blocks(sky_model, above, below, half_rows)
    outgoing = cut_patches(asked, blocks, per_row)
    exposure_data, pixel_mask, kernels, _ = lax.optimization_barrier(
        (exposure_data, pixel_mask, kernels, outgoing)
    )
    patches = lax.all_to_all(outgoing, "sky", split_axis=0, concat_axis=0, tiled=True)
    data = regroup(exposure_data, pixel_mask)
    taps = build_taps(kernels)
    adjoints, residuals = pieces(slot_index, psf_cell, patches, taps, data)
    received = lax.all_to_all(adjoints, "sky", split_axis=0, concat_axis=0, tiled=True)
    received, residual = lax.optimization_barrier((received, ungroup(residuals)))

    partial = fold(asked, received, per_row, half_rows)
    terms = lax.all_to_all(partial, "exp", split_axis=0, concat_axis=0, tiled=True)
    up, middle, down = finish(terms, half_rows, stripe_rows)
    from_below = from_behind(up, "sky", -1)
    from_above = from_behind(down, "sky", 1)
    gradient = add_rims(middle, from_above, from_below)
    return (gradient, residual)


def solution(mesh):
    in_specs = (
        P("sky", None),
        P(("sky", "exp"), None, None),
        P(("sky", "exp"), None, None),
        P(("sky", "exp"), None),
        P(("sky", "exp")),
        P(("sky", "exp")),
        P("exp", None),
    )
    out_specs = (P("sky", "exp"), P(("sky", "exp"), None, None))
    return jax.shard_map(shards, mesh=mesh, in_specs=in_specs, out_specs=out_specs, check_vma=False)
```

```python
import jax
import jax.numpy as jnp
import numpy as np
from jax import lax
from jax.experimental import pallas as pl
from jax.experimental.pallas import tpu as pltpu
from jax.sharding import PartitionSpec as P

B = 128
PSF = 41
HALO = 20
CAP = 2

G = 16
LANES = 128
OUT = B // G
EXT = 11
REACH = 4
TAIL = 8
BLOCKS = OUT * OUT
PATCH_ROWS = 232
ADJ_ROWS = 240
SLOT_ROWS = 128
PITCH = 72
TILES = 6
RES_LEAD = 40
TAP_ROWS = 48
GROUP = 4
BATCH = 4
SLOTS = 8
CHUNK = 9
CHUNK_ROWS = 352
SHIFT = 4
UNKNOWN = 2.0**100
SMALL = pl.CostEstimate(flops=1000, bytes_accessed=1000, transcendentals=0)
F32 = jnp.float32
BF16 = jnp.bfloat16


def whole_vmem():
    return pl.BlockSpec(memory_space=pltpu.VMEM)


def on_chip(x):
    return pltpu.with_memory_space_constraint(x, pltpu.VMEM)


def from_behind(x, axis, by):
    devices = lax.axis_size(axis)
    pairs = [(i, i + by) for i in range(devices) if 0 <= i + by < devices]
    return lax.ppermute(x, axis, pairs)


def swap_groups(x):
    sub = lax.broadcasted_iota(jnp.int32, x.shape, 1)
    group = lax.broadcasted_iota(jnp.int32, x.shape, 2) // G
    for d in (4, 2, 1):
        sub_bit, group_bit = (sub & d) != 0, (group & d) != 0
        up = pltpu.roll(pltpu.roll(x, 8 - d, 1), G * d, 2)
        down = up if d == 4 else pltpu.roll(pltpu.roll(x, d, 1), LANES - G * d, 2)
        x = jnp.where(sub_bit == group_bit, x, jnp.where(group_bit, up, down))
    return x


def reversed_groups(shift=0):
    source = lax.broadcasted_iota(jnp.int32, (2 * LANES, LANES), 0)
    lane = lax.broadcasted_iota(jnp.int32, (2 * LANES, LANES), 1)
    group = (8 - lane // G) % 8
    return (source == LANES - shift + group * G + lane % G).astype(BF16)


def swap_reversed(x):
    group = lax.broadcasted_iota(jnp.int32, (8, LANES), 1) // G
    tiles = []
    for tile in range(x.shape[0]):
        now = pltpu.roll(x[tile], 0, 1, stride=G, stride_axis=0)
        for d in (1, 2, 4):
            now = jnp.where((group & d) != 0, pltpu.roll(now, 8 - d, 0), now)
        tiles.append(pltpu.roll(now, 0, 1, stride=G, stride_axis=0))
    return jnp.stack(tiles, 0)


def regroup_kernel(data_ref, keep_ref, out_ref):
    def per_piece(p, carry):
        known = jnp.where(keep_ref[p] != 0, data_ref[p].astype(F32), UNKNOWN).astype(BF16)
        turned = jnp.dot(known, reversed_groups()[LANES:], preferred_element_type=F32)
        blocks = swap_reversed(turned.reshape(2 * OUT, 8, LANES)).reshape(OUT, 2, 8, LANES)
        for half in range(2):
            out_ref[p, :, half * LANES : (half + 1) * LANES] = (
                blocks[:, half].reshape(BLOCKS, LANES).astype(BF16)
            )
        return carry

    lax.fori_loop(0, data_ref.shape[0], per_piece, 0, unroll=2)


def regroup(exposure_data, pixel_mask):
    pieces = exposure_data.shape[0]
    block = pl.BlockSpec((BATCH, B, B), lambda p: (p, 0, 0))
    return pl.pallas_call(
        regroup_kernel,
        grid=(pieces // BATCH,),
        in_specs=[block, block],
        out_specs=pl.BlockSpec((BATCH, BLOCKS, 2 * LANES), lambda p: (p, 0, 0)),
        out_shape=jax.ShapeDtypeStruct((pieces, BLOCKS, 2 * LANES), BF16),
        cost_estimate=SMALL,
        name="regroup",
    )(exposure_data, pixel_mask)


def taps_kernel(kernel_ref, out_ref, windows, rows):
    lane = lax.broadcasted_iota(jnp.int32, (G, LANES), 1)
    odd = (lane // G) % 2 == 1
    wide = lax.broadcasted_iota(jnp.int32, (TAP_ROWS, LANES), 1) // (2 * G)
    quarter = lax.broadcasted_iota(jnp.int32, (TILES, LANES), 1) // (2 * G)

    kernel = kernel_ref[0].astype(F32)
    spread = pltpu.roll(kernel, G, 1)
    for t in range(1, REACH):
        spread = jnp.where(wide == t, pltpu.roll(kernel, G * t + G, 1), spread)
    windows[...] = spread
    for parity in range(2):
        picked = [windows[pl.ds(parity + 2 * q, TILES, stride=8), :] for q in range(4)]
        for t in range(REACH):
            row = picked[0] if t == 0 else pltpu.roll(picked[0], 2 * G * (4 - t), 1)
            for q in range(1, 4):
                by = (q - t) % 4
                part = picked[q] if by == 0 else pltpu.roll(picked[q], 2 * G * by, 1)
                row = jnp.where(quarter == q, part, row)
            rows[t, parity, :TILES, :] = row

    def per_shift(t, carry):
        before = [jnp.zeros((G, LANES), F32)] * 8
        for tile in range(TILES):
            even_row, odd_row = (
                jnp.broadcast_to(rows[t, parity, tile : tile + 1, :], (G, LANES))
                for parity in range(2)
            )
            even_row = pltpu.roll(even_row, LANES - G, 1, stride=1, stride_axis=0)
            odd_row = pltpu.roll(odd_row, 0, 1, stride=1, stride_axis=0)
            now = jnp.where(odd, odd_row, even_row)
            turns = [now] + [pltpu.roll(now, G * phase, 1) for phase in range(1, 8)]
            for phase in range(8):
                part = turns[phase]
                if phase > 0:
                    part = jnp.where(lane < G * phase, before[phase], part)
                start = pl.multiple_of(t * LANES + phase * G, G)
                lanes = slice(tile * LANES, (tile + 1) * LANES)
                out_ref[0, pl.ds(start, G), lanes] = part.astype(BF16)
            before = turns
        return carry

    lax.fori_loop(0, REACH, per_shift, 0, unroll=REACH)


def padded_kernels(table):
    kernels = table.reshape(table.shape[0], PSF, PSF)
    return jnp.pad(kernels, ((0, 0), (0, TAP_ROWS - PSF), (0, LANES - PSF)))


def build_taps(kernels):
    cells = kernels.shape[0]
    return pl.pallas_call(
        taps_kernel,
        grid=(cells,),
        in_specs=[pl.BlockSpec((1, TAP_ROWS, LANES), lambda c: (c, 0, 0))],
        out_specs=pl.BlockSpec((1, REACH * LANES, TILES * LANES), lambda c: (c, 0, 0)),
        out_shape=jax.ShapeDtypeStruct((cells, REACH * LANES, TILES * LANES), BF16),
        scratch_shapes=[
            pltpu.VMEM((TAP_ROWS, LANES), F32),
            pltpu.VMEM((REACH, 2, 8, LANES), F32),
        ],
        cost_estimate=SMALL,
        name="taps",
    )(kernels)


def moved_tiles(pixels):
    rows, columns = pixels.shape
    turn = reversed_groups(HALO)
    empty = jnp.zeros((rows, LANES), BF16)
    tiles = [pixels[:, at : at + LANES] for at in range(0, columns, LANES)]
    return [
        jnp.dot(jnp.concatenate([old, now], axis=1), turn, preferred_element_type=F32)
        for old, now in zip([empty] + tiles, tiles + [empty])
    ]


def blocks_kernel(stripe_ref, above_ref, below_ref, out_ref, pixels):
    first = 0
    for ref in (above_ref, stripe_ref, below_ref):
        rows = ref.shape[0]
        for tile, moved in enumerate(moved_tiles(ref[...])):
            pixels[first : first + rows, tile * LANES : (tile + 1) * LANES] = moved
        first += rows
    pixels[first:, :] = jnp.zeros((TAIL, PITCH * G), F32)
    for row in range(out_ref.shape[0]):
        tiles = [
            pixels[8 * row : 8 * row + 8, at : at + LANES] for at in range(0, PITCH * G, LANES)
        ]
        out_ref[row] = swap_reversed(jnp.stack(tiles, 0)).reshape(PITCH, LANES)


def stripe_blocks(stripe, above, below, half_rows):
    return pl.pallas_call(
        blocks_kernel,
        in_specs=[whole_vmem(), whole_vmem(), whole_vmem()],
        out_specs=whole_vmem(),
        out_shape=pltpu.VMEM((half_rows, PITCH, LANES), F32),
        scratch_shapes=[pltpu.VMEM((8 * half_rows, PITCH * G), F32)],
        cost_estimate=SMALL,
        name="blocks",
    )(stripe, on_chip(above), on_chip(below))


def cut_kernel(per_row, ids_ref, blocks_ref, out_ref, scratch):
    step = pl.program_id(0)

    def per_slot(n, carry):
        at = step * SLOTS + n
        wanted = ids_ref[at // CAP, 0, at % CAP]

        @pl.when(wanted >= 0)
        def _():
            first_row = wanted // per_row * (2 * OUT)
            first_col = pl.multiple_of(wanted % per_row * OUT, 8)
            for row in range(2 * EXT - 1):
                part = blocks_ref[first_row + row, pl.ds(first_col, G), :]
                scratch[EXT * row : EXT * row + G, :] = part
            out_ref[n] = scratch[:PATCH_ROWS, :].astype(BF16)

        return carry

    lax.fori_loop(0, SLOTS, per_slot, 0)


def cut_patches(ids, blocks, per_row):
    slots = ids.shape[0] * CAP
    return pl.pallas_call(
        lambda *refs: cut_kernel(per_row, *refs),
        grid_spec=pltpu.PrefetchScalarGridSpec(
            num_scalar_prefetch=1,
            grid=(slots // SLOTS,),
            in_specs=[whole_vmem()],
            out_specs=pl.BlockSpec((SLOTS, PATCH_ROWS, LANES), lambda n, ids: (n, 0, 0)),
            scratch_shapes=[pltpu.VMEM((PATCH_ROWS + 8, LANES), F32)],
        ),
        out_shape=jax.ShapeDtypeStruct((slots, PATCH_ROWS, LANES), BF16),
        cost_estimate=SMALL,
        name="cut",
    )(ids, on_chip(blocks))


def block_taps(taps_ref, s, t):
    taps = slice(t * LANES, (t + 1) * LANES)
    upper = taps_ref[0, taps, 2 * s * LANES : (2 * s + 2) * LANES]
    if s == 0:
        lower = jnp.concatenate(
            [jnp.zeros((LANES, LANES), BF16), taps_ref[0, taps, 0:LANES]], axis=1
        )
    else:
        lower = taps_ref[0, taps, (2 * s - 1) * LANES : (2 * s + 1) * LANES]
    return jnp.concatenate([upper, lower], axis=0)


def last_taps(taps_ref, t):
    return taps_ref[0, t * LANES : (t + 1) * LANES, (TILES - 1) * LANES :]


def correlate(read, taps_ref):
    across = (((1,), (1,)), ((), ()))
    total = jnp.zeros((2 * BLOCKS, LANES), F32)
    for t in range(REACH):
        for d in range(TILES // 2):
            taps = taps_ref[0, t * LANES : (t + 1) * LANES, 2 * d * LANES : (2 * d + 2) * LANES]
            total = total + lax.dot_general(
                read(d, t), taps, across, preferred_element_type=F32
            )
    return jnp.concatenate([total[:BLOCKS], total[BLOCKS:]], axis=1)


def convolve(read, taps_ref, rows):
    total = jnp.zeros((rows, 2 * LANES), F32)
    for t in range(REACH):
        for s in range(REACH - 1):
            total = total + jnp.dot(
                read(s, t), block_taps(taps_ref, s, t), preferred_element_type=F32
            )
    last = jnp.zeros((rows, LANES), F32)
    for t in range(0, REACH, 2):
        field = [read(REACH - 1, t + i)[:, LANES:] for i in range(2)]
        taps = [last_taps(taps_ref, t + i) for i in range(2)]
        last = last + jnp.dot(
            jnp.concatenate(field, axis=1),
            jnp.concatenate(taps, axis=0),
            preferred_element_type=F32,
        )
    return jnp.concatenate([total[:, :LANES] + last, total[:, LANES:]], axis=1)


def pieces_kernel(slot_ref, cell_ref, patch_ref, *refs):
    taps, refs = refs[:GROUP], refs[GROUP:]
    data_ref, adjoints, res_out, field, resid, adj_slots, sems = refs
    step = pl.program_id(0)
    slots = lax.rem(step, 2)

    @pl.when(step == 0)
    def _():
        resid[...] = jnp.zeros_like(resid)

    def sent(step):
        at = lax.rem(step, 2)
        return [
            pltpu.make_async_copy(
                adj_slots.at[at, i], adjoints.at[slot_ref[GROUP * step + i]], sems.at[at, i]
            )
            for i in range(GROUP)
        ]

    @pl.when(step >= 2)
    def _():
        for copy in sent(step - 2):
            copy.wait()

    def forward(i, taps_ref, field):
        field[...] = patch_ref[slot_ref[GROUP * step + i]].astype(F32)

        def read_patch(d, t):
            parts = []
            for half in range(2):
                for row in range(OUT):
                    at = EXT * (2 * (row + d) + half) + t
                    pair = [field[at : at + OUT, :], field[at + EXT : at + EXT + OUT, :]]
                    parts.append(jnp.concatenate(pair, axis=1))
            return jnp.concatenate(parts, axis=0).astype(BF16)

        return correlate(read_patch, taps_ref)

    def compare(i, predicted, resid):
        observed = data_ref[i].astype(F32)
        residual = jnp.where(observed < UNKNOWN, predicted - observed, 0.0).astype(BF16)
        res_out[i] = residual
        wide = residual.astype(F32)
        for row in range(OUT):
            first = RES_LEAD + EXT * row
            resid[first : first + OUT, :] = wide[OUT * row : OUT * (row + 1)]

    def backward(i, taps_ref, resid):
        def read_residual(s, t):
            return resid[pl.ds(RES_LEAD - EXT * s - t, SLOT_ROWS), :].astype(BF16)

        adjoint = convolve(read_residual, taps_ref, SLOT_ROWS).astype(BF16)
        adj_slots[slots, i, :SLOT_ROWS] = adjoint[:, :LANES]
        adj_slots[slots, i, SLOT_ROWS:] = adjoint[: ADJ_ROWS - SLOT_ROWS, LANES:]

    for i in range(GROUP):
        compare(i, forward(i, taps[i], field.at[i]), resid.at[i])
    for i in range(GROUP):
        backward(i, taps[i], resid.at[i])
    for copy in sent(step):
        copy.start()

    @pl.when(step == pl.num_programs(0) - 1)
    def _():
        for copy in sent(step - 1) + sent(step):
            copy.wait()


def pieces(slots, cells, patches, taps, data):
    count = data.shape[0]
    cell = [
        pl.BlockSpec(
            (1, REACH * LANES, TILES * LANES),
            lambda p, slots, cells, i=i: (cells[GROUP * p + i], 0, 0),
        )
        for i in range(GROUP)
    ]
    block = pl.BlockSpec((GROUP, BLOCKS, 2 * LANES), lambda p, slots, cells: (p, 0, 0))
    return pl.pallas_call(
        pieces_kernel,
        grid_spec=pltpu.PrefetchScalarGridSpec(
            num_scalar_prefetch=2,
            grid=(count // GROUP,),
            in_specs=[whole_vmem(), *cell, block],
            out_specs=[pl.BlockSpec(memory_space=pltpu.HBM), block],
            scratch_shapes=[
                pltpu.VMEM((GROUP, PATCH_ROWS, LANES), F32),
                pltpu.VMEM((GROUP, RES_LEAD + SLOT_ROWS, 2 * LANES), F32),
                pltpu.VMEM((2, GROUP, ADJ_ROWS, LANES), BF16),
                pltpu.SemaphoreType.DMA((2, GROUP)),
            ],
        ),
        out_shape=[
            jax.ShapeDtypeStruct((patches.shape[0], ADJ_ROWS, LANES), BF16),
            jax.ShapeDtypeStruct(data.shape, BF16),
        ],
        cost_estimate=SMALL,
        name="pieces",
    )(slots, cells, on_chip(patches), *[taps] * GROUP, data)


def ungroup_kernel(res_ref, out_ref):
    turn = reversed_groups()[LANES:]

    def per_piece(p, carry):
        halves = [
            jnp.dot(
                res_ref[p, :, half * LANES : (half + 1) * LANES], turn, preferred_element_type=F32
            ).reshape(OUT, 8, LANES)
            for half in range(2)
        ]
        pixels = swap_reversed(jnp.stack(halves, 1).reshape(2 * OUT, 8, LANES))
        out_ref[p] = pixels.reshape(B, LANES).astype(BF16)
        return carry

    lax.fori_loop(0, res_ref.shape[0], per_piece, 0)


def ungroup(residual):
    count = residual.shape[0]
    return pl.pallas_call(
        ungroup_kernel,
        grid=(count // BATCH,),
        in_specs=[pl.BlockSpec((BATCH, BLOCKS, 2 * LANES), lambda p: (p, 0, 0))],
        out_specs=pl.BlockSpec((BATCH, B, B), lambda p: (p, 0, 0)),
        out_shape=jax.ShapeDtypeStruct((count, B, B), BF16),
        cost_estimate=SMALL,
        name="ungroup",
    )(residual)


def fold_kernel(per_row, half_rows, ids_ref, slot_ref, out_ref, canvas, scratch, packed):
    canvas[...] = jnp.zeros_like(canvas)
    inside = lax.broadcasted_iota(jnp.int32, (G, LANES), 0) < EXT

    def per_slot(n, carry):
        named = ids_ref[n // CAP, 0, n % CAP]

        @pl.when(named >= 0)
        def _():
            first_row = named // per_row * (2 * OUT)
            first_col = pl.multiple_of(named % per_row * OUT, 8)
            scratch[:ADJ_ROWS, :] = slot_ref[n].astype(F32)
            for row in range(EXT):
                for half in range(2 if row < EXT - 1 else 1):
                    first = SLOT_ROWS * half + EXT * row
                    part = jnp.where(inside, scratch[first : first + G, :], 0.0)
                    at = (first_row + 2 * row + half, pl.ds(first_col, G), slice(None))
                    canvas[at] = canvas[at] + part

        return carry

    lax.fori_loop(0, slot_ref.shape[0], per_slot, 0)
    for chunk in range(per_row):
        first = OUT * chunk + 1
        for row in range(half_rows):
            packed[CHUNK * row : CHUNK * row + G, :] = canvas[row, first : first + G, :]
        out_ref[chunk] = packed[...].astype(BF16)


def fold(ids, received, per_row, half_rows):
    return pl.pallas_call(
        lambda *refs: fold_kernel(per_row, half_rows, *refs),
        in_specs=[
            pl.BlockSpec(memory_space=pltpu.SMEM),
            pl.BlockSpec(memory_space=pltpu.VMEM),
        ],
        out_specs=pl.BlockSpec(memory_space=pltpu.VMEM),
        scratch_shapes=[
            pltpu.VMEM((half_rows, PITCH + 8, LANES), F32),
            pltpu.VMEM((ADJ_ROWS + 8, LANES), F32),
            pltpu.VMEM((CHUNK_ROWS, LANES), F32),
        ],
        out_shape=pltpu.VMEM((per_row, CHUNK_ROWS, LANES), BF16),
        cost_estimate=SMALL,
        name="fold",
    )(ids, on_chip(received))


def finish_kernel(half_rows, terms_ref, up_out, middle_out, down_out, summed, canvas):
    total = terms_ref[0].astype(F32)
    for term in range(1, terms_ref.shape[0]):
        total = total + terms_ref[term].astype(F32)
    summed[...] = total
    near = lax.broadcasted_iota(jnp.int32, (8, LANES), 1) < LANES - SHIFT
    for first in range(0, half_rows, 8):
        count = min(8, half_rows - first)
        starts = [CHUNK * (first + row) for row in range(count)]
        tiles = swap_groups(jnp.stack([summed[start : start + 8, :] for start in starts], 0))
        edges = summed[pl.ds(starts[0] + 8, count, stride=CHUNK), :]
        if count < 8:
            edges = jnp.concatenate([edges, jnp.zeros((8 - count, LANES), F32)], axis=0)
        edges = swap_groups(edges.reshape(1, 8, LANES)).reshape(8, LANES)
        for row in range(count):
            tile = pltpu.roll(tiles[row], LANES - SHIFT, 1)
            edge = pltpu.roll(edges, (LANES - SHIFT - G * row) % LANES, 1)
            start = 8 * (first + row)
            canvas[start : start + 8, :] = jnp.where(near, tile, edge)
    middle = middle_out.shape[0]
    up_out[...] = canvas[:HALO, :].astype(BF16)
    middle_out[...] = canvas[HALO : HALO + middle, :]
    down_out[...] = canvas[HALO + middle : 2 * HALO + middle, :].astype(BF16)


def finish(terms, half_rows, rows):
    rim = pltpu.VMEM((HALO, LANES), BF16)
    vmem = pl.BlockSpec(memory_space=pltpu.VMEM)
    return pl.pallas_call(
        lambda *refs: finish_kernel(half_rows, *refs),
        in_specs=[vmem],
        out_specs=[vmem, vmem, vmem],
        out_shape=[rim, jax.ShapeDtypeStruct((rows, LANES), F32), rim],
        scratch_shapes=[
            pltpu.VMEM((CHUNK_ROWS, LANES), F32),
            pltpu.VMEM((8 * half_rows, LANES), F32),
        ],
        cost_estimate=SMALL,
        name="finish",
    )(on_chip(terms))


def rims_kernel(middle_ref, above_ref, below_ref, out_ref):
    rows = out_ref.shape[0]
    out_ref[...] = middle_ref[...]

    @pl.when(pl.program_id(0) == 0)
    def _():
        out_ref[:HALO, :] = out_ref[:HALO, :] + above_ref[...].astype(F32)

    @pl.when(pl.program_id(0) == 1)
    def _():
        out_ref[rows - HALO :, :] = out_ref[rows - HALO :, :] + below_ref[...].astype(F32)


def add_rims(middle, above, below):
    rows = 32
    last = middle.shape[0] // rows - 1
    block = pl.BlockSpec((rows, LANES), lambda i: (i * last, 0))
    return pl.pallas_call(
        rims_kernel,
        grid=(2,),
        in_specs=[block, whole_vmem(), whole_vmem()],
        out_specs=block,
        out_shape=jax.ShapeDtypeStruct(middle.shape, F32),
        input_output_aliases={0: 0},
        cost_estimate=SMALL,
        name="rims",
    )(middle, on_chip(above), on_chip(below))


def shards(sky_model, exposure_data, pixel_mask, block_owner, block_local, psf_cell, psf_table):
    sky_count = lax.axis_size("sky")
    stripe_rows, stripe_cols = sky_model.shape
    per_row = stripe_cols // B
    block_total = stripe_rows // B * per_row
    piece_count = exposure_data.shape[0]
    owner_sky = block_owner[:, 0]
    code = lax.broadcasted_iota(jnp.int32, (piece_count,), 0) * block_total + block_local
    mine = owner_sky[None, :] == lax.broadcasted_iota(jnp.int32, (sky_count, 1), 0)
    first = jnp.min(jnp.where(mine, code[None, :], piece_count * block_total), axis=1)
    last = jnp.max(jnp.where(mine, code[None, :], -1), axis=1)
    turn = np.arange(CAP)[None, None, :]
    earliest, latest = first[:, None, None], last[:, None, None]
    requests = jnp.where(
        turn == 0,
        jnp.where(latest < 0, -1, earliest % block_total),
        jnp.where(latest > earliest, latest % block_total, -1),
    )
    asked = lax.all_to_all(requests, "sky", split_axis=0, concat_axis=0, tiled=True)

    above = from_behind(sky_model[stripe_rows - HALO :], "sky", 1)
    below = from_behind(sky_model[:HALO], "sky", -1)
    half_rows = (stripe_rows + 2 * HALO + TAIL) // 8
    second = jnp.any(mine & (first[:, None] < code[None, :]), axis=0)
    kernels = padded_kernels(psf_table)
    asked, above, below, second = lax.optimization_barrier((asked, above, below, second))
    blocks = stripe_blocks(sky_model, above, below, half_rows)
    outgoing = cut_patches(asked, blocks, per_row)
    exposure_data, pixel_mask, kernels, second, _ = lax.optimization_barrier(
        (exposure_data, pixel_mask, kernels, second, outgoing)
    )
    slot_index = owner_sky * CAP + second.astype(jnp.int32)
    patches = lax.all_to_all(outgoing, "sky", split_axis=0, concat_axis=0, tiled=True)
    data = regroup(exposure_data, pixel_mask)
    taps = build_taps(kernels)
    adjoints, residuals = pieces(slot_index, psf_cell, patches, taps, data)
    received = lax.all_to_all(adjoints, "sky", split_axis=0, concat_axis=0, tiled=True)
    received, residual = lax.optimization_barrier((received, ungroup(residuals)))

    partial = fold(asked, received, per_row, half_rows)
    terms = lax.all_to_all(partial, "exp", split_axis=0, concat_axis=0, tiled=True)
    up, middle, down = finish(terms, half_rows, stripe_rows)
    from_below = from_behind(up, "sky", -1)
    from_above = from_behind(down, "sky", 1)
    gradient = add_rims(middle, from_above, from_below)
    return (gradient, residual)


def solution(mesh):
    in_specs = (
        P("sky", None),
        P(("sky", "exp"), None, None),
        P(("sky", "exp"), None, None),
        P(("sky", "exp"), None),
        P(("sky", "exp")),
        P(("sky", "exp")),
        P("exp", None),
    )
    out_specs = (P("sky", "exp"), P(("sky", "exp"), None, None))
    return jax.shard_map(shards, mesh=mesh, in_specs=in_specs, out_specs=out_specs, check_vma=False)
```

```python
import jax
import jax.numpy as jnp
from jax import lax
from jax.experimental import pallas as pl
from jax.experimental.pallas import tpu as pltpu
from jax.sharding import PartitionSpec as P

B = 128
PSF = 41
HALO = 20
CAP = 2

G = 16
LANES = 128
OUT = B // G
EXT = 11
REACH = 4
TAIL = 8
BLOCKS = OUT * OUT
PATCH_ROWS = 232
ADJ_ROWS = 240
SLOT_ROWS = 128
PITCH = 72
TILES = 6
RES_LEAD = 40
TAP_ROWS = 48
GROUP = 4
BATCH = 4
SLOTS = 8
CHUNK = 9
CHUNK_ROWS = 352
SHIFT = 4
UNKNOWN = 2.0**100
SMALL = pl.CostEstimate(flops=1000, bytes_accessed=1000, transcendentals=0)
F32 = jnp.float32
BF16 = jnp.bfloat16


def whole_vmem():
    return pl.BlockSpec(memory_space=pltpu.VMEM)


def on_chip(x):
    return pltpu.with_memory_space_constraint(x, pltpu.VMEM)


def from_behind(x, axis, by):
    devices = lax.axis_size(axis)
    pairs = [(i, i + by) for i in range(devices) if 0 <= i + by < devices]
    return lax.ppermute(x, axis, pairs)


def swap_groups(x):
    sub = lax.broadcasted_iota(jnp.int32, x.shape, 1)
    group = lax.broadcasted_iota(jnp.int32, x.shape, 2) // G
    for d in (4, 2, 1):
        sub_bit, group_bit = (sub & d) != 0, (group & d) != 0
        up = pltpu.roll(pltpu.roll(x, 8 - d, 1), G * d, 2)
        down = up if d == 4 else pltpu.roll(pltpu.roll(x, d, 1), LANES - G * d, 2)
        x = jnp.where(sub_bit == group_bit, x, jnp.where(group_bit, up, down))
    return x


def reversed_groups(shift=0):
    source = lax.broadcasted_iota(jnp.int32, (2 * LANES, LANES), 0)
    lane = lax.broadcasted_iota(jnp.int32, (2 * LANES, LANES), 1)
    group = (8 - lane // G) % 8
    return (source == LANES - shift + group * G + lane % G).astype(BF16)


def swap_reversed(x):
    group = lax.broadcasted_iota(jnp.int32, (8, LANES), 1) // G
    tiles = []
    for tile in range(x.shape[0]):
        now = pltpu.roll(x[tile], 0, 1, stride=G, stride_axis=0)
        for d in (1, 2, 4):
            now = jnp.where((group & d) != 0, pltpu.roll(now, 8 - d, 0), now)
        tiles.append(pltpu.roll(now, 0, 1, stride=G, stride_axis=0))
    return jnp.stack(tiles, 0)


def regroup_kernel(data_ref, keep_ref, out_ref):
    def per_piece(p, carry):
        known = jnp.where(keep_ref[p] != 0, data_ref[p].astype(F32), UNKNOWN).astype(BF16)
        turned = jnp.dot(known, reversed_groups()[LANES:], preferred_element_type=F32)
        blocks = swap_reversed(turned.reshape(2 * OUT, 8, LANES)).reshape(OUT, 2, 8, LANES)
        for half in range(2):
            out_ref[p, :, half * LANES : (half + 1) * LANES] = (
                blocks[:, half].reshape(BLOCKS, LANES).astype(BF16)
            )
        return carry

    lax.fori_loop(0, data_ref.shape[0], per_piece, 0, unroll=2)


def regroup(exposure_data, pixel_mask):
    pieces = exposure_data.shape[0]
    block = pl.BlockSpec((BATCH, B, B), lambda p: (p, 0, 0))
    return pl.pallas_call(
        regroup_kernel,
        grid=(pieces // BATCH,),
        in_specs=[block, block],
        out_specs=pl.BlockSpec((BATCH, BLOCKS, 2 * LANES), lambda p: (p, 0, 0)),
        out_shape=jax.ShapeDtypeStruct((pieces, BLOCKS, 2 * LANES), BF16),
        cost_estimate=SMALL,
        name="regroup",
    )(exposure_data, pixel_mask)


def taps_kernel(kernel_ref, out_ref, windows, rows):
    lane = lax.broadcasted_iota(jnp.int32, (G, LANES), 1)
    odd = (lane // G) % 2 == 1
    wide = lax.broadcasted_iota(jnp.int32, (TAP_ROWS, LANES), 1) // (2 * G)
    quarter = lax.broadcasted_iota(jnp.int32, (TILES, LANES), 1) // (2 * G)

    kernel = kernel_ref[0].astype(F32)
    spread = pltpu.roll(kernel, G, 1)
    for t in range(1, REACH):
        spread = jnp.where(wide == t, pltpu.roll(kernel, G * t + G, 1), spread)
    windows[...] = spread
    for parity in range(2):
        picked = [windows[pl.ds(parity + 2 * q, TILES, stride=8), :] for q in range(4)]
        for t in range(REACH):
            row = picked[0] if t == 0 else pltpu.roll(picked[0], 2 * G * (4 - t), 1)
            for q in range(1, 4):
                by = (q - t) % 4
                part = picked[q] if by == 0 else pltpu.roll(picked[q], 2 * G * by, 1)
                row = jnp.where(quarter == q, part, row)
            rows[t, parity, :TILES, :] = row

    def per_shift(t, carry):
        before = [jnp.zeros((G, LANES), F32)] * 8
        for tile in range(TILES):
            even_row, odd_row = (
                jnp.broadcast_to(rows[t, parity, tile : tile + 1, :], (G, LANES))
                for parity in range(2)
            )
            even_row = pltpu.roll(even_row, LANES - G, 1, stride=1, stride_axis=0)
            odd_row = pltpu.roll(odd_row, 0, 1, stride=1, stride_axis=0)
            now = jnp.where(odd, odd_row, even_row)
            turns = [now] + [pltpu.roll(now, G * phase, 1) for phase in range(1, 8)]
            for phase in range(8):
                part = turns[phase]
                if phase > 0:
                    part = jnp.where(lane < G * phase, before[phase], part)
                start = pl.multiple_of(t * LANES + phase * G, G)
                lanes = slice(tile * LANES, (tile + 1) * LANES)
                out_ref[0, pl.ds(start, G), lanes] = part.astype(BF16)
            before = turns
        return carry

    lax.fori_loop(0, REACH, per_shift, 0, unroll=REACH)


def padded_kernels(table):
    kernels = table.reshape(table.shape[0], PSF, PSF)
    return jnp.pad(kernels, ((0, 0), (0, TAP_ROWS - PSF), (0, LANES - PSF)))


def build_taps(kernels):
    cells = kernels.shape[0]
    return pl.pallas_call(
        taps_kernel,
        grid=(cells,),
        in_specs=[pl.BlockSpec((1, TAP_ROWS, LANES), lambda c: (c, 0, 0))],
        out_specs=pl.BlockSpec((1, REACH * LANES, TILES * LANES), lambda c: (c, 0, 0)),
        out_shape=jax.ShapeDtypeStruct((cells, REACH * LANES, TILES * LANES), BF16),
        scratch_shapes=[
            pltpu.VMEM((TAP_ROWS, LANES), F32),
            pltpu.VMEM((REACH, 2, 8, LANES), F32),
        ],
        cost_estimate=SMALL,
        name="taps",
    )(kernels)


def moved_tiles(pixels):
    rows, columns = pixels.shape
    turn = reversed_groups(HALO)
    empty = jnp.zeros((rows, LANES), BF16)
    tiles = [pixels[:, at : at + LANES] for at in range(0, columns, LANES)]
    return [
        jnp.dot(jnp.concatenate([old, now], axis=1), turn, preferred_element_type=F32)
        for old, now in zip([empty] + tiles, tiles + [empty])
    ]


def blocks_kernel(stripe_ref, above_ref, below_ref, out_ref, pixels):
    first = 0
    for ref in (above_ref, stripe_ref, below_ref):
        rows = ref.shape[0]
        for tile, moved in enumerate(moved_tiles(ref[...])):
            pixels[first : first + rows, tile * LANES : (tile + 1) * LANES] = moved
        first += rows
    pixels[first:, :] = jnp.zeros((TAIL, PITCH * G), F32)
    for row in range(out_ref.shape[0]):
        tiles = [
            pixels[8 * row : 8 * row + 8, at : at + LANES] for at in range(0, PITCH * G, LANES)
        ]
        out_ref[row] = swap_reversed(jnp.stack(tiles, 0)).reshape(PITCH, LANES)


def stripe_blocks(stripe, above, below, half_rows):
    return pl.pallas_call(
        blocks_kernel,
        in_specs=[whole_vmem(), whole_vmem(), whole_vmem()],
        out_specs=whole_vmem(),
        out_shape=pltpu.VMEM((half_rows, PITCH, LANES), F32),
        scratch_shapes=[pltpu.VMEM((8 * half_rows, PITCH * G), F32)],
        cost_estimate=SMALL,
        name="blocks",
    )(stripe, on_chip(above), on_chip(below))


def cut_kernel(per_row, ids_ref, blocks_ref, out_ref, scratch):
    step = pl.program_id(0)

    def per_slot(n, carry):
        at = step * SLOTS + n
        wanted = ids_ref[at // CAP, 0, at % CAP]

        @pl.when(wanted >= 0)
        def _():
            first_row = wanted // per_row * (2 * OUT)
            first_col = pl.multiple_of(wanted % per_row * OUT, 8)
            for row in range(2 * EXT - 1):
                part = blocks_ref[first_row + row, pl.ds(first_col, G), :]
                scratch[EXT * row : EXT * row + G, :] = part
            out_ref[n] = scratch[:PATCH_ROWS, :].astype(BF16)

        return carry

    lax.fori_loop(0, SLOTS, per_slot, 0)


def cut_patches(ids, blocks, per_row):
    slots = ids.shape[0] * CAP
    return pl.pallas_call(
        lambda *refs: cut_kernel(per_row, *refs),
        grid_spec=pltpu.PrefetchScalarGridSpec(
            num_scalar_prefetch=1,
            grid=(slots // SLOTS,),
            in_specs=[whole_vmem()],
            out_specs=pl.BlockSpec((SLOTS, PATCH_ROWS, LANES), lambda n, ids: (n, 0, 0)),
            scratch_shapes=[pltpu.VMEM((PATCH_ROWS + 8, LANES), F32)],
        ),
        out_shape=jax.ShapeDtypeStruct((slots, PATCH_ROWS, LANES), BF16),
        cost_estimate=SMALL,
        name="cut",
    )(ids, on_chip(blocks))


def block_taps(taps_ref, s, t):
    taps = slice(t * LANES, (t + 1) * LANES)
    upper = taps_ref[0, taps, 2 * s * LANES : (2 * s + 2) * LANES]
    if s == 0:
        lower = jnp.concatenate(
            [jnp.zeros((LANES, LANES), BF16), taps_ref[0, taps, 0:LANES]], axis=1
        )
    else:
        lower = taps_ref[0, taps, (2 * s - 1) * LANES : (2 * s + 1) * LANES]
    return jnp.concatenate([upper, lower], axis=0)


def last_taps(taps_ref, t):
    return taps_ref[0, t * LANES : (t + 1) * LANES, (TILES - 1) * LANES :]


def correlate(read, taps_ref):
    across = (((1,), (1,)), ((), ()))
    total = jnp.zeros((2 * BLOCKS, LANES), F32)
    for t in range(REACH):
        for d in range(TILES // 2):
            taps = taps_ref[0, t * LANES : (t + 1) * LANES, 2 * d * LANES : (2 * d + 2) * LANES]
            total = total + lax.dot_general(
                read(d, t), taps, across, preferred_element_type=F32
            )
    return jnp.concatenate([total[:BLOCKS], total[BLOCKS:]], axis=1)


def convolve(read, taps_ref, rows):
    total = jnp.zeros((rows, 2 * LANES), F32)
    for t in range(REACH):
        for s in range(REACH - 1):
            total = total + jnp.dot(
                read(s, t), block_taps(taps_ref, s, t), preferred_element_type=F32
            )
    last = jnp.zeros((rows, LANES), F32)
    for t in range(0, REACH, 2):
        field = [read(REACH - 1, t + i)[:, LANES:] for i in range(2)]
        taps = [last_taps(taps_ref, t + i) for i in range(2)]
        last = last + jnp.dot(
            jnp.concatenate(field, axis=1),
            jnp.concatenate(taps, axis=0),
            preferred_element_type=F32,
        )
    return jnp.concatenate([total[:, :LANES] + last, total[:, LANES:]], axis=1)


def pieces_kernel(slot_ref, cell_ref, patch_ref, *refs):
    taps, refs = refs[:GROUP], refs[GROUP:]
    data_ref, adjoints, res_out, field, resid, adj_slots, sems = refs
    step = pl.program_id(0)
    slots = lax.rem(step, 2)

    @pl.when(step == 0)
    def _():
        resid[...] = jnp.zeros_like(resid)

    def sent(step):
        at = lax.rem(step, 2)
        return [
            pltpu.make_async_copy(
                adj_slots.at[at, i], adjoints.at[slot_ref[GROUP * step + i]], sems.at[at, i]
            )
            for i in range(GROUP)
        ]

    @pl.when(step >= 2)
    def _():
        for copy in sent(step - 2):
            copy.wait()

    def forward(i, taps_ref, field):
        field[...] = patch_ref[slot_ref[GROUP * step + i]].astype(F32)

        def read_patch(d, t):
            parts = []
            for half in range(2):
                for row in range(OUT):
                    at = EXT * (2 * (row + d) + half) + t
                    pair = [field[at : at + OUT, :], field[at + EXT : at + EXT + OUT, :]]
                    parts.append(jnp.concatenate(pair, axis=1))
            return jnp.concatenate(parts, axis=0).astype(BF16)

        return correlate(read_patch, taps_ref)

    def compare(i, predicted, resid):
        observed = data_ref[i].astype(F32)
        residual = jnp.where(observed < UNKNOWN, predicted - observed, 0.0).astype(BF16)
        res_out[i] = residual
        wide = residual.astype(F32)
        for row in range(OUT):
            first = RES_LEAD + EXT * row
            resid[first : first + OUT, :] = wide[OUT * row : OUT * (row + 1)]

    def backward(i, taps_ref, resid):
        def read_residual(s, t):
            return resid[pl.ds(RES_LEAD - EXT * s - t, SLOT_ROWS), :].astype(BF16)

        adjoint = convolve(read_residual, taps_ref, SLOT_ROWS).astype(BF16)
        adj_slots[slots, i, :SLOT_ROWS] = adjoint[:, :LANES]
        adj_slots[slots, i, SLOT_ROWS:] = adjoint[: ADJ_ROWS - SLOT_ROWS, LANES:]

    for i in range(GROUP):
        compare(i, forward(i, taps[i], field.at[i]), resid.at[i])
    for i in range(GROUP):
        backward(i, taps[i], resid.at[i])
    for copy in sent(step):
        copy.start()

    @pl.when(step == pl.num_programs(0) - 1)
    def _():
        for copy in sent(step - 1) + sent(step):
            copy.wait()


def pieces(slots, cells, patches, taps, data):
    count = data.shape[0]
    cell = [
        pl.BlockSpec(
            (1, REACH * LANES, TILES * LANES),
            lambda p, slots, cells, i=i: (cells[GROUP * p + i], 0, 0),
        )
        for i in range(GROUP)
    ]
    block = pl.BlockSpec((GROUP, BLOCKS, 2 * LANES), lambda p, slots, cells: (p, 0, 0))
    return pl.pallas_call(
        pieces_kernel,
        grid_spec=pltpu.PrefetchScalarGridSpec(
            num_scalar_prefetch=2,
            grid=(count // GROUP,),
            in_specs=[whole_vmem(), *cell, block],
            out_specs=[pl.BlockSpec(memory_space=pltpu.HBM), block],
            scratch_shapes=[
                pltpu.VMEM((GROUP, PATCH_ROWS, LANES), F32),
                pltpu.VMEM((GROUP, RES_LEAD + SLOT_ROWS, 2 * LANES), F32),
                pltpu.VMEM((2, GROUP, ADJ_ROWS, LANES), BF16),
                pltpu.SemaphoreType.DMA((2, GROUP)),
            ],
        ),
        out_shape=[
            jax.ShapeDtypeStruct((patches.shape[0], ADJ_ROWS, LANES), BF16),
            jax.ShapeDtypeStruct(data.shape, BF16),
        ],
        cost_estimate=SMALL,
        name="pieces",
    )(slots, cells, on_chip(patches), *[taps] * GROUP, data)


def ungroup_kernel(res_ref, out_ref):
    turn = reversed_groups()[LANES:]

    def per_piece(p, carry):
        halves = [
            jnp.dot(
                res_ref[p, :, half * LANES : (half + 1) * LANES], turn, preferred_element_type=F32
            ).reshape(OUT, 8, LANES)
            for half in range(2)
        ]
        pixels = swap_reversed(jnp.stack(halves, 1).reshape(2 * OUT, 8, LANES))
        out_ref[p] = pixels.reshape(B, LANES).astype(BF16)
        return carry

    lax.fori_loop(0, res_ref.shape[0], per_piece, 0)


def ungroup(residual):
    count = residual.shape[0]
    return pl.pallas_call(
        ungroup_kernel,
        grid=(count // BATCH,),
        in_specs=[pl.BlockSpec((BATCH, BLOCKS, 2 * LANES), lambda p: (p, 0, 0))],
        out_specs=pl.BlockSpec((BATCH, B, B), lambda p: (p, 0, 0)),
        out_shape=jax.ShapeDtypeStruct((count, B, B), BF16),
        cost_estimate=SMALL,
        name="ungroup",
    )(residual)


def fold_kernel(per_row, half_rows, ids_ref, slot_ref, out_ref, canvas, scratch, packed):
    canvas[...] = jnp.zeros_like(canvas)
    inside = lax.broadcasted_iota(jnp.int32, (G, LANES), 0) < EXT

    def per_slot(n, carry):
        named = ids_ref[n // CAP, 0, n % CAP]

        @pl.when(named >= 0)
        def _():
            first_row = named // per_row * (2 * OUT)
            first_col = pl.multiple_of(named % per_row * OUT, 8)
            scratch[:ADJ_ROWS, :] = slot_ref[n].astype(F32)
            for row in range(EXT):
                for half in range(2 if row < EXT - 1 else 1):
                    first = SLOT_ROWS * half + EXT * row
                    part = jnp.where(inside, scratch[first : first + G, :], 0.0)
                    at = (first_row + 2 * row + half, pl.ds(first_col, G), slice(None))
                    canvas[at] = canvas[at] + part

        return carry

    lax.fori_loop(0, slot_ref.shape[0], per_slot, 0)
    for chunk in range(per_row):
        first = OUT * chunk + 1
        for row in range(half_rows):
            packed[CHUNK * row : CHUNK * row + G, :] = canvas[row, first : first + G, :]
        out_ref[chunk] = packed[...].astype(BF16)


def fold(ids, received, per_row, half_rows):
    return pl.pallas_call(
        lambda *refs: fold_kernel(per_row, half_rows, *refs),
        in_specs=[
            pl.BlockSpec(memory_space=pltpu.SMEM),
            pl.BlockSpec(memory_space=pltpu.VMEM),
        ],
        out_specs=pl.BlockSpec(memory_space=pltpu.VMEM),
        scratch_shapes=[
            pltpu.VMEM((half_rows, PITCH + 8, LANES), F32),
            pltpu.VMEM((ADJ_ROWS + 8, LANES), F32),
            pltpu.VMEM((CHUNK_ROWS, LANES), F32),
        ],
        out_shape=pltpu.VMEM((per_row, CHUNK_ROWS, LANES), BF16),
        cost_estimate=SMALL,
        name="fold",
    )(ids, on_chip(received))


def finish_kernel(half_rows, terms_ref, up_out, middle_out, down_out, summed, canvas):
    total = terms_ref[0].astype(F32)
    for term in range(1, terms_ref.shape[0]):
        total = total + terms_ref[term].astype(F32)
    summed[...] = total
    near = lax.broadcasted_iota(jnp.int32, (8, LANES), 1) < LANES - SHIFT
    for first in range(0, half_rows, 8):
        count = min(8, half_rows - first)
        starts = [CHUNK * (first + row) for row in range(count)]
        tiles = swap_groups(jnp.stack([summed[start : start + 8, :] for start in starts], 0))
        edges = summed[pl.ds(starts[0] + 8, count, stride=CHUNK), :]
        if count < 8:
            edges = jnp.concatenate([edges, jnp.zeros((8 - count, LANES), F32)], axis=0)
        edges = swap_groups(edges.reshape(1, 8, LANES)).reshape(8, LANES)
        for row in range(count):
            tile = pltpu.roll(tiles[row], LANES - SHIFT, 1)
            edge = pltpu.roll(edges, (LANES - SHIFT - G * row) % LANES, 1)
            start = 8 * (first + row)
            canvas[start : start + 8, :] = jnp.where(near, tile, edge)
    middle = middle_out.shape[0]
    up_out[...] = canvas[:HALO, :].astype(BF16)
    middle_out[...] = canvas[HALO : HALO + middle, :]
    down_out[...] = canvas[HALO + middle : 2 * HALO + middle, :].astype(BF16)


def finish(terms, half_rows, rows):
    rim = pltpu.VMEM((HALO, LANES), BF16)
    vmem = pl.BlockSpec(memory_space=pltpu.VMEM)
    return pl.pallas_call(
        lambda *refs: finish_kernel(half_rows, *refs),
        in_specs=[vmem],
        out_specs=[vmem, vmem, vmem],
        out_shape=[rim, jax.ShapeDtypeStruct((rows, LANES), F32), rim],
        scratch_shapes=[
            pltpu.VMEM((CHUNK_ROWS, LANES), F32),
            pltpu.VMEM((8 * half_rows, LANES), F32),
        ],
        cost_estimate=SMALL,
        name="finish",
    )(on_chip(terms))


def rims_kernel(middle_ref, above_ref, below_ref, out_ref):
    rows = out_ref.shape[0]
    out_ref[...] = middle_ref[...]

    @pl.when(pl.program_id(0) == 0)
    def _():
        out_ref[:HALO, :] = out_ref[:HALO, :] + above_ref[...].astype(F32)

    @pl.when(pl.program_id(0) == 1)
    def _():
        out_ref[rows - HALO :, :] = out_ref[rows - HALO :, :] + below_ref[...].astype(F32)


def add_rims(middle, above, below):
    rows = 32
    last = middle.shape[0] // rows - 1
    block = pl.BlockSpec((rows, LANES), lambda i: (i * last, 0))
    return pl.pallas_call(
        rims_kernel,
        grid=(2,),
        in_specs=[block, whole_vmem(), whole_vmem()],
        out_specs=block,
        out_shape=jax.ShapeDtypeStruct(middle.shape, F32),
        input_output_aliases={0: 0},
        cost_estimate=SMALL,
        name="rims",
    )(middle, on_chip(above), on_chip(below))


def shards(sky_model, exposure_data, pixel_mask, block_owner, block_local, psf_cell, psf_table):
    sky_count = lax.axis_size("sky")
    stripe_rows, stripe_cols = sky_model.shape
    per_row = stripe_cols // B
    block_total = stripe_rows // B * per_row
    piece_count = exposure_data.shape[0]
    owner_sky = block_owner[:, 0]
    code = lax.broadcasted_iota(jnp.int32, (piece_count,), 0) * block_total + block_local
    mine = owner_sky[None, :] == lax.broadcasted_iota(jnp.int32, (sky_count, 1), 0)
    first = jnp.min(jnp.where(mine, code[None, :], piece_count * block_total), axis=1)
    last = jnp.max(jnp.where(mine, code[None, :], -1), axis=1)
    requests = jnp.stack(
        [
            jnp.where(last < 0, -1, first % block_total),
            jnp.where(last > first, last % block_total, -1),
        ],
        axis=1,
    )
    asked = lax.all_to_all(
        requests[:, None, :], "sky", split_axis=0, concat_axis=0, tiled=True
    )
    above = from_behind(sky_model[stripe_rows - HALO :], "sky", 1)
    below = from_behind(sky_model[:HALO], "sky", -1)
    half_rows = (stripe_rows + 2 * HALO + TAIL) // 8
    second = jnp.any(mine & (first[:, None] < code[None, :]), axis=0)
    slot_index = owner_sky * CAP + second.astype(jnp.int32)
    kernels = padded_kernels(psf_table)
    asked, above, below, slot_index = lax.optimization_barrier((asked, above, below, slot_index))
    blocks = stripe_blocks(sky_model, above, below, half_rows)
    outgoing = cut_patches(asked, blocks, per_row)
    exposure_data, pixel_mask, kernels, _ = lax.optimization_barrier(
        (exposure_data, pixel_mask, kernels, outgoing)
    )
    patches = lax.all_to_all(outgoing, "sky", split_axis=0, concat_axis=0, tiled=True)
    data = regroup(exposure_data, pixel_mask)
    taps = build_taps(kernels)
    adjoints, residuals = pieces(slot_index, psf_cell, patches, taps, data)
    received = lax.all_to_all(adjoints, "sky", split_axis=0, concat_axis=0, tiled=True)
    received, residual = lax.optimization_barrier((received, ungroup(residuals)))

    partial = fold(asked, received, per_row, half_rows)
    terms = lax.all_to_all(partial, "exp", split_axis=0, concat_axis=0, tiled=True)
    up, middle, down = finish(terms, half_rows, stripe_rows)
    from_below = from_behind(up, "sky", -1)
    from_above = from_behind(down, "sky", 1)
    gradient = add_rims(middle, from_above, from_below)
    return (gradient, residual)


def solution(mesh):
    in_specs = (
        P("sky", None),
        P(("sky", "exp"), None, None),
        P(("sky", "exp"), None, None),
        P(("sky", "exp"), None),
        P(("sky", "exp")),
        P(("sky", "exp")),
        P("exp", None),
    )
    out_specs = (P("sky", "exp"), P(("sky", "exp"), None, None))
    return jax.shard_map(shards, mesh=mesh, in_specs=in_specs, out_specs=out_specs, check_vma=False)
```

```python
import jax
import jax.numpy as jnp
from jax import lax
from jax.experimental import pallas as pl
from jax.experimental.pallas import tpu as pltpu
from jax.sharding import PartitionSpec as P

B = 128
PSF = 41
HALO = 20
CAP = 2

G = 16
LANES = 128
OUT = B // G
EXT = 11
REACH = 4
TAIL = 8
BLOCKS = OUT * OUT
PATCH_ROWS = 232
ADJ_ROWS = 240
SLOT_ROWS = 128
PITCH = 72
TILES = 6
RES_LEAD = 40
TAP_ROWS = 48
GROUP = 4
BATCH = 4
SLOTS = 8
CHUNK = 9
CHUNK_ROWS = 352
SHIFT = 4
UNKNOWN = 2.0**100
SMALL = pl.CostEstimate(flops=1000, bytes_accessed=1000, transcendentals=0)
F32 = jnp.float32
BF16 = jnp.bfloat16


def whole_vmem():
    return pl.BlockSpec(memory_space=pltpu.VMEM)


def on_chip(x):
    return pltpu.with_memory_space_constraint(x, pltpu.VMEM)


def from_behind(x, axis, by):
    devices = lax.axis_size(axis)
    pairs = [(i, i + by) for i in range(devices) if 0 <= i + by < devices]
    return lax.ppermute(x, axis, pairs)


def swap_groups(x):
    sub = lax.broadcasted_iota(jnp.int32, x.shape, 1)
    group = lax.broadcasted_iota(jnp.int32, x.shape, 2) // G
    for d in (4, 2, 1):
        sub_bit, group_bit = (sub & d) != 0, (group & d) != 0
        up = pltpu.roll(pltpu.roll(x, 8 - d, 1), G * d, 2)
        down = up if d == 4 else pltpu.roll(pltpu.roll(x, d, 1), LANES - G * d, 2)
        x = jnp.where(sub_bit == group_bit, x, jnp.where(group_bit, up, down))
    return x


def reversed_groups(shift=0):
    source = lax.broadcasted_iota(jnp.int32, (2 * LANES, LANES), 0)
    lane = lax.broadcasted_iota(jnp.int32, (2 * LANES, LANES), 1)
    group = (8 - lane // G) % 8
    return (source == LANES - shift + group * G + lane % G).astype(BF16)


def swap_reversed(x):
    group = lax.broadcasted_iota(jnp.int32, (8, LANES), 1) // G
    tiles = []
    for tile in range(x.shape[0]):
        now = pltpu.roll(x[tile], 0, 1, stride=G, stride_axis=0)
        for d in (1, 2, 4):
            now = jnp.where((group & d) != 0, pltpu.roll(now, 8 - d, 0), now)
        tiles.append(pltpu.roll(now, 0, 1, stride=G, stride_axis=0))
    return jnp.stack(tiles, 0)


def regroup_kernel(data_ref, keep_ref, out_ref):
    def per_piece(p, carry):
        known = jnp.where(keep_ref[p] != 0, data_ref[p].astype(F32), UNKNOWN).astype(BF16)
        turned = jnp.dot(known, reversed_groups()[LANES:], preferred_element_type=F32)
        blocks = swap_reversed(turned.reshape(2 * OUT, 8, LANES)).reshape(OUT, 2, 8, LANES)
        for half in range(2):
            out_ref[p, :, half * LANES : (half + 1) * LANES] = (
                blocks[:, half].reshape(BLOCKS, LANES).astype(BF16)
            )
        return carry

    lax.fori_loop(0, data_ref.shape[0], per_piece, 0, unroll=2)


def regroup(exposure_data, pixel_mask):
    pieces = exposure_data.shape[0]
    block = pl.BlockSpec((BATCH, B, B), lambda p: (p, 0, 0))
    return pl.pallas_call(
        regroup_kernel,
        grid=(pieces // BATCH,),
        in_specs=[block, block],
        out_specs=pl.BlockSpec((BATCH, BLOCKS, 2 * LANES), lambda p: (p, 0, 0)),
        out_shape=jax.ShapeDtypeStruct((pieces, BLOCKS, 2 * LANES), BF16),
        cost_estimate=SMALL,
        name="regroup",
    )(exposure_data, pixel_mask)


def taps_kernel(kernel_ref, out_ref, windows, rows):
    lane = lax.broadcasted_iota(jnp.int32, (G, LANES), 1)
    odd = (lane // G) % 2 == 1
    wide = lax.broadcasted_iota(jnp.int32, (TAP_ROWS, LANES), 1) // (2 * G)
    quarter = lax.broadcasted_iota(jnp.int32, (TILES, LANES), 1) // (2 * G)

    kernel = kernel_ref[0].astype(F32)
    spread = pltpu.roll(kernel, G, 1)
    for t in range(1, REACH):
        spread = jnp.where(wide == t, pltpu.roll(kernel, G * t + G, 1), spread)
    windows[...] = spread
    for parity in range(2):
        picked = [windows[pl.ds(parity + 2 * q, TILES, stride=8), :] for q in range(4)]
        for t in range(REACH):
            row = picked[0] if t == 0 else pltpu.roll(picked[0], 2 * G * (4 - t), 1)
            for q in range(1, 4):
                by = (q - t) % 4
                part = picked[q] if by == 0 else pltpu.roll(picked[q], 2 * G * by, 1)
                row = jnp.where(quarter == q, part, row)
            rows[t, parity, :TILES, :] = row

    def per_shift(t, carry):
        before = [jnp.zeros((G, LANES), F32)] * 8
        for tile in range(TILES):
            even_row, odd_row = (
                jnp.broadcast_to(rows[t, parity, tile : tile + 1, :], (G, LANES))
                for parity in range(2)
            )
            even_row = pltpu.roll(even_row, LANES - G, 1, stride=1, stride_axis=0)
            odd_row = pltpu.roll(odd_row, 0, 1, stride=1, stride_axis=0)
            now = jnp.where(odd, odd_row, even_row)
            turns = [now] + [pltpu.roll(now, G * phase, 1) for phase in range(1, 8)]
            for phase in range(8):
                part = turns[phase]
                if phase > 0:
                    part = jnp.where(lane < G * phase, before[phase], part)
                start = pl.multiple_of(t * LANES + phase * G, G)
                lanes = slice(tile * LANES, (tile + 1) * LANES)
                out_ref[0, pl.ds(start, G), lanes] = part.astype(BF16)
            before = turns
        return carry

    lax.fori_loop(0, REACH, per_shift, 0)


def padded_kernels(table):
    kernels = table.reshape(table.shape[0], PSF, PSF)
    return jnp.pad(kernels, ((0, 0), (0, TAP_ROWS - PSF), (0, LANES - PSF)))


def build_taps(kernels):
    cells = kernels.shape[0]
    return pl.pallas_call(
        taps_kernel,
        grid=(cells,),
        in_specs=[pl.BlockSpec((1, TAP_ROWS, LANES), lambda c: (c, 0, 0))],
        out_specs=pl.BlockSpec((1, REACH * LANES, TILES * LANES), lambda c: (c, 0, 0)),
        out_shape=jax.ShapeDtypeStruct((cells, REACH * LANES, TILES * LANES), BF16),
        scratch_shapes=[
            pltpu.VMEM((TAP_ROWS, LANES), F32),
            pltpu.VMEM((REACH, 2, 8, LANES), F32),
        ],
        cost_estimate=SMALL,
        name="taps",
    )(kernels)


def moved_tiles(pixels):
    rows, columns = pixels.shape
    turn = reversed_groups(HALO)
    empty = jnp.zeros((rows, LANES), BF16)
    tiles = [pixels[:, at : at + LANES] for at in range(0, columns, LANES)]
    return [
        jnp.dot(jnp.concatenate([old, now], axis=1), turn, preferred_element_type=F32)
        for old, now in zip([empty] + tiles, tiles + [empty])
    ]


def blocks_kernel(stripe_ref, above_ref, below_ref, out_ref, pixels):
    first = 0
    for ref in (above_ref, stripe_ref, below_ref):
        rows = ref.shape[0]
        for tile, moved in enumerate(moved_tiles(ref[...])):
            pixels[first : first + rows, tile * LANES : (tile + 1) * LANES] = moved
        first += rows
    pixels[first:, :] = jnp.zeros((TAIL, PITCH * G), F32)
    for row in range(out_ref.shape[0]):
        tiles = [
            pixels[8 * row : 8 * row + 8, at : at + LANES] for at in range(0, PITCH * G, LANES)
        ]
        out_ref[row] = swap_reversed(jnp.stack(tiles, 0)).reshape(PITCH, LANES)


def stripe_blocks(stripe, above, below, half_rows):
    return pl.pallas_call(
        blocks_kernel,
        in_specs=[whole_vmem(), whole_vmem(), whole_vmem()],
        out_specs=whole_vmem(),
        out_shape=pltpu.VMEM((half_rows, PITCH, LANES), F32),
        scratch_shapes=[pltpu.VMEM((8 * half_rows, PITCH * G), F32)],
        cost_estimate=SMALL,
        name="blocks",
    )(stripe, on_chip(above), on_chip(below))


def cut_kernel(per_row, ids_ref, blocks_ref, out_ref, scratch):
    step = pl.program_id(0)

    def per_slot(n, carry):
        at = step * SLOTS + n
        wanted = ids_ref[at // CAP, 0, at % CAP]

        @pl.when(wanted >= 0)
        def _():
            first_row = wanted // per_row * (2 * OUT)
            first_col = pl.multiple_of(wanted % per_row * OUT, 8)
            for row in range(2 * EXT - 1):
                part = blocks_ref[first_row + row, pl.ds(first_col, G), :]
                scratch[EXT * row : EXT * row + G, :] = part
            out_ref[n] = scratch[:PATCH_ROWS, :].astype(BF16)

        return carry

    lax.fori_loop(0, SLOTS, per_slot, 0)


def cut_patches(ids, blocks, per_row):
    slots = ids.shape[0] * CAP
    return pl.pallas_call(
        lambda *refs: cut_kernel(per_row, *refs),
        grid_spec=pltpu.PrefetchScalarGridSpec(
            num_scalar_prefetch=1,
            grid=(slots // SLOTS,),
            in_specs=[whole_vmem()],
            out_specs=pl.BlockSpec((SLOTS, PATCH_ROWS, LANES), lambda n, ids: (n, 0, 0)),
            scratch_shapes=[pltpu.VMEM((PATCH_ROWS + 8, LANES), F32)],
        ),
        out_shape=jax.ShapeDtypeStruct((slots, PATCH_ROWS, LANES), BF16),
        cost_estimate=SMALL,
        name="cut",
    )(ids, on_chip(blocks))


def block_taps(taps_ref, s, t):
    taps = slice(t * LANES, (t + 1) * LANES)
    upper = taps_ref[0, taps, 2 * s * LANES : (2 * s + 2) * LANES]
    if s == 0:
        lower = jnp.concatenate(
            [jnp.zeros((LANES, LANES), BF16), taps_ref[0, taps, 0:LANES]], axis=1
        )
    else:
        lower = taps_ref[0, taps, (2 * s - 1) * LANES : (2 * s + 1) * LANES]
    return jnp.concatenate([upper, lower], axis=0)


def last_taps(taps_ref, t):
    return taps_ref[0, t * LANES : (t + 1) * LANES, (TILES - 1) * LANES :]


def correlate(read, taps_ref):
    across = (((1,), (1,)), ((), ()))
    total = jnp.zeros((2 * BLOCKS, LANES), F32)
    for t in range(REACH):
        for d in range(TILES // 2):
            taps = taps_ref[0, t * LANES : (t + 1) * LANES, 2 * d * LANES : (2 * d + 2) * LANES]
            total = total + lax.dot_general(
                read(d, t), taps, across, preferred_element_type=F32
            )
    return jnp.concatenate([total[:BLOCKS], total[BLOCKS:]], axis=1)


def convolve(read, taps_ref, rows):
    total = jnp.zeros((rows, 2 * LANES), F32)
    for t in range(REACH):
        for s in range(REACH - 1):
            total = total + jnp.dot(
                read(s, t), block_taps(taps_ref, s, t), preferred_element_type=F32
            )
    last = jnp.zeros((rows, LANES), F32)
    for t in range(0, REACH, 2):
        field = [read(REACH - 1, t + i)[:, LANES:] for i in range(2)]
        taps = [last_taps(taps_ref, t + i) for i in range(2)]
        last = last + jnp.dot(
            jnp.concatenate(field, axis=1),
            jnp.concatenate(taps, axis=0),
            preferred_element_type=F32,
        )
    return jnp.concatenate([total[:, :LANES] + last, total[:, LANES:]], axis=1)


def pieces_kernel(slot_ref, cell_ref, patch_ref, *refs):
    taps, refs = refs[:GROUP], refs[GROUP:]
    data_ref, adjoints, res_out, field, resid, adj_slots, sems = refs
    step = pl.program_id(0)
    slots = lax.rem(step, 2)

    @pl.when(step == 0)
    def _():
        resid[...] = jnp.zeros_like(resid)

    def sent(step):
        at = lax.rem(step, 2)
        return [
            pltpu.make_async_copy(
                adj_slots.at[at, i], adjoints.at[slot_ref[GROUP * step + i]], sems.at[at, i]
            )
            for i in range(GROUP)
        ]

    @pl.when(step >= 2)
    def _():
        for copy in sent(step - 2):
            copy.wait()

    def forward(i, taps_ref, field):
        field[...] = patch_ref[slot_ref[GROUP * step + i]].astype(F32)

        def read_patch(d, t):
            parts = []
            for half in range(2):
                for row in range(OUT):
                    at = EXT * (2 * (row + d) + half) + t
                    pair = [field[at : at + OUT, :], field[at + EXT : at + EXT + OUT, :]]
                    parts.append(jnp.concatenate(pair, axis=1))
            return jnp.concatenate(parts, axis=0).astype(BF16)

        return correlate(read_patch, taps_ref)

    def compare(i, predicted, resid):
        observed = data_ref[i].astype(F32)
        residual = jnp.where(observed < UNKNOWN, predicted - observed, 0.0).astype(BF16)
        res_out[i] = residual
        wide = residual.astype(F32)
        for row in range(OUT):
            first = RES_LEAD + EXT * row
            resid[first : first + OUT, :] = wide[OUT * row : OUT * (row + 1)]

    def backward(i, taps_ref, resid):
        def read_residual(s, t):
            return resid[pl.ds(RES_LEAD - EXT * s - t, SLOT_ROWS), :].astype(BF16)

        adjoint = convolve(read_residual, taps_ref, SLOT_ROWS).astype(BF16)
        adj_slots[slots, i, :SLOT_ROWS] = adjoint[:, :LANES]
        adj_slots[slots, i, SLOT_ROWS:] = adjoint[: ADJ_ROWS - SLOT_ROWS, LANES:]

    for i in range(GROUP):
        compare(i, forward(i, taps[i], field.at[i]), resid.at[i])
    for i in range(GROUP):
        backward(i, taps[i], resid.at[i])
    for copy in sent(step):
        copy.start()

    @pl.when(step == pl.num_programs(0) - 1)
    def _():
        for copy in sent(step - 1) + sent(step):
            copy.wait()


def pieces(slots, cells, patches, taps, data):
    count = data.shape[0]
    cell = [
        pl.BlockSpec(
            (1, REACH * LANES, TILES * LANES),
            lambda p, slots, cells, i=i: (cells[GROUP * p + i], 0, 0),
        )
        for i in range(GROUP)
    ]
    block = pl.BlockSpec((GROUP, BLOCKS, 2 * LANES), lambda p, slots, cells: (p, 0, 0))
    return pl.pallas_call(
        pieces_kernel,
        grid_spec=pltpu.PrefetchScalarGridSpec(
            num_scalar_prefetch=2,
            grid=(count // GROUP,),
            in_specs=[whole_vmem(), *cell, block],
            out_specs=[pl.BlockSpec(memory_space=pltpu.HBM), block],
            scratch_shapes=[
                pltpu.VMEM((GROUP, PATCH_ROWS, LANES), F32),
                pltpu.VMEM((GROUP, RES_LEAD + SLOT_ROWS, 2 * LANES), F32),
                pltpu.VMEM((2, GROUP, ADJ_ROWS, LANES), BF16),
                pltpu.SemaphoreType.DMA((2, GROUP)),
            ],
        ),
        out_shape=[
            jax.ShapeDtypeStruct((patches.shape[0], ADJ_ROWS, LANES), BF16),
            jax.ShapeDtypeStruct(data.shape, BF16),
        ],
        cost_estimate=SMALL,
        name="pieces",
    )(slots, cells, on_chip(patches), *[taps] * GROUP, data)


def ungroup_kernel(res_ref, out_ref):
    turn = reversed_groups()[LANES:]

    def per_piece(p, carry):
        halves = [
            jnp.dot(
                res_ref[p, :, half * LANES : (half + 1) * LANES], turn, preferred_element_type=F32
            ).reshape(OUT, 8, LANES)
            for half in range(2)
        ]
        pixels = swap_reversed(jnp.stack(halves, 1).reshape(2 * OUT, 8, LANES))
        out_ref[p] = pixels.reshape(B, LANES).astype(BF16)
        return carry

    lax.fori_loop(0, res_ref.shape[0], per_piece, 0)


def ungroup(residual):
    count = residual.shape[0]
    return pl.pallas_call(
        ungroup_kernel,
        grid=(count // BATCH,),
        in_specs=[pl.BlockSpec((BATCH, BLOCKS, 2 * LANES), lambda p: (p, 0, 0))],
        out_specs=pl.BlockSpec((BATCH, B, B), lambda p: (p, 0, 0)),
        out_shape=jax.ShapeDtypeStruct((count, B, B), BF16),
        cost_estimate=SMALL,
        name="ungroup",
    )(residual)


def fold_kernel(per_row, half_rows, ids_ref, slot_ref, out_ref, canvas, scratch, packed):
    canvas[...] = jnp.zeros_like(canvas)
    inside = lax.broadcasted_iota(jnp.int32, (G, LANES), 0) < EXT

    def per_slot(n, carry):
        named = ids_ref[n // CAP, 0, n % CAP]

        @pl.when(named >= 0)
        def _():
            first_row = named // per_row * (2 * OUT)
            first_col = pl.multiple_of(named % per_row * OUT, 8)
            scratch[:ADJ_ROWS, :] = slot_ref[n].astype(F32)
            for row in range(EXT):
                for half in range(2 if row < EXT - 1 else 1):
                    first = SLOT_ROWS * half + EXT * row
                    part = jnp.where(inside, scratch[first : first + G, :], 0.0)
                    at = (first_row + 2 * row + half, pl.ds(first_col, G), slice(None))
                    canvas[at] = canvas[at] + part

        return carry

    lax.fori_loop(0, slot_ref.shape[0], per_slot, 0)
    for chunk in range(per_row):
        first = OUT * chunk + 1
        for row in range(half_rows):
            packed[CHUNK * row : CHUNK * row + G, :] = canvas[row, first : first + G, :]
        out_ref[chunk] = packed[...].astype(BF16)


def fold(ids, received, per_row, half_rows):
    return pl.pallas_call(
        lambda *refs: fold_kernel(per_row, half_rows, *refs),
        in_specs=[
            pl.BlockSpec(memory_space=pltpu.SMEM),
            pl.BlockSpec(memory_space=pltpu.VMEM),
        ],
        out_specs=pl.BlockSpec(memory_space=pltpu.VMEM),
        scratch_shapes=[
            pltpu.VMEM((half_rows, PITCH + 8, LANES), F32),
            pltpu.VMEM((ADJ_ROWS + 8, LANES), F32),
            pltpu.VMEM((CHUNK_ROWS, LANES), F32),
        ],
        out_shape=pltpu.VMEM((per_row, CHUNK_ROWS, LANES), BF16),
        cost_estimate=SMALL,
        name="fold",
    )(ids, on_chip(received))


def finish_kernel(half_rows, terms_ref, up_out, middle_out, down_out, summed, canvas):
    total = terms_ref[0].astype(F32)
    for term in range(1, terms_ref.shape[0]):
        total = total + terms_ref[term].astype(F32)
    summed[...] = total
    near = lax.broadcasted_iota(jnp.int32, (8, LANES), 1) < LANES - SHIFT
    for first in range(0, half_rows, 8):
        count = min(8, half_rows - first)
        starts = [CHUNK * (first + row) for row in range(count)]
        tiles = swap_groups(jnp.stack([summed[start : start + 8, :] for start in starts], 0))
        edges = summed[pl.ds(starts[0] + 8, count, stride=CHUNK), :]
        if count < 8:
            edges = jnp.concatenate([edges, jnp.zeros((8 - count, LANES), F32)], axis=0)
        edges = swap_groups(edges.reshape(1, 8, LANES)).reshape(8, LANES)
        for row in range(count):
            tile = pltpu.roll(tiles[row], LANES - SHIFT, 1)
            edge = pltpu.roll(edges, (LANES - SHIFT - G * row) % LANES, 1)
            start = 8 * (first + row)
            canvas[start : start + 8, :] = jnp.where(near, tile, edge)
    middle = middle_out.shape[0]
    up_out[...] = canvas[:HALO, :].astype(BF16)
    middle_out[...] = canvas[HALO : HALO + middle, :]
    down_out[...] = canvas[HALO + middle : 2 * HALO + middle, :].astype(BF16)


def finish(terms, half_rows, rows):
    rim = pltpu.VMEM((HALO, LANES), BF16)
    vmem = pl.BlockSpec(memory_space=pltpu.VMEM)
    return pl.pallas_call(
        lambda *refs: finish_kernel(half_rows, *refs),
        in_specs=[vmem],
        out_specs=[vmem, vmem, vmem],
        out_shape=[rim, jax.ShapeDtypeStruct((rows, LANES), F32), rim],
        scratch_shapes=[
            pltpu.VMEM((CHUNK_ROWS, LANES), F32),
            pltpu.VMEM((8 * half_rows, LANES), F32),
        ],
        cost_estimate=SMALL,
        name="finish",
    )(on_chip(terms))


def rims_kernel(middle_ref, above_ref, below_ref, out_ref):
    rows = out_ref.shape[0]
    out_ref[...] = middle_ref[...]

    @pl.when(pl.program_id(0) == 0)
    def _():
        out_ref[:HALO, :] = out_ref[:HALO, :] + above_ref[...].astype(F32)

    @pl.when(pl.program_id(0) == 1)
    def _():
        out_ref[rows - HALO :, :] = out_ref[rows - HALO :, :] + below_ref[...].astype(F32)


def add_rims(middle, above, below):
    rows = 32
    last = middle.shape[0] // rows - 1
    block = pl.BlockSpec((rows, LANES), lambda i: (i * last, 0))
    return pl.pallas_call(
        rims_kernel,
        grid=(2,),
        in_specs=[block, whole_vmem(), whole_vmem()],
        out_specs=block,
        out_shape=jax.ShapeDtypeStruct(middle.shape, F32),
        input_output_aliases={0: 0},
        cost_estimate=SMALL,
        name="rims",
    )(middle, on_chip(above), on_chip(below))


def shards(sky_model, exposure_data, pixel_mask, block_owner, block_local, psf_cell, psf_table):
    sky_count = lax.axis_size("sky")
    stripe_rows, stripe_cols = sky_model.shape
    per_row = stripe_cols // B
    block_total = stripe_rows // B * per_row
    piece_count = exposure_data.shape[0]
    owner_sky = block_owner[:, 0]
    code = lax.broadcasted_iota(jnp.int32, (piece_count,), 0) * block_total + block_local
    mine = owner_sky[None, :] == lax.broadcasted_iota(jnp.int32, (sky_count, 1), 0)
    first = jnp.min(jnp.where(mine, code[None, :], piece_count * block_total), axis=1)
    last = jnp.max(jnp.where(mine, code[None, :], -1), axis=1)
    requests = jnp.stack(
        [
            jnp.where(last < 0, -1, first % block_total),
            jnp.where(last > first, last % block_total, -1),
        ],
        axis=1,
    )
    asked = lax.all_to_all(
        requests[:, None, :], "sky", split_axis=0, concat_axis=0, tiled=True
    )
    above = from_behind(sky_model[stripe_rows - HALO :], "sky", 1)
    below = from_behind(sky_model[:HALO], "sky", -1)
    half_rows = (stripe_rows + 2 * HALO + TAIL) // 8
    second = jnp.any(mine & (first[:, None] < code[None, :]), axis=0)
    kernels = padded_kernels(psf_table)
    asked, above, below, second = lax.optimization_barrier((asked, above, below, second))
    blocks = stripe_blocks(sky_model, above, below, half_rows)
    outgoing = cut_patches(asked, blocks, per_row)
    exposure_data, pixel_mask, kernels, second, _ = lax.optimization_barrier(
        (exposure_data, pixel_mask, kernels, second, outgoing)
    )
    slot_index = owner_sky * CAP + second.astype(jnp.int32)
    patches = lax.all_to_all(outgoing, "sky", split_axis=0, concat_axis=0, tiled=True)
    data = regroup(exposure_data, pixel_mask)
    taps = build_taps(kernels)
    adjoints, residuals = pieces(slot_index, psf_cell, patches, taps, data)
    received = lax.all_to_all(adjoints, "sky", split_axis=0, concat_axis=0, tiled=True)
    received, residual = lax.optimization_barrier((received, ungroup(residuals)))

    partial = fold(asked, received, per_row, half_rows)
    terms = lax.all_to_all(partial, "exp", split_axis=0, concat_axis=0, tiled=True)
    up, middle, down = finish(terms, half_rows, stripe_rows)
    from_below = from_behind(up, "sky", -1)
    from_above = from_behind(down, "sky", 1)
    gradient = add_rims(middle, from_above, from_below)
    return (gradient, residual)


def solution(mesh):
    in_specs = (
        P("sky", None),
        P(("sky", "exp"), None, None),
        P(("sky", "exp"), None, None),
        P(("sky", "exp"), None),
        P(("sky", "exp")),
        P(("sky", "exp")),
        P("exp", None),
    )
    out_specs = (P("sky", "exp"), P(("sky", "exp"), None, None))
    return jax.shard_map(shards, mesh=mesh, in_specs=in_specs, out_specs=out_specs, check_vma=False)
```

```python
import jax
import jax.numpy as jnp
from jax import lax
from jax.experimental import pallas as pl
from jax.experimental.pallas import tpu as pltpu
from jax.sharding import PartitionSpec as P

B = 128
PSF = 41
HALO = 20
CAP = 2

G = 16
LANES = 128
OUT = B // G
EXT = 11
REACH = 4
TAIL = 8
BLOCKS = OUT * OUT
PATCH_ROWS = 232
ADJ_ROWS = 240
SLOT_ROWS = 128
PITCH = 72
TILES = 6
RES_LEAD = 40
TAP_ROWS = 48
GROUP = 4
BATCH = 4
SLOTS = 8
CHUNK = 9
CHUNK_ROWS = 352
SHIFT = 4
UNKNOWN = 2.0**100
SMALL = pl.CostEstimate(flops=1000, bytes_accessed=1000, transcendentals=0)
F32 = jnp.float32
BF16 = jnp.bfloat16


def whole_vmem():
    return pl.BlockSpec(memory_space=pltpu.VMEM)


def on_chip(x):
    return pltpu.with_memory_space_constraint(x, pltpu.VMEM)


def from_behind(x, axis, by):
    devices = lax.axis_size(axis)
    pairs = [(i, i + by) for i in range(devices) if 0 <= i + by < devices]
    return lax.ppermute(x, axis, pairs)


def swap_groups(x):
    sub = lax.broadcasted_iota(jnp.int32, x.shape, 1)
    group = lax.broadcasted_iota(jnp.int32, x.shape, 2) // G
    for d in (4, 2, 1):
        sub_bit, group_bit = (sub & d) != 0, (group & d) != 0
        up = pltpu.roll(pltpu.roll(x, 8 - d, 1), G * d, 2)
        down = up if d == 4 else pltpu.roll(pltpu.roll(x, d, 1), LANES - G * d, 2)
        x = jnp.where(sub_bit == group_bit, x, jnp.where(group_bit, up, down))
    return x


def reversed_groups(shift=0):
    source = lax.broadcasted_iota(jnp.int32, (2 * LANES, LANES), 0)
    lane = lax.broadcasted_iota(jnp.int32, (2 * LANES, LANES), 1)
    group = (8 - lane // G) % 8
    return (source == LANES - shift + group * G + lane % G).astype(BF16)


def swap_reversed(x):
    group = lax.broadcasted_iota(jnp.int32, (8, LANES), 1) // G
    tiles = []
    for tile in range(x.shape[0]):
        now = pltpu.roll(x[tile], 0, 1, stride=G, stride_axis=0)
        for d in (1, 2, 4):
            now = jnp.where((group & d) != 0, pltpu.roll(now, 8 - d, 0), now)
        tiles.append(pltpu.roll(now, 0, 1, stride=G, stride_axis=0))
    return jnp.stack(tiles, 0)


def regroup_kernel(data_ref, keep_ref, out_ref):
    def per_piece(p, carry):
        known = jnp.where(keep_ref[p] != 0, data_ref[p].astype(F32), UNKNOWN).astype(BF16)
        turned = jnp.dot(known, reversed_groups()[LANES:], preferred_element_type=F32)
        blocks = swap_reversed(turned.reshape(2 * OUT, 8, LANES)).reshape(OUT, 2, 8, LANES)
        for half in range(2):
            out_ref[p, :, half * LANES : (half + 1) * LANES] = (
                blocks[:, half].reshape(BLOCKS, LANES).astype(BF16)
            )
        return carry

    lax.fori_loop(0, data_ref.shape[0], per_piece, 0, unroll=2)


def regroup(exposure_data, pixel_mask):
    pieces = exposure_data.shape[0]
    block = pl.BlockSpec((BATCH, B, B), lambda p: (p, 0, 0))
    return pl.pallas_call(
        regroup_kernel,
        grid=(pieces // BATCH,),
        in_specs=[block, block],
        out_specs=pl.BlockSpec((BATCH, BLOCKS, 2 * LANES), lambda p: (p, 0, 0)),
        out_shape=jax.ShapeDtypeStruct((pieces, BLOCKS, 2 * LANES), BF16),
        cost_estimate=SMALL,
        name="regroup",
    )(exposure_data, pixel_mask)


def taps_kernel(kernel_ref, out_ref, windows, rows):
    lane = lax.broadcasted_iota(jnp.int32, (G, LANES), 1)
    odd = (lane // G) % 2 == 1
    wide = lax.broadcasted_iota(jnp.int32, (TAP_ROWS, LANES), 1) // (2 * G)
    quarter = lax.broadcasted_iota(jnp.int32, (TILES, LANES), 1) // (2 * G)

    kernel = kernel_ref[0].astype(F32)
    spread = pltpu.roll(kernel, G, 1)
    for t in range(1, REACH):
        spread = jnp.where(wide == t, pltpu.roll(kernel, G * t + G, 1), spread)
    windows[...] = spread
    for parity in range(2):
        picked = [windows[pl.ds(parity + 2 * q, TILES, stride=8), :] for q in range(4)]
        for t in range(REACH):
            row = picked[0] if t == 0 else pltpu.roll(picked[0], 2 * G * (4 - t), 1)
            for q in range(1, 4):
                by = (q - t) % 4
                part = picked[q] if by == 0 else pltpu.roll(picked[q], 2 * G * by, 1)
                row = jnp.where(quarter == q, part, row)
            rows[t, parity, :TILES, :] = row

    def per_shift(t, carry):
        before = [jnp.zeros((G, LANES), F32)] * 8
        for tile in range(TILES):
            even_row, odd_row = (
                jnp.broadcast_to(rows[t, parity, tile : tile + 1, :], (G, LANES))
                for parity in range(2)
            )
            even_row = pltpu.roll(even_row, LANES - G, 1, stride=1, stride_axis=0)
            odd_row = pltpu.roll(odd_row, 0, 1, stride=1, stride_axis=0)
            now = jnp.where(odd, odd_row, even_row)
            turns = [now] + [pltpu.roll(now, G * phase, 1) for phase in range(1, 8)]
            for phase in range(8):
                part = turns[phase]
                if phase > 0:
                    part = jnp.where(lane < G * phase, before[phase], part)
                start = pl.multiple_of(t * LANES + phase * G, G)
                lanes = slice(tile * LANES, (tile + 1) * LANES)
                out_ref[0, pl.ds(start, G), lanes] = part.astype(BF16)
            before = turns
        return carry

    lax.fori_loop(0, REACH, per_shift, 0)


def padded_kernels(table):
    kernels = table.reshape(table.shape[0], PSF, PSF)
    return jnp.pad(kernels, ((0, 0), (0, TAP_ROWS - PSF), (0, LANES - PSF)))


def build_taps(kernels):
    cells = kernels.shape[0]
    return pl.pallas_call(
        taps_kernel,
        grid=(cells,),
        in_specs=[pl.BlockSpec((1, TAP_ROWS, LANES), lambda c: (c, 0, 0))],
        out_specs=pl.BlockSpec((1, REACH * LANES, TILES * LANES), lambda c: (c, 0, 0)),
        out_shape=jax.ShapeDtypeStruct((cells, REACH * LANES, TILES * LANES), BF16),
        scratch_shapes=[
            pltpu.VMEM((TAP_ROWS, LANES), F32),
            pltpu.VMEM((REACH, 2, 8, LANES), F32),
        ],
        cost_estimate=SMALL,
        name="taps",
    )(kernels)


def moved_tiles(pixels):
    rows, columns = pixels.shape
    turn = reversed_groups(HALO)
    empty = jnp.zeros((rows, LANES), BF16)
    tiles = [pixels[:, at : at + LANES] for at in range(0, columns, LANES)]
    return [
        jnp.dot(jnp.concatenate([old, now], axis=1), turn, preferred_element_type=F32)
        for old, now in zip([empty] + tiles, tiles + [empty])
    ]


def blocks_kernel(stripe_ref, above_ref, below_ref, out_ref, pixels):
    first = 0
    for ref in (above_ref, stripe_ref, below_ref):
        rows = ref.shape[0]
        for tile, moved in enumerate(moved_tiles(ref[...])):
            pixels[first : first + rows, tile * LANES : (tile + 1) * LANES] = moved
        first += rows
    pixels[first:, :] = jnp.zeros((TAIL, PITCH * G), F32)
    for row in range(out_ref.shape[0]):
        tiles = [
            pixels[8 * row : 8 * row + 8, at : at + LANES] for at in range(0, PITCH * G, LANES)
        ]
        out_ref[row] = swap_reversed(jnp.stack(tiles, 0)).reshape(PITCH, LANES)


def stripe_blocks(stripe, above, below, half_rows):
    return pl.pallas_call(
        blocks_kernel,
        in_specs=[whole_vmem(), whole_vmem(), whole_vmem()],
        out_specs=whole_vmem(),
        out_shape=pltpu.VMEM((half_rows, PITCH, LANES), F32),
        scratch_shapes=[pltpu.VMEM((8 * half_rows, PITCH * G), F32)],
        cost_estimate=SMALL,
        name="blocks",
    )(stripe, on_chip(above), on_chip(below))


def cut_kernel(per_row, ids_ref, blocks_ref, out_ref, scratch):
    step = pl.program_id(0)

    def per_slot(n, carry):
        at = step * SLOTS + n
        wanted = ids_ref[at // CAP, 0, at % CAP]

        @pl.when(wanted >= 0)
        def _():
            first_row = wanted // per_row * (2 * OUT)
            first_col = pl.multiple_of(wanted % per_row * OUT, 8)
            for row in range(2 * EXT - 1):
                part = blocks_ref[first_row + row, pl.ds(first_col, G), :]
                scratch[EXT * row : EXT * row + G, :] = part
            out_ref[n] = scratch[:PATCH_ROWS, :].astype(BF16)

        return carry

    lax.fori_loop(0, SLOTS, per_slot, 0)


def cut_patches(ids, blocks, per_row):
    slots = ids.shape[0] * CAP
    return pl.pallas_call(
        lambda *refs: cut_kernel(per_row, *refs),
        grid_spec=pltpu.PrefetchScalarGridSpec(
            num_scalar_prefetch=1,
            grid=(slots // SLOTS,),
            in_specs=[whole_vmem()],
            out_specs=pl.BlockSpec((SLOTS, PATCH_ROWS, LANES), lambda n, ids: (n, 0, 0)),
            scratch_shapes=[pltpu.VMEM((PATCH_ROWS + 8, LANES), F32)],
        ),
        out_shape=jax.ShapeDtypeStruct((slots, PATCH_ROWS, LANES), BF16),
        cost_estimate=SMALL,
        name="cut",
    )(ids, on_chip(blocks))


def block_taps(taps_ref, s, t):
    taps = slice(t * LANES, (t + 1) * LANES)
    upper = taps_ref[0, taps, 2 * s * LANES : (2 * s + 2) * LANES]
    if s == 0:
        lower = jnp.concatenate(
            [jnp.zeros((LANES, LANES), BF16), taps_ref[0, taps, 0:LANES]], axis=1
        )
    else:
        lower = taps_ref[0, taps, (2 * s - 1) * LANES : (2 * s + 1) * LANES]
    return jnp.concatenate([upper, lower], axis=0)


def last_taps(taps_ref, t):
    return taps_ref[0, t * LANES : (t + 1) * LANES, (TILES - 1) * LANES :]


def correlate(read, taps_ref):
    across = (((1,), (1,)), ((), ()))
    total = jnp.zeros((2 * BLOCKS, LANES), F32)
    for t in range(REACH):
        for d in range(TILES // 2):
            taps = taps_ref[0, t * LANES : (t + 1) * LANES, 2 * d * LANES : (2 * d + 2) * LANES]
            total = total + lax.dot_general(
                read(d, t), taps, across, preferred_element_type=F32
            )
    return jnp.concatenate([total[:BLOCKS], total[BLOCKS:]], axis=1)


def convolve(read, taps_ref, rows):
    total = jnp.zeros((rows, 2 * LANES), F32)
    for t in range(REACH):
        for s in range(REACH - 1):
            total = total + jnp.dot(
                read(s, t), block_taps(taps_ref, s, t), preferred_element_type=F32
            )
    last = jnp.zeros((rows, LANES), F32)
    for t in range(0, REACH, 2):
        field = [read(REACH - 1, t + i)[:, LANES:] for i in range(2)]
        taps = [last_taps(taps_ref, t + i) for i in range(2)]
        last = last + jnp.dot(
            jnp.concatenate(field, axis=1),
            jnp.concatenate(taps, axis=0),
            preferred_element_type=F32,
        )
    return jnp.concatenate([total[:, :LANES] + last, total[:, LANES:]], axis=1)


def pieces_kernel(slot_ref, cell_ref, patch_ref, *refs):
    taps, refs = refs[:GROUP], refs[GROUP:]
    data_ref, adjoints, res_out, field, resid, adj_slots, sems = refs
    step = pl.program_id(0)
    slots = lax.rem(step, 2)

    @pl.when(step == 0)
    def _():
        resid[...] = jnp.zeros_like(resid)

    def sent(step):
        at = lax.rem(step, 2)
        return [
            pltpu.make_async_copy(
                adj_slots.at[at, i], adjoints.at[slot_ref[GROUP * step + i]], sems.at[at, i]
            )
            for i in range(GROUP)
        ]

    @pl.when(step >= 2)
    def _():
        for copy in sent(step - 2):
            copy.wait()

    def forward(i, taps_ref, field):
        field[...] = patch_ref[slot_ref[GROUP * step + i]].astype(F32)

        def read_patch(d, t):
            parts = []
            for half in range(2):
                for row in range(OUT):
                    at = EXT * (2 * (row + d) + half) + t
                    pair = [field[at : at + OUT, :], field[at + EXT : at + EXT + OUT, :]]
                    parts.append(jnp.concatenate(pair, axis=1))
            return jnp.concatenate(parts, axis=0).astype(BF16)

        return correlate(read_patch, taps_ref)

    def compare(i, predicted, resid):
        observed = data_ref[i].astype(F32)
        residual = jnp.where(observed < UNKNOWN, predicted - observed, 0.0).astype(BF16)
        res_out[i] = residual
        wide = residual.astype(F32)
        for row in range(OUT):
            first = RES_LEAD + EXT * row
            resid[first : first + OUT, :] = wide[OUT * row : OUT * (row + 1)]

    def backward(i, taps_ref, resid):
        def read_residual(s, t):
            return resid[pl.ds(RES_LEAD - EXT * s - t, SLOT_ROWS), :].astype(BF16)

        adjoint = convolve(read_residual, taps_ref, SLOT_ROWS).astype(BF16)
        adj_slots[slots, i, :SLOT_ROWS] = adjoint[:, :LANES]
        adj_slots[slots, i, SLOT_ROWS:] = adjoint[: ADJ_ROWS - SLOT_ROWS, LANES:]

    for i in range(GROUP):
        compare(i, forward(i, taps[i], field.at[i]), resid.at[i])
    for i in range(GROUP):
        backward(i, taps[i], resid.at[i])
    for copy in sent(step):
        copy.start()

    @pl.when(step == pl.num_programs(0) - 1)
    def _():
        for copy in sent(step - 1) + sent(step):
            copy.wait()


def pieces(slots, cells, patches, taps, data):
    count = data.shape[0]
    cell = [
        pl.BlockSpec(
            (1, REACH * LANES, TILES * LANES),
            lambda p, slots, cells, i=i: (cells[GROUP * p + i], 0, 0),
        )
        for i in range(GROUP)
    ]
    block = pl.BlockSpec((GROUP, BLOCKS, 2 * LANES), lambda p, slots, cells: (p, 0, 0))
    return pl.pallas_call(
        pieces_kernel,
        grid_spec=pltpu.PrefetchScalarGridSpec(
            num_scalar_prefetch=2,
            grid=(count // GROUP,),
            in_specs=[whole_vmem(), *cell, block],
            out_specs=[pl.BlockSpec(memory_space=pltpu.HBM), block],
            scratch_shapes=[
                pltpu.VMEM((GROUP, PATCH_ROWS, LANES), F32),
                pltpu.VMEM((GROUP, RES_LEAD + SLOT_ROWS, 2 * LANES), F32),
                pltpu.VMEM((2, GROUP, ADJ_ROWS, LANES), BF16),
                pltpu.SemaphoreType.DMA((2, GROUP)),
            ],
        ),
        out_shape=[
            jax.ShapeDtypeStruct((patches.shape[0], ADJ_ROWS, LANES), BF16),
            jax.ShapeDtypeStruct(data.shape, BF16),
        ],
        cost_estimate=SMALL,
        name="pieces",
    )(slots, cells, on_chip(patches), *[taps] * GROUP, data)


def ungroup_kernel(res_ref, out_ref):
    turn = reversed_groups()[LANES:]

    def per_piece(p, carry):
        halves = [
            jnp.dot(
                res_ref[p, :, half * LANES : (half + 1) * LANES], turn, preferred_element_type=F32
            ).reshape(OUT, 8, LANES)
            for half in range(2)
        ]
        pixels = swap_reversed(jnp.stack(halves, 1).reshape(2 * OUT, 8, LANES))
        out_ref[p] = pixels.reshape(B, LANES).astype(BF16)
        return carry

    lax.fori_loop(0, res_ref.shape[0], per_piece, 0)


def ungroup(residual):
    count = residual.shape[0]
    return pl.pallas_call(
        ungroup_kernel,
        grid=(count // BATCH,),
        in_specs=[pl.BlockSpec((BATCH, BLOCKS, 2 * LANES), lambda p: (p, 0, 0))],
        out_specs=pl.BlockSpec((BATCH, B, B), lambda p: (p, 0, 0)),
        out_shape=jax.ShapeDtypeStruct((count, B, B), BF16),
        cost_estimate=SMALL,
        name="ungroup",
    )(residual)


def fold_kernel(per_row, half_rows, ids_ref, slot_ref, out_ref, canvas, scratch, packed):
    canvas[...] = jnp.zeros_like(canvas)
    inside = lax.broadcasted_iota(jnp.int32, (G, LANES), 0) < EXT

    def per_slot(n, carry):
        named = ids_ref[n // CAP, 0, n % CAP]

        @pl.when(named >= 0)
        def _():
            first_row = named // per_row * (2 * OUT)
            first_col = pl.multiple_of(named % per_row * OUT, 8)
            scratch[:ADJ_ROWS, :] = slot_ref[n].astype(F32)
            for row in range(EXT):
                for half in range(2 if row < EXT - 1 else 1):
                    first = SLOT_ROWS * half + EXT * row
                    part = jnp.where(inside, scratch[first : first + G, :], 0.0)
                    at = (first_row + 2 * row + half, pl.ds(first_col, G), slice(None))
                    canvas[at] = canvas[at] + part

        return carry

    lax.fori_loop(0, slot_ref.shape[0], per_slot, 0)
    for chunk in range(per_row):
        first = OUT * chunk + 1
        for row in range(half_rows):
            packed[CHUNK * row : CHUNK * row + G, :] = canvas[row, first : first + G, :]
        out_ref[chunk] = packed[...].astype(BF16)


def fold(ids, received, per_row, half_rows):
    return pl.pallas_call(
        lambda *refs: fold_kernel(per_row, half_rows, *refs),
        in_specs=[
            pl.BlockSpec(memory_space=pltpu.SMEM),
            pl.BlockSpec(memory_space=pltpu.VMEM),
        ],
        out_specs=pl.BlockSpec(memory_space=pltpu.VMEM),
        scratch_shapes=[
            pltpu.VMEM((half_rows, PITCH + 8, LANES), F32),
            pltpu.VMEM((ADJ_ROWS + 8, LANES), F32),
            pltpu.VMEM((CHUNK_ROWS, LANES), F32),
        ],
        out_shape=pltpu.VMEM((per_row, CHUNK_ROWS, LANES), BF16),
        cost_estimate=SMALL,
        name="fold",
    )(ids, on_chip(received))


def finish_kernel(half_rows, terms_ref, up_out, middle_out, down_out, summed, canvas):
    total = terms_ref[0].astype(F32)
    for term in range(1, terms_ref.shape[0]):
        total = total + terms_ref[term].astype(F32)
    summed[...] = total
    near = lax.broadcasted_iota(jnp.int32, (8, LANES), 1) < LANES - SHIFT
    for first in range(0, half_rows, 8):
        count = min(8, half_rows - first)
        starts = [CHUNK * (first + row) for row in range(count)]
        tiles = swap_groups(jnp.stack([summed[start : start + 8, :] for start in starts], 0))
        edges = summed[pl.ds(starts[0] + 8, count, stride=CHUNK), :]
        if count < 8:
            edges = jnp.concatenate([edges, jnp.zeros((8 - count, LANES), F32)], axis=0)
        edges = swap_groups(edges.reshape(1, 8, LANES)).reshape(8, LANES)
        for row in range(count):
            tile = pltpu.roll(tiles[row], LANES - SHIFT, 1)
            edge = pltpu.roll(edges, (LANES - SHIFT - G * row) % LANES, 1)
            start = 8 * (first + row)
            canvas[start : start + 8, :] = jnp.where(near, tile, edge)
    middle = middle_out.shape[0]
    up_out[...] = canvas[:HALO, :].astype(BF16)
    middle_out[...] = canvas[HALO : HALO + middle, :]
    down_out[...] = canvas[HALO + middle : 2 * HALO + middle, :].astype(BF16)


def finish(terms, half_rows, rows):
    rim = pltpu.VMEM((HALO, LANES), BF16)
    vmem = pl.BlockSpec(memory_space=pltpu.VMEM)
    return pl.pallas_call(
        lambda *refs: finish_kernel(half_rows, *refs),
        in_specs=[vmem],
        out_specs=[vmem, vmem, vmem],
        out_shape=[rim, pltpu.VMEM((rows, LANES), F32), rim],
        scratch_shapes=[
            pltpu.VMEM((CHUNK_ROWS, LANES), F32),
            pltpu.VMEM((8 * half_rows, LANES), F32),
        ],
        cost_estimate=SMALL,
        name="finish",
    )(on_chip(terms))


def rims_kernel(middle_ref, above_ref, below_ref, out_ref):
    rows = out_ref.shape[0]
    out_ref[...] = middle_ref[...]
    out_ref[:HALO, :] = out_ref[:HALO, :] + above_ref[...].astype(F32)
    out_ref[rows - HALO :, :] = out_ref[rows - HALO :, :] + below_ref[...].astype(F32)


def add_rims(middle, above, below):
    return pl.pallas_call(
        rims_kernel,
        in_specs=[whole_vmem(), whole_vmem(), whole_vmem()],
        out_specs=whole_vmem(),
        out_shape=jax.ShapeDtypeStruct(middle.shape, F32),
        cost_estimate=SMALL,
        name="rims",
    )(on_chip(middle), on_chip(above), on_chip(below))


def shards(sky_model, exposure_data, pixel_mask, block_owner, block_local, psf_cell, psf_table):
    sky_count = lax.axis_size("sky")
    stripe_rows, stripe_cols = sky_model.shape
    per_row = stripe_cols // B
    block_total = stripe_rows // B * per_row
    piece_count = exposure_data.shape[0]
    owner_sky = block_owner[:, 0]
    code = lax.broadcasted_iota(jnp.int32, (piece_count,), 0) * block_total + block_local
    mine = owner_sky[None, :] == lax.broadcasted_iota(jnp.int32, (sky_count, 1), 0)
    first = jnp.min(jnp.where(mine, code[None, :], piece_count * block_total), axis=1)
    last = jnp.max(jnp.where(mine, code[None, :], -1), axis=1)
    requests = jnp.stack(
        [
            jnp.where(last < 0, -1, first % block_total),
            jnp.where(last > first, last % block_total, -1),
        ],
        axis=1,
    )
    asked = lax.all_to_all(
        requests[:, None, :], "sky", split_axis=0, concat_axis=0, tiled=True
    )
    above = from_behind(sky_model[stripe_rows - HALO :], "sky", 1)
    below = from_behind(sky_model[:HALO], "sky", -1)
    half_rows = (stripe_rows + 2 * HALO + TAIL) // 8
    second = jnp.any(mine & (first[:, None] < code[None, :]), axis=0)
    kernels = padded_kernels(psf_table)
    asked, above, below, second = lax.optimization_barrier((asked, above, below, second))
    blocks = stripe_blocks(sky_model, above, below, half_rows)
    outgoing = cut_patches(asked, blocks, per_row)
    exposure_data, pixel_mask, kernels, second, _ = lax.optimization_barrier(
        (exposure_data, pixel_mask, kernels, second, outgoing)
    )
    slot_index = owner_sky * CAP + second.astype(jnp.int32)
    patches = lax.all_to_all(outgoing, "sky", split_axis=0, concat_axis=0, tiled=True)
    data = regroup(exposure_data, pixel_mask)
    taps = build_taps(kernels)
    adjoints, residuals = pieces(slot_index, psf_cell, patches, taps, data)
    received = lax.all_to_all(adjoints, "sky", split_axis=0, concat_axis=0, tiled=True)
    received, residual = lax.optimization_barrier((received, ungroup(residuals)))

    partial = fold(asked, received, per_row, half_rows)
    terms = lax.all_to_all(partial, "exp", split_axis=0, concat_axis=0, tiled=True)
    up, middle, down = finish(terms, half_rows, stripe_rows)
    from_below = from_behind(up, "sky", -1)
    from_above = from_behind(down, "sky", 1)
    gradient = add_rims(middle, from_above, from_below)
    return (gradient, residual)


def solution(mesh):
    in_specs = (
        P("sky", None),
        P(("sky", "exp"), None, None),
        P(("sky", "exp"), None, None),
        P(("sky", "exp"), None),
        P(("sky", "exp")),
        P(("sky", "exp")),
        P("exp", None),
    )
    out_specs = (P("sky", "exp"), P(("sky", "exp"), None, None))
    return jax.shard_map(shards, mesh=mesh, in_specs=in_specs, out_specs=out_specs, check_vma=False)
```
